32 devices in a mesh: src: 2 (over x), rcv: 4 (over y, core), foc: 4 (over z).
Axes of the slice: x: 2, y: 2, z: 4, core: 2. Of those that a mesh axis runs over, the one named last changes fastest.
Arguments:
- reflection: bfloat16 [2, 256, 256, 1024], P(None, 'foc', 'src', 'rcv'), may hold values from -0.1875 to 0.1875
- direct_wave: bfloat16 [2, 256, 32, 1024], P(None, None, 'foc', 'rcv'), may hold values from -6 to 6
- onset_receiver: int32 [32, 1024], P('foc', 'rcv'), may hold values from 128 to 1023
- onset_source: int32 [32, 256], P('foc', 'src'), may hold values from 128 to 1023
Outputs:
- focusing: bfloat16 [2, 256, 32, 1024], P(None, None, 'foc', 'rcv')
- muted_trace: bfloat16 [32, 256, 1024], P('foc', 'src')
The draws below stay inside these ranges and needn't reach their ends.
Inputs may be any that keep to these rules, and one draw needn't show every extreme that they name: `onset_receiver`: onset sample of the muting window of each focal point and receiver; samples before it are kept. `onset_source`: onset sample of the muting window of each focal point and source; samples before it are kept.
All inputs are finite; a program needn't handle non-finite values.
Results may differ from the reference program's by a relative error of at most 0.029.
Values may be sent and summed in bfloat16 or wider, within the bound.
No kernel may reach another device: no remote copies, remote signals or barrier semaphores. Data moves between devices by JAX's collectives and lax.ppermute only.
A program may use at most 128 MiB of HBM per device.

```python
import math
import jax
import jax.numpy as jnp
from jax import lax

F = 256
NS = 256
NR = 1024
NP = 32
NT = 1024
ITERS = 2
N_SRC = 2


def with_ends(drawn, own_key, least, largest):
    index_at = [jax.random.randint(jax.random.fold_in(own_key, axis), (), 0, length) for axis, length in enumerate(drawn.shape)]
    longest = drawn.shape.index(max(drawn.shape))
    next_to = index_at[:longest] + [(index_at[longest] + 1) % drawn.shape[longest]] + index_at[longest + 1:]
    return drawn.at[tuple(index_at)].set(least).at[tuple(next_to)].set(largest)


def block_scale(rng, shape, shards, low, top_value):
    gain = 1.0
    for dim, blocks in shards:
        steps = jax.random.uniform(jax.random.fold_in(jax.random.fold_in(rng, 6), dim), (blocks,), jnp.float32, low / len(shards), top_value / len(shards))
        gain = gain * jnp.repeat(jnp.exp(steps), shape[dim] // blocks).reshape((-1,) + (1,) * (len(shape) - 1 - dim))
    return gain


def normal_values(own_key, shape, spread, bound, cuts=(), kind=jnp.bfloat16):
    result = jax.random.normal(own_key, shape, jnp.float32) * spread
    if len(cuts) > 0:
        result = block_scale(own_key, shape, cuts, -0.22, 0.18) * result
    return jnp.clip(result, min=-bound, max=bound).astype(kind)


def setup_inputs(seed: int = 0) -> dict:
    keys = jax.random.split(jax.random.key(seed), 5)
    return {
        "reflection": normal_values(keys[0], (2, F, NS, NR), NR ** -0.5, 0.1875, ((1, 4), (2, 2), (3, 4))),
        "direct_wave": normal_values(keys[1], (2, F, NP, NR), 1.0, 6.0, ((2, 4), (3, 4))),
        "onset_receiver": with_ends(jax.random.randint(keys[2], (NP, NR), NT // 8, NT), jax.random.fold_in(keys[2], 1), NT // 8, NT - 1).astype(jnp.int32),
        "onset_source": with_ends(jax.random.randint(keys[3], (NP, NS), NT // 8, NT), jax.random.fold_in(keys[3], 1), NT // 8, NT - 1).astype(jnp.int32),
    }


def basis_table():
    frequency_bins = jnp.arange(F, dtype=jnp.int32) + 1
    samples = jnp.arange(NT, dtype=jnp.int32)
    phases = frequency_bins[:, None] * samples[None, :] % NT
    angles = phases.astype(jnp.float32) * (2.0 * math.pi / NT)
    norming = math.sqrt(2.0 / NT)
    return (jnp.stack([jnp.cos(angles), -jnp.sin(angles)]) * norming).astype(jnp.bfloat16)

def mute_traces(spectrum, onsets, basis_rows):
    spectrum = lax.optimization_barrier(spectrum)
    signal = jnp.einsum('cwpr,cwt->prt', spectrum.astype(jnp.float32), basis_rows.astype(jnp.float32))
    samples = jnp.arange(NT, dtype=jnp.int32)
    window = samples[None, None, :] < onsets[:, :, None]
    muted_trace = lax.optimization_barrier(jnp.where(window, signal, 0.0).astype(jnp.bfloat16))
    returned = jnp.einsum('prt,cwt->cwpr', muted_trace.astype(jnp.float32), basis_rows.astype(jnp.float32))
    return (muted_trace, returned)

def convolve(reflection, focusing):
    real_out = jnp.einsum('wsr,wpr->wps', reflection[0], focusing[0]) - jnp.einsum('wsr,wpr->wps', reflection[1], focusing[1])
    imag_out = jnp.einsum('wsr,wpr->wps', reflection[0], focusing[1]) + jnp.einsum('wsr,wpr->wps', reflection[1], focusing[0])
    return jnp.stack([real_out, imag_out])

def correlate(reflection, spectrum):
    real_out = jnp.einsum('wsr,wps->wpr', reflection[0], spectrum[0]) + jnp.einsum('wsr,wps->wpr', reflection[1], spectrum[1])
    imag_out = jnp.einsum('wsr,wps->wpr', reflection[0], spectrum[1]) - jnp.einsum('wsr,wps->wpr', reflection[1], spectrum[0])
    return jnp.stack([real_out, imag_out])

def reference(reflection, direct_wave, onset_receiver, onset_source):
    basis_rows = basis_table()
    whole_reflection = reflection.astype(jnp.float32)
    focusing = direct_wave
    group_size = NS // N_SRC
    muted_trace = jnp.zeros((NP, NS, NT), jnp.bfloat16)
    for iteration in range(ITERS):
        focusing_wide = lax.optimization_barrier(focusing).astype(jnp.float32)
        spectrum = convolve(whole_reflection, focusing_wide)
        muted_trace, returned = mute_traces(spectrum.astype(jnp.bfloat16), onset_source, basis_rows)
        returned_wide = lax.optimization_barrier(returned.astype(jnp.bfloat16)).astype(jnp.float32)

        def add_group(group_index, running):
            first_row = (group_index * group_size).astype(jnp.int32)
            group_rows = lax.dynamic_slice_in_dim(whole_reflection, first_row, group_size, 2)
            chosen = lax.dynamic_slice_in_dim(returned_wide, first_row, group_size, 3)
            group_term = lax.optimization_barrier(correlate(group_rows, chosen).astype(jnp.bfloat16))
            return running + group_term.astype(jnp.float32)
        summed = lax.fori_loop(0, N_SRC, add_group, jnp.zeros((2, F, NP, NR), jnp.float32))
        unused, update = mute_traces(summed.astype(jnp.bfloat16), onset_receiver, basis_rows)
        focusing = (direct_wave.astype(jnp.float32) + update).astype(jnp.bfloat16)
    return (focusing, muted_trace)
```

```python
import functools
import math

import jax
import jax.numpy as jnp
from jax import lax
from jax.experimental import pallas as pl
from jax.experimental.pallas import tpu as pltpu
from jax.sharding import PartitionSpec as P

F = 256
NT = 1024
ITERS = 2
LANES = 128
BLOCK_W = 16
CHUNKS = 1
F32 = jnp.float32
BF16 = jnp.bfloat16
VMEM_BYTES = 48 * 1024 * 1024


def basis_table():
    frequency_bins = jnp.arange(F, dtype=jnp.int32) + 1
    samples = jnp.arange(NT, dtype=jnp.int32)
    phases = frequency_bins[:, None] * samples[None, :] % NT
    angles = phases.astype(jnp.float32) * (2.0 * math.pi / NT)
    norming = math.sqrt(2.0 / NT)
    return (jnp.stack([jnp.cos(angles), -jnp.sin(angles)]) * norming).astype(jnp.bfloat16)


def mute_traces(spectrum, onsets, basis_rows):
    focal_count = spectrum.shape[2]
    samples = jnp.arange(NT, dtype=jnp.int32)

    def one_focus(focal_index, carry):
        muted_all, returned_all = carry
        one_spectrum = lax.dynamic_slice_in_dim(spectrum, focal_index, 1, 2)
        one_onset = lax.dynamic_slice_in_dim(onsets, focal_index, 1, 0)
        signal = jnp.einsum(
            "cwpr,cwt->prt", one_spectrum, basis_rows, preferred_element_type=jnp.float32
        )
        window = samples[None, None, :] < one_onset[:, :, None]
        muted_one = jnp.where(window, signal, 0.0).astype(jnp.bfloat16)
        returned = jnp.einsum(
            "prt,cwt->cwpr", muted_one, basis_rows, preferred_element_type=jnp.float32
        )
        muted_all = lax.dynamic_update_slice_in_dim(muted_all, muted_one, focal_index, 0)
        returned_all = lax.dynamic_update_slice_in_dim(returned_all, returned, focal_index, 2)
        return (muted_all, returned_all)

    initial = (
        jnp.zeros((focal_count, spectrum.shape[3], NT), jnp.bfloat16),
        jnp.zeros(spectrum.shape, jnp.float32),
    )
    return lax.fori_loop(0, focal_count, one_focus, initial)


def convolve(reflection, focusing):
    real_out = jnp.einsum(
        "wsr,wpr->wps", reflection[0], focusing[0], preferred_element_type=jnp.float32
    ) - jnp.einsum("wsr,wpr->wps", reflection[1], focusing[1], preferred_element_type=jnp.float32)
    imag_out = jnp.einsum(
        "wsr,wpr->wps", reflection[0], focusing[1], preferred_element_type=jnp.float32
    ) + jnp.einsum("wsr,wpr->wps", reflection[1], focusing[0], preferred_element_type=jnp.float32)
    return jnp.stack([real_out, imag_out])


def correlate(reflection, spectrum):
    real_out = jnp.einsum(
        "wsr,wps->wpr", reflection[0], spectrum[0], preferred_element_type=jnp.float32
    ) + jnp.einsum("wsr,wps->wpr", reflection[1], spectrum[1], preferred_element_type=jnp.float32)
    imag_out = jnp.einsum(
        "wsr,wps->wpr", reflection[0], spectrum[1], preferred_element_type=jnp.float32
    ) - jnp.einsum("wsr,wps->wpr", reflection[1], spectrum[0], preferred_element_type=jnp.float32)
    return jnp.stack([real_out, imag_out])


def renew(shares, direct_wave, onset_receiver, basis_rows, source_index):
    share_width = shares.shape[3]
    offset = source_index * share_width
    onset_share = lax.dynamic_slice_in_dim(onset_receiver, offset, share_width, 1)
    direct_share = lax.dynamic_slice_in_dim(direct_wave, offset, share_width, 3)
    unused, update = mute_traces(shares, onset_share, basis_rows)
    renewed = (direct_share.astype(jnp.float32) + update).astype(jnp.bfloat16)
    return lax.all_gather(renewed, "src", axis=3, tiled=True)


def general(reflection, direct_wave, onset_receiver, onset_source):
    basis_rows = basis_table()
    source_index = lax.axis_index("src")
    whole_reflection = lax.all_gather(reflection, "foc", axis=1, tiled=True)
    focusing = direct_wave
    muted_trace = None
    for iteration in range(ITERS):
        partial_value = convolve(whole_reflection, focusing)
        spectrum = lax.psum(partial_value.astype(jnp.bfloat16), "rcv")
        muted_trace, returned = mute_traces(spectrum, onset_source, basis_rows)
        partial_adjoint = correlate(whole_reflection, returned.astype(jnp.bfloat16))
        shares = lax.psum_scatter(
            partial_adjoint.astype(jnp.bfloat16), "src", scatter_dimension=3, tiled=True
        )
        focusing = renew(shares, direct_wave, onset_receiver, basis_rows, source_index)
    return (focusing, muted_trace)


def swap(value, axis, mask, count):
    return lax.ppermute(value, axis, [(i, i ^ mask) for i in range(count)])


def ordered_basis(foc_index, foc_count, freq_count, chunk_count):
    width = freq_count // chunk_count
    row = jnp.arange(foc_count * 2 * freq_count, dtype=jnp.int32)
    within = row % width
    part = row // width % 2
    piece = row // (2 * width) % foc_count
    chunk = row // (2 * width * foc_count)
    frequency = jnp.bitwise_xor(piece, foc_index) * freq_count + chunk * width + within
    samples = jnp.arange(NT, dtype=jnp.int32)

    def table(freq, quarter, sample):
        phases = ((freq + 1) * sample + quarter * (NT // 4)) % NT
        angles = phases.astype(F32) * (2.0 * math.pi / NT)
        return (jnp.cos(angles) * math.sqrt(2.0 / NT)).astype(BF16)

    rows = table(frequency[:, None], part[:, None], samples[None, :])
    columns = table(frequency[None, :], part[None, :], samples[:, None])
    return rows, columns


def params(*semantics):
    return pltpu.CompilerParams(dimension_semantics=semantics, vmem_limit_bytes=VMEM_BYTES)


def split_kernel(ids, wave_ref, *refs):
    outs, hold = refs[:-1], refs[-1]
    width, focal = wave_ref.shape[1], wave_ref.shape[2]
    hold[...] = wave_ref[0].astype(F32).reshape(width * focal, LANES)
    chunk = width // len(outs)
    for p in range(focal):
        rows = hold[pl.ds(p, width, stride=focal), :].astype(BF16)
        for c, out in enumerate(outs):
            out[0, p] = rows[c * chunk : (c + 1) * chunk]


def split_wave(ids, wave, piece, foc_count, chunk_count):
    freq = wave.shape[1] // foc_count
    focal = wave.shape[2]
    chunk = freq // chunk_count
    return pl.pallas_call(
        split_kernel,
        name="split_wave",
        out_shape=[jax.ShapeDtypeStruct((2, focal, chunk, LANES), BF16)] * chunk_count,
        grid_spec=pltpu.PrefetchScalarGridSpec(
            num_scalar_prefetch=1,
            grid=(2,),
            in_specs=[
                pl.BlockSpec((1, freq, focal, LANES), lambda c, ids: (c, ids[2] ^ piece, 0, ids[0]))
            ],
            out_specs=[pl.BlockSpec((1, focal, chunk, LANES), lambda c, ids: (c, 0, 0, 0))]
            * chunk_count,
            scratch_shapes=[pltpu.VMEM((freq * focal, LANES), F32)],
        ),
        compiler_params=params("arbitrary"),
        cost_estimate=pl.CostEstimate(
            flops=0, bytes_accessed=8 * focal * freq * LANES, transcendentals=0
        ),
    )(ids, wave)


def convolve_kernel(pieces, ids, refl_ref, *refs):
    own, other = refs[:pieces], refs[pieces : 2 * pieces]
    keep_ref, send_ref, hold, result = refs[2 * pieces :]
    half, me = ids[0], ids[1]
    focal, width = own[0].shape[1], own[0].shape[2]
    sources = refl_ref.shape[2]
    rows = pieces * 2 * focal
    per = 2 * focal * width
    for place, group in ((half, own), (1 - half, other)):
        for k in range(pieces):
            hold[place, pl.ds(k * per, per), :] = group[k][...].astype(F32).reshape(per, LANES)
    for w in range(width):
        left = jnp.concatenate(
            [hold[0, pl.ds(w, rows, stride=width), :], hold[1, pl.ds(w, rows, stride=width), :]], 1
        ).astype(BF16)
        right = refl_ref[:, w].reshape(2 * sources, 2 * LANES)
        both = lax.dot_general(left, right, (((1,), (1,)), ((), ())), preferred_element_type=F32)
        by_real = both[:, :LANES].reshape(pieces, 2, focal, LANES)
        by_imag = both[:, LANES:].reshape(pieces, 2, focal, LANES)
        value = jnp.stack([by_real[:, 0] - by_imag[:, 1], by_real[:, 1] + by_imag[:, 0]], 1)
        result[pl.ds(w, rows, stride=width), :] = value.reshape(rows, LANES)
    share = focal // 4
    size = share * width
    for place, out in ((0, keep_ref), (1, send_ref)):
        for y in range(2):
            group = (2 * y + place) ^ me
            for k in range(pieces):
                for c in range(2):
                    start = ((k * 2 + c) * focal + group * share) * width
                    block = result[pl.ds(pl.multiple_of(start, size), size), :]
                    out[y, k, c] = block.reshape(share, width, LANES).astype(BF16)


def convolve_chunk(ids, reflection, own, other, chunk_index):
    pieces = len(own)
    parts, focal, chunk, lanes = own[0].shape
    sources = reflection.shape[2]
    steps = chunk // BLOCK_W
    offset = chunk_index * steps
    share = focal // 4
    rows = pieces * 2 * focal
    piece_spec = pl.BlockSpec((2, focal, BLOCK_W, LANES), lambda g, ids: (0, 0, g, 0))
    out_spec = pl.BlockSpec(
        (2, pieces, 2, share, BLOCK_W, LANES), lambda g, ids: (0, 0, 0, 0, g, 0)
    )
    out = jax.ShapeDtypeStruct((2, pieces, 2, share, chunk, LANES), BF16)
    return pl.pallas_call(
        functools.partial(convolve_kernel, pieces),
        name="convolve",
        out_shape=[out, out],
        grid_spec=pltpu.PrefetchScalarGridSpec(
            num_scalar_prefetch=1,
            grid=(steps,),
            in_specs=[
                pl.BlockSpec(
                    (2, BLOCK_W, sources, 2 * LANES), lambda g, ids: (0, offset + g, 0, 0)
                )
            ]
            + [piece_spec] * (2 * pieces),
            out_specs=[out_spec, out_spec],
            scratch_shapes=[
                pltpu.VMEM((2, rows * BLOCK_W, LANES), F32),
                pltpu.VMEM((rows * BLOCK_W, LANES), F32),
            ],
        ),
        compiler_params=params("arbitrary"),
        cost_estimate=pl.CostEstimate(
            flops=2 * chunk * rows * 256 * 256,
            bytes_accessed=chunk * (2 * sources * 512 + rows * 768),
            transcendentals=0,
        ),
    )(ids, reflection, *own, *other)


def correlate_kernel(pieces, ids, refl_ref, *refs):
    sources_of = [refs[j * pieces : (j + 1) * pieces] for j in range(4)]
    outs = refs[4 * pieces : 6 * pieces]
    hold, result = refs[6 * pieces :]
    half, me = ids[0], ids[1]
    share, width = refs[0].shape[1], refs[0].shape[2]
    focal = 4 * share
    sources = refl_ref.shape[2]
    rows = pieces * focal
    size = share * width
    for j in range(4):
        group = j ^ me
        for k in range(pieces):
            start = pl.multiple_of((k * focal + group * share) * width, size)
            for c in range(2):
                block = sources_of[j][k][c].astype(F32).reshape(size, LANES)
                hold[c, pl.ds(start, size), :] = block
    for w in range(width):
        real = hold[0, pl.ds(w, rows, stride=width), :].astype(BF16)
        imag = hold[1, pl.ds(w, rows, stride=width), :].astype(BF16)
        left = jnp.concatenate(
            [jnp.concatenate([real, imag], 1), jnp.concatenate([imag, -real], 1)], 0
        )
        right = refl_ref[:, w].reshape(2 * sources, 2 * LANES)
        value = lax.dot_general(left, right, (((1,), (0,)), ((), ())), preferred_element_type=F32)
        result[0, pl.ds(w, 2 * rows, stride=width), :] = value[:, :LANES]
        result[1, pl.ds(w, 2 * rows, stride=width), :] = value[:, LANES:]
    size = focal * width
    for place, group in ((half, outs[:pieces]), (1 - half, outs[pieces:])):
        for k in range(pieces):
            for c in range(2):
                block = result[place, pl.ds((c * pieces + k) * size, size), :]
                group[k][c] = block.reshape(focal, width, LANES).astype(BF16)


def correlate_chunk(ids, reflection, parts_of, chunk_index):
    pieces = len(parts_of[0])
    two, share, chunk, lanes = parts_of[0][0].shape
    focal = 4 * share
    sources = reflection.shape[2]
    steps = chunk // BLOCK_W
    offset = chunk_index * steps
    rows = pieces * 2 * focal
    in_spec = pl.BlockSpec((2, share, BLOCK_W, LANES), lambda g, ids: (0, 0, g, 0))
    out_spec = pl.BlockSpec((2, focal, BLOCK_W, LANES), lambda g, ids: (0, 0, g, 0))
    out = jax.ShapeDtypeStruct((2, focal, chunk, LANES), BF16)
    results = pl.pallas_call(
        functools.partial(correlate_kernel, pieces),
        name="correlate",
        out_shape=[out] * (2 * pieces),
        grid_spec=pltpu.PrefetchScalarGridSpec(
            num_scalar_prefetch=1,
            grid=(steps,),
            in_specs=[
                pl.BlockSpec(
                    (2, BLOCK_W, sources, 2 * LANES), lambda g, ids: (0, offset + g, 0, 0)
                )
            ]
            + [in_spec] * (4 * pieces),
            out_specs=[out_spec] * (2 * pieces),
            scratch_shapes=[
                pltpu.VMEM((2, rows // 2 * BLOCK_W, LANES), F32),
                pltpu.VMEM((2, rows * BLOCK_W, LANES), F32),
            ],
        ),
        compiler_params=params("arbitrary"),
        cost_estimate=pl.CostEstimate(
            flops=2 * chunk * rows * 256 * 256,
            bytes_accessed=chunk * (2 * sources * 512 + rows * 768),
            transcendentals=0,
        ),
    )(ids, reflection, *[v for group in parts_of for v in group])
    return results[:pieces], results[pieces:]


def gather_rows(refs, index):
    return jnp.concatenate([ref[c, index] for ref in refs for c in range(2)], 0)


def windowed(columns_ref, rows, onsets):
    signal = jnp.dot(columns_ref[...], rows, preferred_element_type=F32)
    sample = lax.broadcasted_iota(jnp.int32, signal.shape, 0)
    return jnp.where(sample < onsets, signal, 0.0).astype(BF16)


def mute_source_kernel(count, ids, onset_ref, rows_ref, columns_ref, *refs):
    ins, outs = refs[:count], refs[count:]
    share, width = ins[0].shape[1], ins[0].shape[2]
    first = ids[1] * share
    spectrum = jnp.concatenate([gather_rows(ins, p) for p in range(share)], 1)
    onsets = jnp.concatenate([onset_ref[pl.ds(first + p, 1), :] for p in range(share)], 1)
    muted = windowed(columns_ref, spectrum, onsets)
    back = jnp.dot(rows_ref[...], muted, preferred_element_type=F32).astype(BF16)
    for i, out in enumerate(outs):
        for c in range(2):
            for p in range(share):
                start = (2 * i + c) * width
                out[c, p] = back[start : start + width, p * LANES : (p + 1) * LANES]


def whole(shape):
    return pl.BlockSpec(shape, lambda *index: (0,) * len(shape))


def mute_source(ids, onset, rows, columns, pieces):
    shape = pieces[0].shape
    count = len(pieces)
    return pl.pallas_call(
        functools.partial(mute_source_kernel, count),
        name="mute_source",
        out_shape=[jax.ShapeDtypeStruct(shape, BF16)] * count,
        grid_spec=pltpu.PrefetchScalarGridSpec(
            num_scalar_prefetch=1,
            grid=(1,),
            in_specs=[whole(onset.shape), whole(rows.shape), whole(columns.shape)]
            + [whole(shape)] * count,
            out_specs=[whole(shape)] * count,
        ),
        compiler_params=params("arbitrary"),
        cost_estimate=pl.CostEstimate(
            flops=4 * NT * 2 * F * shape[1] * LANES, bytes_accessed=3 << 20, transcendentals=0
        ),
    )(ids, onset, rows, columns, *pieces)


def trace_kernel(pieces, ids, onset_ref, rows_ref, *refs):
    ins, out_ref, hold = refs[:-2], refs[-2], refs[-1]
    share = ins[0].shape[1]
    step = pl.program_id(0)
    count = len(ins) // 4

    @pl.when(step == 0)
    def unpack():
        for j in range(4):
            for p in range(share):
                hold[j * share + p] = gather_rows(ins[j * count : (j + 1) * count], p)

    signal = lax.dot_general(
        hold[step], rows_ref[...], (((0,), (0,)), ((), ())), preferred_element_type=F32
    )
    sample = lax.broadcasted_iota(jnp.int32, signal.shape, 1)
    out_ref[0] = jnp.where(sample < onset_ref[0], signal, 0.0).astype(BF16)


def trace_source(ids, onset, rows, parts_of):
    focal, sources = onset.shape
    shape = parts_of[0][0].shape
    share = shape[1]
    flat = [v for group in parts_of for v in group]

    def place(g, ids):
        return ((g // share) ^ ids[1]) * share + g % share, 0, 0

    return pl.pallas_call(
        functools.partial(trace_kernel, len(parts_of[0])),
        name="trace_source",
        out_shape=jax.ShapeDtypeStruct((focal, sources, NT), BF16),
        grid_spec=pltpu.PrefetchScalarGridSpec(
            num_scalar_prefetch=1,
            grid=(focal,),
            in_specs=[pl.BlockSpec((1, sources, 1), place), whole(rows.shape)]
            + [whole(shape)] * len(flat),
            out_specs=pl.BlockSpec((1, sources, NT), place),
            scratch_shapes=[pltpu.VMEM((focal, 2 * F, LANES), BF16)],
        ),
        compiler_params=params("arbitrary"),
        cost_estimate=pl.CostEstimate(
            flops=2 * NT * 2 * F * focal * LANES, bytes_accessed=5 << 20, transcendentals=0
        ),
    )(ids, onset[:, :, None], rows, *flat)


def updated(count, ids, onset_ref, rows_ref, columns_ref, refs, step, group):
    ins, arrived, direct = refs[0], refs[1], refs[2]
    spectra = []
    for p in range(group):
        parts = []
        for i, ref in enumerate(ins):
            for c in range(2):
                value = ref[c, p]
                if i in arrived:
                    value = (value.astype(F32) + arrived[i][c, p].astype(F32)).astype(BF16)
                parts.append(value)
        spectra.append(jnp.concatenate(parts, 0))
    onsets = jnp.concatenate(
        [onset_ref[pl.ds(step * group + p, 1), :] for p in range(group)], 1
    )
    muted = windowed(columns_ref, jnp.concatenate(spectra, 1), onsets)
    back = jnp.dot(rows_ref[...], muted, preferred_element_type=F32)
    width = ins[0].shape[2]
    for i in range(count):
        for c in range(2):
            for p in range(group):
                start = (2 * i + c) * width
                block = back[start : start + width, p * LANES : (p + 1) * LANES]
                yield i, c, p, direct[i][c, p].astype(F32) + block


def mute_receiver_kernel(count, own, ids, onset_ref, rows_ref, columns_ref, *refs):
    ins, extra = refs[:count], refs[count : count + len(own)]
    direct = refs[count + len(own) : 2 * count + len(own)]
    outs = refs[2 * count + len(own) :]
    group = ins[0].shape[1]
    state = (ins, dict(zip(own, extra)), direct)
    step = pl.program_id(0)
    for i, c, p, value in updated(
        count, ids, onset_ref, rows_ref, columns_ref, state, step, group
    ):
        outs[i][c, p] = value.astype(BF16)


def mute_receiver_last_kernel(
    count, own, pieces, ids, onset_ref, rows_ref, columns_ref, *refs
):
    ins, extra = refs[:count], refs[count : count + len(own)]
    direct = refs[count + len(own) : 2 * count + len(own)]
    out_ref, hold = refs[2 * count + len(own) :]
    group, width = ins[0].shape[1], ins[0].shape[2]
    focal = out_ref.shape[2]
    chunks = count // pieces
    state = (ins, dict(zip(own, extra)), direct)
    step = pl.program_id(0)
    for i, c, p, value in updated(
        count, ids, onset_ref, rows_ref, columns_ref, state, step, group
    ):
        chunk, k = i // pieces, i % pieces
        first = c * F + ((k ^ ids[2]) * chunks + chunk) * width
        hold[pl.ds(first * focal + step * group + p, width, stride=focal), :] = value

    @pl.when(step == pl.num_programs(0) - 1)
    def flush():
        out_ref[...] = hold[...].astype(BF16).reshape(out_ref.shape)


def mute_receiver(ids, onset, rows, columns, pieces, arrived, direct, last, piece_count):
    shape = pieces[0].shape
    focal = shape[1]
    count = len(pieces)
    own = sorted(arrived)
    group = 2
    steps = focal // group
    spec = pl.BlockSpec((2, group) + shape[2:], lambda g, ids: (0, g, 0, 0))
    common = dict(
        num_scalar_prefetch=1,
        grid=(steps,),
        in_specs=[
            pl.BlockSpec((focal, LANES), lambda g, ids: (0, ids[0])),
            whole(rows.shape),
            whole(columns.shape),
        ]
        + [spec] * (2 * count + len(own)),
    )
    if last:
        kernel = functools.partial(mute_receiver_last_kernel, count, own, piece_count)
        out_shape = jax.ShapeDtypeStruct((2, F, focal, LANES), BF16)
        grid_spec = pltpu.PrefetchScalarGridSpec(
            out_specs=whole(out_shape.shape),
            scratch_shapes=[pltpu.VMEM((2 * F * focal, LANES), F32)],
            **common,
        )
    else:
        kernel = functools.partial(mute_receiver_kernel, count, own)
        out_shape = [jax.ShapeDtypeStruct(shape, BF16)] * count
        grid_spec = pltpu.PrefetchScalarGridSpec(out_specs=[spec] * count, **common)
    return pl.pallas_call(
        kernel,
        name="mute_receiver",
        out_shape=out_shape,
        grid_spec=grid_spec,
        compiler_params=params("arbitrary"),
        cost_estimate=pl.CostEstimate(
            flops=4 * NT * 2 * F * focal * LANES, bytes_accessed=5 << 20, transcendentals=0
        ),
    )(ids, onset, rows, columns, *pieces, *[arrived[i] for i in own], *direct)


def join_kernel(ids, own_ref, other_ref, out_ref):
    half = ids[0]
    out_ref[:, :, :, pl.ds(pl.multiple_of(half * LANES, LANES), LANES)] = own_ref[...]
    out_ref[:, :, :, pl.ds(pl.multiple_of((1 - half) * LANES, LANES), LANES)] = other_ref[...]


def join_halves(ids, own, other):
    two, freq, focal, lanes = own.shape
    step = freq // 4
    spec = pl.BlockSpec((1, step, focal, lanes), lambda c, g, ids: (c, g, 0, 0))
    return pl.pallas_call(
        join_kernel,
        name="join_halves",
        out_shape=jax.ShapeDtypeStruct((two, freq, focal, 2 * lanes), BF16),
        grid_spec=pltpu.PrefetchScalarGridSpec(
            num_scalar_prefetch=1,
            grid=(two, 4),
            in_specs=[spec, spec],
            out_specs=pl.BlockSpec((1, step, focal, 2 * lanes), lambda c, g, ids: (c, g, 0, 0)),
        ),
        compiler_params=params("arbitrary", "arbitrary"),
        cost_estimate=pl.CostEstimate(
            flops=0, bytes_accessed=8 * two * freq * focal * lanes, transcendentals=0
        ),
    )(ids, own, other)


def add(left, right):
    return (left.astype(F32) + right.astype(F32)).astype(BF16)


def resident(counts, reflection, direct_wave, onset_receiver, onset_source):
    src_count, rcv_count, foc_count = counts
    ids = jnp.stack([lax.axis_index("src"), lax.axis_index("rcv"), lax.axis_index("foc")])
    ids = ids.astype(jnp.int32)
    freq = reflection.shape[1]
    pieces = range(foc_count)
    order = [k for k in (2, 3, 1, 0) if k < foc_count]
    chunks = range(CHUNKS)

    def to_foc(value, k):
        return value if k == 0 else swap(value, "foc", k, foc_count)

    def to_src(value):
        return swap(value, "src", 1, src_count)

    def to_core(value):
        return swap(value, "rcv", 1, rcv_count)

    def to_y(value):
        return swap(value, "rcv", 2, rcv_count)

    direct = [[None] * foc_count for c in chunks]
    for k in order:
        for c, value in enumerate(split_wave(ids, direct_wave, k, foc_count, CHUNKS)):
            direct[c][k] = value
    rows, columns = ordered_basis(ids[2], foc_count, freq, CHUNKS)
    focusing = direct
    muted_trace = None
    for iteration in range(ITERS):
        last = iteration == ITERS - 1
        spectrum = []
        for c in chunks:
            own = [to_foc(focusing[c][k], k) for k in pieces]
            other = [to_src(value) for value in own]
            keep, send = convolve_chunk(ids, reflection, own, other, c)
            got = to_core(send)
            beyond = to_y(add(keep[1], got[1]))
            total = (
                keep[0].astype(F32) + got[0].astype(F32) + beyond.astype(F32)
            ).astype(BF16)
            spectrum += [to_foc(total[k], k) for k in pieces]
        returned = mute_source(ids, onset_source, rows, columns, spectrum)
        kept = [[None] * foc_count for c in chunks]
        arrived = {}
        ready = [[None] * foc_count for c in chunks]
        for c in chunks:
            mine = [to_foc(returned[c * foc_count + k], k) for k in pieces]
            across = [to_y(value) for value in mine]
            groups = [mine, [to_core(v) for v in mine], across, [to_core(v) for v in across]]
            own, other = correlate_chunk(ids, reflection, groups, c)
            for k in order:
                got = to_src(other[k])
                if k == 0:
                    ready[c][k] = own[k]
                    arrived[c * foc_count] = got
                else:
                    ready[c][k] = to_foc(add(own[k], got), k)
        flat = [v for group in ready for v in group]
        flat_direct = [v for group in direct for v in group]
        renewed = mute_receiver(
            ids, onset_receiver, rows, columns, flat, arrived, flat_direct, last, foc_count
        )
        if last:
            across = [to_y(value) for value in spectrum]
            groups = [
                spectrum,
                [to_core(v) for v in spectrum],
                across,
                [to_core(v) for v in across],
            ]
            muted_trace = trace_source(ids, onset_source, rows, groups)
            return join_halves(ids, renewed, to_src(renewed)), muted_trace
        focusing = [renewed[c * foc_count : (c + 1) * foc_count] for c in chunks]


def local(counts, reflection, direct_wave, onset_receiver, onset_source):
    src_count, rcv_count, foc_count = counts
    two, freq, sources, receivers = reflection.shape
    focal = direct_wave.shape[2]
    fits = (
        (src_count, rcv_count) == (2, 4)
        and foc_count in (2, 4)
        and sources == LANES
        and receivers == 2 * LANES
        and focal == 8
        and freq % (CHUNKS * BLOCK_W) == 0
        and freq * foc_count == F
    )
    if fits:
        return resident(counts, reflection, direct_wave, onset_receiver, onset_source)
    return general(reflection, direct_wave, onset_receiver, onset_source)


def solution(mesh):
    in_specs = (
        P(None, "foc", "src", "rcv"),
        P(None, None, "foc", "rcv"),
        P("foc", "rcv"),
        P("foc", "src"),
    )
    out_specs = (P(None, None, "foc", "rcv"), P("foc", "src", None))
    counts = (mesh.shape["src"], mesh.shape["rcv"], mesh.shape["foc"])
    return jax.shard_map(
        functools.partial(local, counts),
        mesh=mesh,
        in_specs=in_specs,
        out_specs=out_specs,
        check_vma=False,
    )
```

```python
import functools
import math

import jax
import jax.numpy as jnp
from jax import lax
from jax.experimental import pallas as pl
from jax.experimental.pallas import tpu as pltpu
from jax.sharding import PartitionSpec as P

F = 256
NT = 1024
ITERS = 2
LANES = 128
BLOCK_W = 16
HALVES = 2
F32 = jnp.float32
BF16 = jnp.bfloat16
VMEM_BYTES = 24 * 1024 * 1024


def basis_table():
    frequency_bins = jnp.arange(F, dtype=jnp.int32) + 1
    samples = jnp.arange(NT, dtype=jnp.int32)
    phases = frequency_bins[:, None] * samples[None, :] % NT
    angles = phases.astype(jnp.float32) * (2.0 * math.pi / NT)
    norming = math.sqrt(2.0 / NT)
    return (jnp.stack([jnp.cos(angles), -jnp.sin(angles)]) * norming).astype(jnp.bfloat16)


def mute_traces(spectrum, onsets, basis_rows):
    focal_count = spectrum.shape[2]
    samples = jnp.arange(NT, dtype=jnp.int32)

    def one_focus(focal_index, carry):
        muted_all, returned_all = carry
        one_spectrum = lax.dynamic_slice_in_dim(spectrum, focal_index, 1, 2)
        one_onset = lax.dynamic_slice_in_dim(onsets, focal_index, 1, 0)
        signal = jnp.einsum(
            "cwpr,cwt->prt", one_spectrum, basis_rows, preferred_element_type=jnp.float32
        )
        window = samples[None, None, :] < one_onset[:, :, None]
        muted_one = jnp.where(window, signal, 0.0).astype(jnp.bfloat16)
        returned = jnp.einsum(
            "prt,cwt->cwpr", muted_one, basis_rows, preferred_element_type=jnp.float32
        )
        muted_all = lax.dynamic_update_slice_in_dim(muted_all, muted_one, focal_index, 0)
        returned_all = lax.dynamic_update_slice_in_dim(returned_all, returned, focal_index, 2)
        return (muted_all, returned_all)

    initial = (
        jnp.zeros((focal_count, spectrum.shape[3], NT), jnp.bfloat16),
        jnp.zeros(spectrum.shape, jnp.float32),
    )
    return lax.fori_loop(0, focal_count, one_focus, initial)


def convolve(reflection, focusing):
    real_out = jnp.einsum(
        "wsr,wpr->wps", reflection[0], focusing[0], preferred_element_type=jnp.float32
    ) - jnp.einsum("wsr,wpr->wps", reflection[1], focusing[1], preferred_element_type=jnp.float32)
    imag_out = jnp.einsum(
        "wsr,wpr->wps", reflection[0], focusing[1], preferred_element_type=jnp.float32
    ) + jnp.einsum("wsr,wpr->wps", reflection[1], focusing[0], preferred_element_type=jnp.float32)
    return jnp.stack([real_out, imag_out])


def correlate(reflection, spectrum):
    real_out = jnp.einsum(
        "wsr,wps->wpr", reflection[0], spectrum[0], preferred_element_type=jnp.float32
    ) + jnp.einsum("wsr,wps->wpr", reflection[1], spectrum[1], preferred_element_type=jnp.float32)
    imag_out = jnp.einsum(
        "wsr,wps->wpr", reflection[0], spectrum[1], preferred_element_type=jnp.float32
    ) - jnp.einsum("wsr,wps->wpr", reflection[1], spectrum[0], preferred_element_type=jnp.float32)
    return jnp.stack([real_out, imag_out])


def renew(shares, direct_wave, onset_receiver, basis_rows, source_index):
    share_width = shares.shape[3]
    offset = source_index * share_width
    onset_share = lax.dynamic_slice_in_dim(onset_receiver, offset, share_width, 1)
    direct_share = lax.dynamic_slice_in_dim(direct_wave, offset, share_width, 3)
    unused, update = mute_traces(shares, onset_share, basis_rows)
    renewed = (direct_share.astype(jnp.float32) + update).astype(jnp.bfloat16)
    return lax.all_gather(renewed, "src", axis=3, tiled=True)


def general(reflection, direct_wave, onset_receiver, onset_source):
    basis_rows = basis_table()
    source_index = lax.axis_index("src")
    whole_reflection = lax.all_gather(reflection, "foc", axis=1, tiled=True)
    focusing = direct_wave
    muted_trace = None
    for iteration in range(ITERS):
        partial_value = convolve(whole_reflection, focusing)
        spectrum = lax.psum(partial_value.astype(jnp.bfloat16), "rcv")
        muted_trace, returned = mute_traces(spectrum, onset_source, basis_rows)
        partial_adjoint = correlate(whole_reflection, returned.astype(jnp.bfloat16))
        shares = lax.psum_scatter(
            partial_adjoint.astype(jnp.bfloat16), "src", scatter_dimension=3, tiled=True
        )
        focusing = renew(shares, direct_wave, onset_receiver, basis_rows, source_index)
    return (focusing, muted_trace)


VMEM_SPEC = pl.BlockSpec(memory_space=pltpu.VMEM)
SMEM_SPEC = pl.BlockSpec(memory_space=pltpu.SMEM)


def swap(value, axis, mask, count):
    return lax.ppermute(value, axis, [(i, i ^ mask) for i in range(count)])


def call(kernel, name, out_shape, flops, size, operands, scratch=()):
    many = isinstance(out_shape, list)
    return pl.pallas_call(
        kernel,
        name=name,
        out_shape=out_shape,
        in_specs=[SMEM_SPEC] + [VMEM_SPEC] * (len(operands) - 1),
        out_specs=[VMEM_SPEC] * len(out_shape) if many else VMEM_SPEC,
        scratch_shapes=list(scratch),
        compiler_params=pltpu.CompilerParams(vmem_limit_bytes=VMEM_BYTES),
        cost_estimate=pl.CostEstimate(flops=flops, bytes_accessed=size, transcendentals=0),
    )(*operands)


def table(frequency, part, sample):
    phase = ((frequency + 1) * sample + part * (NT // 4)) & (NT - 1)
    x = (jnp.abs(phase - NT // 2) - NT // 4).astype(F32) * (4.0 / NT)
    square = x * x
    total = jnp.zeros_like(x)
    for order in (11, 9, 7, 5, 3, 1):
        sign = -1.0 if order % 4 == 3 else 1.0
        total = total * square + sign * (math.pi / 2) ** order / math.factorial(order)
    return (total * x * math.sqrt(2.0 / NT)).astype(BF16)


def basis_kernel(ids, rows_ref, columns_ref):
    size = rows_ref.shape[0]
    freq = BLOCK_W * 4
    pieces = size // (2 * freq)
    for k in range(pieces):
        first = (k ^ ids[2]) * freq
        for c in range(2):
            frequency = lax.broadcasted_iota(jnp.int32, (freq, NT), 0) + first
            sample = lax.broadcasted_iota(jnp.int32, (freq, NT), 1)
            start = (2 * k + c) * freq
            rows_ref[start : start + freq, :] = table(frequency, c, sample)
        lane = lax.broadcasted_iota(jnp.int32, (NT, 2 * freq), 1)
        sample = lax.broadcasted_iota(jnp.int32, (NT, 2 * freq), 0)
        part = (lane >= freq).astype(jnp.int32)
        start = 2 * k * freq
        columns_ref[:, start : start + 2 * freq] = table(lane - part * freq + first, part, sample)


def basis(ids):
    size = 2 * F
    return call(
        basis_kernel,
        "basis",
        [jax.ShapeDtypeStruct((size, NT), BF16), jax.ShapeDtypeStruct((NT, size), BF16)],
        40 * size * NT,
        4 * size * NT,
        (ids,),
    )


def split_kernel(both, ids, wave_ref, out_ref, hold):
    width, focal = wave_ref.shape[1], wave_ref.shape[2]
    for place in range(2 if both else 1):
        lanes = slice(place * LANES, (place + 1) * LANES)
        hold[...] = wave_ref[0, :, :, lanes].astype(F32).reshape(width * focal, LANES)
        for p in range(focal):
            rows = hold[pl.ds(p, width, stride=focal), :].astype(BF16)
            if both:
                out_ref[place, 0, p] = rows
            else:
                out_ref[0, p] = rows


def split_wave(ids, wave, piece, foc_count, both):
    freq = wave.shape[1] // foc_count
    focal = wave.shape[2]
    if both:
        shape = (2, 2, focal, freq, LANES)
        in_spec = pl.BlockSpec(
            (1, freq, focal, 2 * LANES), lambda c, ids: (c, ids[2] ^ piece, 0, 0)
        )
        out_spec = pl.BlockSpec((2, 1, focal, freq, LANES), lambda c, ids: (0, c, 0, 0, 0))
    else:
        shape = (2, focal, freq, LANES)
        in_spec = pl.BlockSpec(
            (1, freq, focal, LANES), lambda c, ids: (c, ids[2] ^ piece, 0, ids[0])
        )
        out_spec = pl.BlockSpec((1, focal, freq, LANES), lambda c, ids: (c, 0, 0, 0))
    return pl.pallas_call(
        functools.partial(split_kernel, both),
        name="split_wave",
        out_shape=jax.ShapeDtypeStruct(shape, BF16),
        grid_spec=pltpu.PrefetchScalarGridSpec(
            num_scalar_prefetch=1,
            grid=(2,),
            in_specs=[in_spec],
            out_specs=out_spec,
            scratch_shapes=[pltpu.VMEM((freq * focal, LANES), F32)],
        ),
        compiler_params=pltpu.CompilerParams(vmem_limit_bytes=VMEM_BYTES),
        cost_estimate=pl.CostEstimate(
            flops=0, bytes_accessed=8 * focal * freq * LANES, transcendentals=0
        ),
    )(ids, wave)


def convolve_kernel(plan, pieces, focal, ids, refl_ref, *refs):
    ins = refs[: len(plan)]
    keep_ref, send_ref, hold, result = refs[len(plan) :]
    half, me = ids[0], ids[1]
    sources = refl_ref.shape[2]
    rows = pieces * 2 * focal
    share = focal // 4

    def block(b, carry):
        first = pl.multiple_of(b * BLOCK_W, BLOCK_W)
        window = pl.ds(first, BLOCK_W)

        def put(place, k, c, start, value):
            size = value.shape[0] * BLOCK_W
            at = ((k * 2 + c) * focal + start) * BLOCK_W
            hold[place, at : at + size, :] = value.astype(F32).reshape(size, LANES)

        for ref, (kind, k, start) in zip(ins, plan):
            for c in range(2):
                if kind == "both":
                    put(0, k, c, start, ref[0, c, :, window, :])
                    put(1, k, c, start, ref[1, c, :, window, :])
                elif kind == "own":
                    put(half, k, c, start, ref[c, :, window, :])
                else:
                    put(1 - half, k, c, start, ref[c, :, window, :])
        for w in range(BLOCK_W):
            step = pl.ds(w, rows, stride=BLOCK_W)
            left = jnp.concatenate([hold[0, step, :], hold[1, step, :]], 1).astype(BF16)
            right = refl_ref[:, first + w].reshape(2 * sources, 2 * LANES)
            both = lax.dot_general(
                left, right, (((1,), (1,)), ((), ())), preferred_element_type=F32
            )
            by_real = both[:, :LANES].reshape(pieces, 2, focal, LANES)
            by_imag = both[:, LANES:].reshape(pieces, 2, focal, LANES)
            value = jnp.stack(
                [by_real[:, 0] - by_imag[:, 1], by_real[:, 1] + by_imag[:, 0]], 1
            )
            result[step, :] = value.reshape(rows, LANES)
        size = share * BLOCK_W
        for place, out in ((0, keep_ref), (1, send_ref)):
            for y in range(2):
                group = (2 * y + place) ^ me
                for k in range(pieces):
                    for c in range(2):
                        start = ((k * 2 + c) * focal + group * share) * BLOCK_W
                        part = result[pl.ds(pl.multiple_of(start, size), size), :]
                        out[y, k, c, :, window, :] = part.reshape(
                            share, BLOCK_W, LANES
                        ).astype(BF16)
        return carry

    lax.fori_loop(0, refl_ref.shape[1] // BLOCK_W, block, 0)


def convolve_pieces(ids, reflection, plan, arrays, pieces, focal):
    two, freq, sources, receivers = reflection.shape
    rows = pieces * 2 * focal
    out = jax.ShapeDtypeStruct((2, pieces, 2, focal // 4, freq, LANES), BF16)
    return call(
        functools.partial(convolve_kernel, plan, pieces, focal),
        "convolve",
        [out, out],
        2 * freq * rows * 256 * 256,
        freq * (2 * sources * 512 + rows * 768),
        (ids, reflection, *arrays),
        [
            pltpu.VMEM((2, rows * BLOCK_W, LANES), F32),
            pltpu.VMEM((rows * BLOCK_W, LANES), F32),
        ],
    )


def correlate_kernel(pieces, ids, refl_ref, *refs):
    ins = [refs[j * pieces : (j + 1) * pieces] for j in range(4)]
    outs = refs[4 * pieces : -2]
    hold, result = refs[-2:]
    half, me = ids[0], ids[1]
    share = ins[0][0].shape[1]
    focal = 4 * share
    sources = refl_ref.shape[2]
    rows = pieces * focal
    part_size = focal // HALVES

    def block(b, carry):
        first = pl.multiple_of(b * BLOCK_W, BLOCK_W)
        window = pl.ds(first, BLOCK_W)
        size = share * BLOCK_W
        for j in range(4):
            group = j ^ me
            for k in range(pieces):
                start = pl.multiple_of((k * focal + group * share) * BLOCK_W, size)
                for c in range(2):
                    value = ins[j][k][c, :, window, :].astype(F32).reshape(size, LANES)
                    hold[c, pl.ds(start, size), :] = value
        for w in range(BLOCK_W):
            step = pl.ds(w, rows, stride=BLOCK_W)
            real = hold[0, step, :].astype(BF16)
            imag = hold[1, step, :].astype(BF16)
            left = jnp.concatenate(
                [jnp.concatenate([real, imag], 1), jnp.concatenate([imag, -real], 1)], 0
            )
            right = refl_ref[:, first + w].reshape(2 * sources, 2 * LANES)
            value = lax.dot_general(
                left, right, (((1,), (0,)), ((), ())), preferred_element_type=F32
            )
            step = pl.ds(w, 2 * rows, stride=BLOCK_W)
            result[0, step, :] = value[:, :LANES]
            result[1, step, :] = value[:, LANES:]
        size = part_size * BLOCK_W
        index = 0
        for place in (half, 1 - half):
            for q in range(HALVES):
                for group in PAIRS:
                    for i, k in enumerate(group):
                        for c in range(2):
                            at = ((c * pieces + k) * focal + q * part_size) * BLOCK_W
                            part = result[place, at : at + size, :]
                            outs[index][i, c, :, window, :] = part.reshape(
                                part_size, BLOCK_W, LANES
                            ).astype(BF16)
                    index += 1
        return carry

    lax.fori_loop(0, refl_ref.shape[1] // BLOCK_W, block, 0)


PAIRS = ((2, 3), (1, 0))


def correlate_pieces(ids, reflection, groups):
    pieces = len(groups[0])
    two, share, freq, lanes = groups[0][0].shape
    focal = 4 * share
    sources = reflection.shape[2]
    rows = pieces * 2 * focal
    out = jax.ShapeDtypeStruct((2, 2, focal // HALVES, freq, LANES), BF16)
    count = HALVES * len(PAIRS)
    results = call(
        functools.partial(correlate_kernel, pieces),
        "correlate",
        [out] * (2 * count),
        2 * freq * rows * 256 * 256,
        freq * (2 * sources * 512 + rows * 768),
        (ids, reflection, *[v for group in groups for v in group]),
        [
            pltpu.VMEM((2, rows // 2 * BLOCK_W, LANES), F32),
            pltpu.VMEM((2, rows * BLOCK_W, LANES), F32),
        ],
    )
    return results[:count], results[count:]


def windowed(columns_ref, rows, onsets):
    signal = jnp.dot(columns_ref[...], rows, preferred_element_type=F32)
    sample = lax.broadcasted_iota(jnp.int32, signal.shape, 0)
    return jnp.where(sample < onsets, signal, 0.0).astype(BF16)


def mute_source_kernel(copy, ids, onset_ref, rows_ref, columns_ref, *refs):
    pieces = (len(refs) - copy) // 2
    ins, outs = refs[:pieces], refs[pieces : 2 * pieces]
    share, width = ins[0].shape[1], ins[0].shape[2]
    first = ids[1] * share
    if copy:
        for k in range(pieces):
            refs[-1][k] = ins[k][...]
    spectrum = jnp.concatenate(
        [
            jnp.concatenate([ref[c, p] for ref in ins for c in range(2)], 0)
            for p in range(share)
        ],
        1,
    )
    onsets = jnp.concatenate([onset_ref[pl.ds(first + p, 1), :] for p in range(share)], 1)
    muted = windowed(columns_ref, spectrum, onsets)
    back = jnp.dot(rows_ref[...], muted, preferred_element_type=F32).astype(BF16)
    for i, out in enumerate(outs):
        for c in range(2):
            for p in range(share):
                start = (2 * i + c) * width
                out[c, p] = back[start : start + width, p * LANES : (p + 1) * LANES]


def mute_source(ids, onset, rows, columns, pieces, copy):
    shape = pieces[0].shape
    outs = [jax.ShapeDtypeStruct(shape, BF16)] * len(pieces)
    if copy:
        outs = outs + [jax.ShapeDtypeStruct((len(pieces),) + shape, BF16)]
    return call(
        functools.partial(mute_source_kernel, int(copy)),
        "mute_source",
        outs,
        4 * NT * 2 * F * shape[1] * LANES,
        3 << 20,
        (ids, onset, rows, columns, *pieces),
    )


def trace_kernel(ids, onset_ref, rows_ref, *refs):
    ins, out_ref = refs[:4], refs[4]
    pieces, two, share = ins[0].shape[:3]
    step = pl.program_id(0)
    for j in range(4):

        @pl.when(step // share == j)
        def one():
            p = step % share
            spectrum = jnp.concatenate(
                [ins[j][k, c, p] for k in range(pieces) for c in range(2)], 0
            )
            signal = lax.dot_general(
                spectrum, rows_ref[...], (((0,), (0,)), ((), ())), preferred_element_type=F32
            )
            sample = lax.broadcasted_iota(jnp.int32, signal.shape, 1)
            out_ref[0] = jnp.where(sample < onset_ref[0], signal, 0.0).astype(BF16)


def trace_source(ids, onset, rows, groups):
    focal, sources = onset.shape
    share = groups[0].shape[2]

    def place(g, ids):
        return ((g // share) ^ ids[1]) * share + g % share, 0, 0

    return pl.pallas_call(
        trace_kernel,
        name="trace_source",
        out_shape=jax.ShapeDtypeStruct((focal, sources, NT), BF16),
        grid_spec=pltpu.PrefetchScalarGridSpec(
            num_scalar_prefetch=1,
            grid=(focal,),
            in_specs=[pl.BlockSpec((1, sources, 1), place)] + [VMEM_SPEC] * 5,
            out_specs=pl.BlockSpec((1, sources, NT), place),
        ),
        compiler_params=pltpu.CompilerParams(vmem_limit_bytes=VMEM_BYTES),
        cost_estimate=pl.CostEstimate(
            flops=2 * NT * 2 * F * focal * LANES, bytes_accessed=5 << 20, transcendentals=0
        ),
    )(ids, onset[:, :, None], rows, *groups)


def mute_receiver_kernel(first, both, last, ids, onset_ref, rows_ref, columns_ref, *refs):
    near, extra, one, two, three = refs[:5]
    pieces = 4
    direct = refs[5 : 5 + pieces]
    outs = refs[5 + pieces :]
    half = ids[0]
    count, width = one.shape[1], one.shape[2]
    lanes = pl.ds(pl.multiple_of(half * LANES, LANES), LANES)

    def part(k, c, p):
        if k == 0:
            return (near[1, c, p].astype(F32) + extra[1, c, p].astype(F32)).astype(BF16)
        return (None, one, two, three)[k][c, p]

    step = 2
    for start in range(0, count, step):
        group = range(start, start + step)
        spectrum = jnp.concatenate(
            [
                jnp.concatenate([part(k, c, p) for k in range(pieces) for c in range(2)], 0)
                for p in group
            ],
            1,
        )
        onsets = jnp.concatenate(
            [onset_ref[first + p : first + p + 1, lanes] for p in group], 1
        )
        muted = windowed(columns_ref, spectrum, onsets)
        back = jnp.dot(rows_ref[...], muted, preferred_element_type=F32)
        for k in range(pieces):
            for c in range(2):
                for i, p in enumerate(group):
                    at = (2 * k + c) * width
                    block = back[at : at + width, i * LANES : (i + 1) * LANES]
                    if k in both:
                        wave = direct[k][half, c, first + p]
                    else:
                        wave = direct[k][c, first + p]
                    value = (wave.astype(F32) + block).astype(BF16)
                    if last:
                        outs[0][c, k ^ ids[2], p] = value
                    else:
                        outs[k][c, p] = value


def mute_receiver(ids, onset, rows, columns, arrays, direct, first, both, last):
    shape = arrays[2].shape
    count, freq = shape[1], shape[2]
    if last:
        outs = jax.ShapeDtypeStruct((2, 4, count, freq, LANES), BF16)
    else:
        outs = [jax.ShapeDtypeStruct(shape, BF16)] * 4
    return call(
        functools.partial(mute_receiver_kernel, first, both, last),
        "mute_receiver",
        outs,
        4 * NT * 2 * F * count * LANES,
        4 << 20,
        (ids, onset, rows, columns, *arrays, *direct),
    )


def join_kernel(ids, *refs):
    ins, out_ref, hold = refs[:HALVES], refs[-2], refs[-1]
    two, one, count, width, lanes = ins[0].shape
    focal = HALVES * count
    for c in range(2):
        for q, ref in enumerate(ins):
            for p in range(count):
                hold[pl.ds(c * width * focal + q * count + p, width, stride=focal), :] = ref[
                    c, 0, p
                ].astype(F32)
    out_ref[...] = hold[...].astype(BF16).reshape(out_ref.shape)


def join_halves(ids, parts, mask, into=None):
    two, foc_count, count, freq, lanes = parts[0].shape
    focal = HALVES * count
    spec = pl.BlockSpec((two, 1, count, freq, lanes), lambda g, ids: (0, g, 0, 0, 0))
    extra = [] if into is None else [into]
    return pl.pallas_call(
        join_kernel,
        name="join_halves",
        out_shape=jax.ShapeDtypeStruct((two, foc_count * freq, focal, 2 * lanes), BF16),
        grid_spec=pltpu.PrefetchScalarGridSpec(
            num_scalar_prefetch=1,
            grid=(foc_count,),
            in_specs=[spec] * HALVES + [pl.BlockSpec(memory_space=pl.ANY)] * len(extra),
            out_specs=pl.BlockSpec(
                (two, freq, focal, lanes), lambda g, ids: (0, g, 0, ids[0] ^ mask)
            ),
            scratch_shapes=[pltpu.VMEM((two * freq * focal, lanes), F32)],
        ),
        input_output_aliases={1 + HALVES: 0} if extra else {},
        compiler_params=pltpu.CompilerParams(vmem_limit_bytes=VMEM_BYTES),
        cost_estimate=pl.CostEstimate(
            flops=0, bytes_accessed=8 * foc_count * freq * focal * lanes, transcendentals=0
        ),
    )(ids, *parts, *extra)


def add(left, right):
    return (left.astype(F32) + right.astype(F32)).astype(BF16)


def resident(counts, reflection, direct_wave, onset_receiver, onset_source):
    src_count, rcv_count, foc_count = counts
    ids = jnp.stack([lax.axis_index("src"), lax.axis_index("rcv"), lax.axis_index("foc")])
    ids = ids.astype(jnp.int32)
    focal = direct_wave.shape[2]
    pieces = range(foc_count)
    near = (0, 1)

    def to_foc(value, k):
        return value if k == 0 else swap(value, "foc", k, foc_count)

    def to_src(value):
        return swap(value, "src", 1, src_count)

    def to_core(value):
        return swap(value, "rcv", 1, rcv_count)

    def to_y(value):
        return swap(value, "rcv", 2, rcv_count)

    direct = [None] * foc_count
    for k in (2, 3, 1, 0):
        direct[k] = split_wave(ids, direct_wave, k, foc_count, k in near)
    rows, columns = basis(ids)
    plan, arrays = [("both", 0, 0)], [direct[0]]
    for k in (2, 3, 1):
        got = to_foc(direct[k], k)
        if k in near:
            plan, arrays = plan + [("both", k, 0)], arrays + [got]
        else:
            plan = plan + [("own", k, 0), ("other", k, 0)]
            arrays = arrays + [got, to_src(got)]
    arrays[0], rows, columns = lax.optimization_barrier((arrays[0], rows, columns))
    for iteration in range(ITERS):
        last = iteration == ITERS - 1
        keep, send = convolve_pieces(ids, reflection, tuple(plan), arrays, foc_count, focal)
        got = to_core(send)
        beyond = to_y(add(keep[1], got[1]))
        total = (keep[0].astype(F32) + got[0].astype(F32) + beyond.astype(F32)).astype(BF16)
        spectrum = [to_foc(total[k], k) for k in pieces]
        returned = mute_source(ids, onset_source, rows, columns, spectrum, last)
        mine = [to_foc(returned[k], k) for k in pieces]
        across = [to_y(value) for value in mine]
        groups = [mine, [to_core(v) for v in mine], across, [to_core(v) for v in across]]
        own, other = correlate_pieces(ids, reflection, groups)
        renewed = []
        plan, arrays = [], []
        count = focal // HALVES
        for q in range(HALVES):
            far, close = 2 * q, 2 * q + 1
            got_far, got_close = to_src(other[far]), to_src(other[close])
            ready = (
                own[close],
                got_close,
                to_foc(add(own[close][0], got_close[0]), 1),
                to_foc(add(own[far][0], got_far[0]), 2),
                to_foc(add(own[far][1], got_far[1]), 3),
            )
            fresh = mute_receiver(
                ids, onset_receiver, rows, columns, ready, direct, q * count, near, last
            )
            if last:
                renewed.append(fresh)
                continue
            for k in (2, 3, 1, 0):
                value = to_foc(fresh[k], k)
                plan += [("own", k, q * count), ("other", k, q * count)]
                arrays += [value, to_src(value)]
        if last:
            crossed = [to_src(value) for value in renewed]
            mine = returned[-1]
            across = to_y(mine)
            groups = [mine, to_core(mine), across, to_core(across)]
            muted_trace = trace_source(ids, onset_source, rows, groups)
            partly = join_halves(ids, renewed, 0)
            return join_halves(ids, crossed, 1, partly), muted_trace


def local(counts, reflection, direct_wave, onset_receiver, onset_source):
    src_count, rcv_count, foc_count = counts
    two, freq, sources, receivers = reflection.shape
    focal = direct_wave.shape[2]
    fits = (
        (src_count, rcv_count, foc_count) == (2, 4, 4)
        and sources == LANES
        and receivers == 2 * LANES
        and focal == 8
        and freq == 4 * BLOCK_W
        and freq * foc_count == F
    )
    if fits:
        return resident(counts, reflection, direct_wave, onset_receiver, onset_source)
    return general(reflection, direct_wave, onset_receiver, onset_source)


def solution(mesh):
    in_specs = (
        P(None, "foc", "src", "rcv"),
        P(None, None, "foc", "rcv"),
        P("foc", "rcv"),
        P("foc", "src"),
    )
    out_specs = (P(None, None, "foc", "rcv"), P("foc", "src", None))
    counts = (mesh.shape["src"], mesh.shape["rcv"], mesh.shape["foc"])
    return jax.shard_map(
        functools.partial(local, counts),
        mesh=mesh,
        in_specs=in_specs,
        out_specs=out_specs,
        check_vma=False,
    )
```

```python
import functools
import math

import jax
import jax.numpy as jnp
from jax import lax
from jax.experimental import pallas as pl
from jax.experimental.pallas import tpu as pltpu
from jax.sharding import PartitionSpec as P

F = 256
NT = 1024
ITERS = 2
LANES = 128
BLOCK_W = 16
HALVES = 2
F32 = jnp.float32
BF16 = jnp.bfloat16
VMEM_BYTES = 24 * 1024 * 1024


def basis_table():
    frequency_bins = jnp.arange(F, dtype=jnp.int32) + 1
    samples = jnp.arange(NT, dtype=jnp.int32)
    phases = frequency_bins[:, None] * samples[None, :] % NT
    angles = phases.astype(jnp.float32) * (2.0 * math.pi / NT)
    norming = math.sqrt(2.0 / NT)
    return (jnp.stack([jnp.cos(angles), -jnp.sin(angles)]) * norming).astype(jnp.bfloat16)


def mute_traces(spectrum, onsets, basis_rows):
    focal_count = spectrum.shape[2]
    samples = jnp.arange(NT, dtype=jnp.int32)

    def one_focus(focal_index, carry):
        muted_all, returned_all = carry
        one_spectrum = lax.dynamic_slice_in_dim(spectrum, focal_index, 1, 2)
        one_onset = lax.dynamic_slice_in_dim(onsets, focal_index, 1, 0)
        signal = jnp.einsum(
            "cwpr,cwt->prt", one_spectrum, basis_rows, preferred_element_type=jnp.float32
        )
        window = samples[None, None, :] < one_onset[:, :, None]
        muted_one = jnp.where(window, signal, 0.0).astype(jnp.bfloat16)
        returned = jnp.einsum(
            "prt,cwt->cwpr", muted_one, basis_rows, preferred_element_type=jnp.float32
        )
        muted_all = lax.dynamic_update_slice_in_dim(muted_all, muted_one, focal_index, 0)
        returned_all = lax.dynamic_update_slice_in_dim(returned_all, returned, focal_index, 2)
        return (muted_all, returned_all)

    initial = (
        jnp.zeros((focal_count, spectrum.shape[3], NT), jnp.bfloat16),
        jnp.zeros(spectrum.shape, jnp.float32),
    )
    return lax.fori_loop(0, focal_count, one_focus, initial)


def convolve(reflection, focusing):
    real_out = jnp.einsum(
        "wsr,wpr->wps", reflection[0], focusing[0], preferred_element_type=jnp.float32
    ) - jnp.einsum("wsr,wpr->wps", reflection[1], focusing[1], preferred_element_type=jnp.float32)
    imag_out = jnp.einsum(
        "wsr,wpr->wps", reflection[0], focusing[1], preferred_element_type=jnp.float32
    ) + jnp.einsum("wsr,wpr->wps", reflection[1], focusing[0], preferred_element_type=jnp.float32)
    return jnp.stack([real_out, imag_out])


def correlate(reflection, spectrum):
    real_out = jnp.einsum(
        "wsr,wps->wpr", reflection[0], spectrum[0], preferred_element_type=jnp.float32
    ) + jnp.einsum("wsr,wps->wpr", reflection[1], spectrum[1], preferred_element_type=jnp.float32)
    imag_out = jnp.einsum(
        "wsr,wps->wpr", reflection[0], spectrum[1], preferred_element_type=jnp.float32
    ) - jnp.einsum("wsr,wps->wpr", reflection[1], spectrum[0], preferred_element_type=jnp.float32)
    return jnp.stack([real_out, imag_out])


def renew(shares, direct_wave, onset_receiver, basis_rows, source_index):
    share_width = shares.shape[3]
    offset = source_index * share_width
    onset_share = lax.dynamic_slice_in_dim(onset_receiver, offset, share_width, 1)
    direct_share = lax.dynamic_slice_in_dim(direct_wave, offset, share_width, 3)
    unused, update = mute_traces(shares, onset_share, basis_rows)
    renewed = (direct_share.astype(jnp.float32) + update).astype(jnp.bfloat16)
    return lax.all_gather(renewed, "src", axis=3, tiled=True)


def general(reflection, direct_wave, onset_receiver, onset_source):
    basis_rows = basis_table()
    source_index = lax.axis_index("src")
    whole_reflection = lax.all_gather(reflection, "foc", axis=1, tiled=True)
    focusing = direct_wave
    muted_trace = None
    for iteration in range(ITERS):
        partial_value = convolve(whole_reflection, focusing)
        spectrum = lax.psum(partial_value.astype(jnp.bfloat16), "rcv")
        muted_trace, returned = mute_traces(spectrum, onset_source, basis_rows)
        partial_adjoint = correlate(whole_reflection, returned.astype(jnp.bfloat16))
        shares = lax.psum_scatter(
            partial_adjoint.astype(jnp.bfloat16), "src", scatter_dimension=3, tiled=True
        )
        focusing = renew(shares, direct_wave, onset_receiver, basis_rows, source_index)
    return (focusing, muted_trace)


VMEM_SPEC = pl.BlockSpec(memory_space=pltpu.VMEM)
SMEM_SPEC = pl.BlockSpec(memory_space=pltpu.SMEM)


def swap(value, axis, mask, count):
    return lax.ppermute(value, axis, [(i, i ^ mask) for i in range(count)])


def call(kernel, name, out_shape, flops, size, operands, scratch=()):
    many = isinstance(out_shape, list)
    return pl.pallas_call(
        kernel,
        name=name,
        out_shape=out_shape,
        in_specs=[SMEM_SPEC] + [VMEM_SPEC] * (len(operands) - 1),
        out_specs=[VMEM_SPEC] * len(out_shape) if many else VMEM_SPEC,
        scratch_shapes=list(scratch),
        compiler_params=pltpu.CompilerParams(vmem_limit_bytes=VMEM_BYTES),
        cost_estimate=pl.CostEstimate(flops=flops, bytes_accessed=size, transcendentals=0),
    )(*operands)


def table(frequency, part, sample):
    phase = ((frequency + 1) * sample + part * (NT // 4)) & (NT - 1)
    x = (jnp.abs(phase - NT // 2) - NT // 4).astype(F32) * (4.0 / NT)
    square = x * x
    total = jnp.zeros_like(x)
    for order in (11, 9, 7, 5, 3, 1):
        sign = -1.0 if order % 4 == 3 else 1.0
        total = total * square + sign * (math.pi / 2) ** order / math.factorial(order)
    return (total * x * math.sqrt(2.0 / NT)).astype(BF16)


def basis_kernel(ids, rows_ref, columns_ref):
    size = rows_ref.shape[0]
    freq = BLOCK_W * 4
    pieces = size // (2 * freq)
    for k in range(pieces):
        first = (k ^ ids[2]) * freq
        for c in range(2):
            frequency = lax.broadcasted_iota(jnp.int32, (freq, NT), 0) + first
            sample = lax.broadcasted_iota(jnp.int32, (freq, NT), 1)
            start = (2 * k + c) * freq
            rows_ref[start : start + freq, :] = table(frequency, c, sample)
        lane = lax.broadcasted_iota(jnp.int32, (NT, 2 * freq), 1)
        sample = lax.broadcasted_iota(jnp.int32, (NT, 2 * freq), 0)
        part = (lane >= freq).astype(jnp.int32)
        start = 2 * k * freq
        columns_ref[:, start : start + 2 * freq] = table(lane - part * freq + first, part, sample)


def basis(ids):
    size = 2 * F
    return call(
        basis_kernel,
        "basis",
        [jax.ShapeDtypeStruct((size, NT), BF16), jax.ShapeDtypeStruct((NT, size), BF16)],
        40 * size * NT,
        4 * size * NT,
        (ids,),
    )


def split_kernel(both, ids, wave_ref, out_ref, hold):
    width, focal = wave_ref.shape[1], wave_ref.shape[2]
    for place in range(2 if both else 1):
        lanes = slice(place * LANES, (place + 1) * LANES)
        hold[...] = wave_ref[0, :, :, lanes].astype(F32).reshape(width * focal, LANES)
        for p in range(focal):
            rows = hold[pl.ds(p, width, stride=focal), :].astype(BF16)
            if both:
                out_ref[place, 0, p] = rows
            else:
                out_ref[0, p] = rows


def split_wave(ids, wave, piece, foc_count, both):
    freq = wave.shape[1] // foc_count
    focal = wave.shape[2]
    if both:
        shape = (2, 2, focal, freq, LANES)
        in_spec = pl.BlockSpec(
            (1, freq, focal, 2 * LANES), lambda c, ids: (c, ids[2] ^ piece, 0, 0)
        )
        out_spec = pl.BlockSpec((2, 1, focal, freq, LANES), lambda c, ids: (0, c, 0, 0, 0))
    else:
        shape = (2, focal, freq, LANES)
        in_spec = pl.BlockSpec(
            (1, freq, focal, LANES), lambda c, ids: (c, ids[2] ^ piece, 0, ids[0])
        )
        out_spec = pl.BlockSpec((1, focal, freq, LANES), lambda c, ids: (c, 0, 0, 0))
    return pl.pallas_call(
        functools.partial(split_kernel, both),
        name="split_wave",
        out_shape=jax.ShapeDtypeStruct(shape, BF16),
        grid_spec=pltpu.PrefetchScalarGridSpec(
            num_scalar_prefetch=1,
            grid=(2,),
            in_specs=[in_spec],
            out_specs=out_spec,
            scratch_shapes=[pltpu.VMEM((freq * focal, LANES), F32)],
        ),
        compiler_params=pltpu.CompilerParams(vmem_limit_bytes=VMEM_BYTES),
        cost_estimate=pl.CostEstimate(
            flops=0, bytes_accessed=8 * focal * freq * LANES, transcendentals=0
        ),
    )(ids, wave)


def convolve_kernel(plan, pieces, focal, ids, refl_ref, *refs):
    ins = refs[: len(plan)]
    keep_ref, send_ref, hold, result = refs[len(plan) :]
    half, me = ids[0], ids[1]
    sources = refl_ref.shape[2]
    rows = pieces * 2 * focal
    share = focal // 4

    def block(b, carry):
        first = pl.multiple_of(b * BLOCK_W, BLOCK_W)
        window = pl.ds(first, BLOCK_W)

        def put(place, k, c, start, value):
            size = value.shape[0] * BLOCK_W
            at = ((k * 2 + c) * focal + start) * BLOCK_W
            hold[place, at : at + size, :] = value.astype(F32).reshape(size, LANES)

        for ref, (kind, k, start) in zip(ins, plan):
            for c in range(2):
                if kind == "both":
                    put(0, k, c, start, ref[0, c, :, window, :])
                    put(1, k, c, start, ref[1, c, :, window, :])
                elif kind == "own":
                    put(half, k, c, start, ref[c, :, window, :])
                else:
                    put(1 - half, k, c, start, ref[c, :, window, :])
        for w in range(BLOCK_W):
            step = pl.ds(w, rows, stride=BLOCK_W)
            left = jnp.concatenate([hold[0, step, :], hold[1, step, :]], 1).astype(BF16)
            right = refl_ref[:, first + w].reshape(2 * sources, 2 * LANES)
            both = lax.dot_general(
                left, right, (((1,), (1,)), ((), ())), preferred_element_type=F32
            )
            by_real = both[:, :LANES].reshape(pieces, 2, focal, LANES)
            by_imag = both[:, LANES:].reshape(pieces, 2, focal, LANES)
            value = jnp.stack(
                [by_real[:, 0] - by_imag[:, 1], by_real[:, 1] + by_imag[:, 0]], 1
            )
            result[step, :] = value.reshape(rows, LANES)
        size = share * BLOCK_W
        for place, out in ((0, keep_ref), (1, send_ref)):
            for y in range(2):
                group = (2 * y + place) ^ me
                for k in range(pieces):
                    for c in range(2):
                        start = ((k * 2 + c) * focal + group * share) * BLOCK_W
                        part = result[pl.ds(pl.multiple_of(start, size), size), :]
                        out[y, k, c, :, window, :] = part.reshape(
                            share, BLOCK_W, LANES
                        ).astype(BF16)
        return carry

    lax.fori_loop(0, refl_ref.shape[1] // BLOCK_W, block, 0)


def convolve_pieces(ids, reflection, plan, arrays, pieces, focal):
    two, freq, sources, receivers = reflection.shape
    rows = pieces * 2 * focal
    out = jax.ShapeDtypeStruct((2, pieces, 2, focal // 4, freq, LANES), BF16)
    return call(
        functools.partial(convolve_kernel, plan, pieces, focal),
        "convolve",
        [out, out],
        2 * freq * rows * 256 * 256,
        freq * (2 * sources * 512 + rows * 768),
        (ids, reflection, *arrays),
        [
            pltpu.VMEM((2, rows * BLOCK_W, LANES), F32),
            pltpu.VMEM((rows * BLOCK_W, LANES), F32),
        ],
    )


def correlate_kernel(pieces, ids, refl_ref, *refs):
    ins = [refs[j * pieces : (j + 1) * pieces] for j in range(4)]
    outs = refs[4 * pieces : -2]
    hold, result = refs[-2:]
    half, me = ids[0], ids[1]
    share = ins[0][0].shape[1]
    focal = 4 * share
    sources = refl_ref.shape[2]
    rows = pieces * focal
    part_size = focal // HALVES

    def block(b, carry):
        first = pl.multiple_of(b * BLOCK_W, BLOCK_W)
        window = pl.ds(first, BLOCK_W)
        size = share * BLOCK_W
        for j in range(4):
            group = j ^ me
            for k in range(pieces):
                start = pl.multiple_of((k * focal + group * share) * BLOCK_W, size)
                for c in range(2):
                    value = ins[j][k][c, :, window, :].astype(F32).reshape(size, LANES)
                    hold[c, pl.ds(start, size), :] = value
        for w in range(BLOCK_W):
            step = pl.ds(w, rows, stride=BLOCK_W)
            real = hold[0, step, :].astype(BF16)
            imag = hold[1, step, :].astype(BF16)
            left = jnp.concatenate(
                [jnp.concatenate([real, imag], 1), jnp.concatenate([imag, -real], 1)], 0
            )
            right = refl_ref[:, first + w].reshape(2 * sources, 2 * LANES)
            value = lax.dot_general(
                left, right, (((1,), (0,)), ((), ())), preferred_element_type=F32
            )
            step = pl.ds(w, 2 * rows, stride=BLOCK_W)
            result[0, step, :] = value[:, :LANES]
            result[1, step, :] = value[:, LANES:]
        size = part_size * BLOCK_W
        index = 0
        for place in (half, 1 - half):
            for q in range(HALVES):
                for group in PAIRS:
                    for i, k in enumerate(group):
                        for c in range(2):
                            at = ((c * pieces + k) * focal + q * part_size) * BLOCK_W
                            part = result[place, at : at + size, :]
                            outs[index][i, c, :, window, :] = part.reshape(
                                part_size, BLOCK_W, LANES
                            ).astype(BF16)
                    index += 1
        return carry

    lax.fori_loop(0, refl_ref.shape[1] // BLOCK_W, block, 0)


PAIRS = ((2, 3), (1, 0))


def correlate_pieces(ids, reflection, groups):
    pieces = len(groups[0])
    two, share, freq, lanes = groups[0][0].shape
    focal = 4 * share
    sources = reflection.shape[2]
    rows = pieces * 2 * focal
    out = jax.ShapeDtypeStruct((2, 2, focal // HALVES, freq, LANES), BF16)
    count = HALVES * len(PAIRS)
    results = call(
        functools.partial(correlate_kernel, pieces),
        "correlate",
        [out] * (2 * count),
        2 * freq * rows * 256 * 256,
        freq * (2 * sources * 512 + rows * 768),
        (ids, reflection, *[v for group in groups for v in group]),
        [
            pltpu.VMEM((2, rows // 2 * BLOCK_W, LANES), F32),
            pltpu.VMEM((2, rows * BLOCK_W, LANES), F32),
        ],
    )
    return results[:count], results[count:]


def windowed(columns_ref, rows, onsets):
    signal = jnp.dot(columns_ref[...], rows, preferred_element_type=F32)
    sample = lax.broadcasted_iota(jnp.int32, signal.shape, 0)
    return jnp.where(sample < onsets, signal, 0.0).astype(BF16)


def mute_source_kernel(copy, ids, onset_ref, rows_ref, columns_ref, *refs):
    pieces = (len(refs) - copy) // 2
    ins, outs = refs[:pieces], refs[pieces : 2 * pieces]
    share, width = ins[0].shape[1], ins[0].shape[2]
    first = ids[1] * share
    if copy:
        for k in range(pieces):
            refs[-1][k] = ins[k][...]
    spectrum = jnp.concatenate(
        [
            jnp.concatenate([ref[c, p] for ref in ins for c in range(2)], 0)
            for p in range(share)
        ],
        1,
    )
    onsets = jnp.concatenate([onset_ref[pl.ds(first + p, 1), :] for p in range(share)], 1)
    muted = windowed(columns_ref, spectrum, onsets)
    back = jnp.dot(rows_ref[...], muted, preferred_element_type=F32).astype(BF16)
    for i, out in enumerate(outs):
        for c in range(2):
            for p in range(share):
                start = (2 * i + c) * width
                out[c, p] = back[start : start + width, p * LANES : (p + 1) * LANES]


def mute_source(ids, onset, rows, columns, pieces, copy):
    shape = pieces[0].shape
    outs = [jax.ShapeDtypeStruct(shape, BF16)] * len(pieces)
    if copy:
        outs = outs + [jax.ShapeDtypeStruct((len(pieces),) + shape, BF16)]
    return call(
        functools.partial(mute_source_kernel, int(copy)),
        "mute_source",
        outs,
        4 * NT * 2 * F * shape[1] * LANES,
        3 << 20,
        (ids, onset, rows, columns, *pieces),
    )


def trace_kernel(ids, onset_ref, rows_ref, *refs):
    ins, out_ref = refs[:4], refs[4]
    pieces, two, share = ins[0].shape[:3]
    step = pl.program_id(0)
    for j in range(4):

        @pl.when(step // share == j)
        def one():
            p = step % share
            spectrum = jnp.concatenate(
                [ins[j][k, c, p] for k in range(pieces) for c in range(2)], 0
            )
            signal = lax.dot_general(
                spectrum, rows_ref[...], (((0,), (0,)), ((), ())), preferred_element_type=F32
            )
            sample = lax.broadcasted_iota(jnp.int32, signal.shape, 1)
            out_ref[0] = jnp.where(sample < onset_ref[0], signal, 0.0).astype(BF16)


def trace_source(ids, onset, rows, groups):
    focal, sources = onset.shape
    share = groups[0].shape[2]

    def place(g, ids):
        return ((g // share) ^ ids[1]) * share + g % share, 0, 0

    return pl.pallas_call(
        trace_kernel,
        name="trace_source",
        out_shape=jax.ShapeDtypeStruct((focal, sources, NT), BF16),
        grid_spec=pltpu.PrefetchScalarGridSpec(
            num_scalar_prefetch=1,
            grid=(focal,),
            in_specs=[pl.BlockSpec((1, sources, 1), place)] + [VMEM_SPEC] * 5,
            out_specs=pl.BlockSpec((1, sources, NT), place),
        ),
        compiler_params=pltpu.CompilerParams(vmem_limit_bytes=VMEM_BYTES),
        cost_estimate=pl.CostEstimate(
            flops=2 * NT * 2 * F * focal * LANES, bytes_accessed=5 << 20, transcendentals=0
        ),
    )(ids, onset[:, :, None], rows, *groups)


def mute_receiver_kernel(first, both, last, ids, onset_ref, rows_ref, columns_ref, *refs):
    two, three, one, near, extra = refs[:5]
    pieces = 4
    direct = refs[5 : 5 + pieces]
    outs = refs[5 + pieces :]
    half = ids[0]
    count, width = one.shape[1], one.shape[2]
    lanes = pl.ds(pl.multiple_of(half * LANES, LANES), LANES)

    def part(k, c, p):
        if k == 0:
            return (near[1, c, p].astype(F32) + extra[1, c, p].astype(F32)).astype(BF16)
        return (None, one, two, three)[k][c, p]

    step = 2
    for start in range(0, count, step):
        group = range(start, start + step)
        spectrum = jnp.concatenate(
            [
                jnp.concatenate([part(k, c, p) for k in range(pieces) for c in range(2)], 0)
                for p in group
            ],
            1,
        )
        onsets = jnp.concatenate(
            [onset_ref[first + p : first + p + 1, lanes] for p in group], 1
        )
        muted = windowed(columns_ref, spectrum, onsets)
        back = jnp.dot(rows_ref[...], muted, preferred_element_type=F32)
        for k in range(pieces):
            for c in range(2):
                for i, p in enumerate(group):
                    at = (2 * k + c) * width
                    block = back[at : at + width, i * LANES : (i + 1) * LANES]
                    if k in both:
                        wave = direct[k][half, c, first + p]
                    else:
                        wave = direct[k][c, first + p]
                    value = (wave.astype(F32) + block).astype(BF16)
                    if last:
                        outs[0][c, k ^ ids[2], p] = value
                    else:
                        outs[k][c, p] = value


def mute_receiver(ids, onset, rows, columns, arrays, direct, first, both, last):
    shape = arrays[2].shape
    count, freq = shape[1], shape[2]
    if last:
        outs = jax.ShapeDtypeStruct((2, 4, count, freq, LANES), BF16)
    else:
        outs = [jax.ShapeDtypeStruct(shape, BF16)] * 4
    return call(
        functools.partial(mute_receiver_kernel, first, both, last),
        "mute_receiver",
        outs,
        4 * NT * 2 * F * count * LANES,
        4 << 20,
        (ids, onset, rows, columns, *arrays, *direct),
    )


def join_kernel(ids, *refs):
    ins, out_ref, hold = refs[:HALVES], refs[-2], refs[-1]
    two, foc_count, count, width, lanes = ins[0].shape
    focal = HALVES * count
    step = pl.program_id(0)
    for c in range(2):
        for q, ref in enumerate(ins):
            for p in range(count):
                hold[pl.ds(c * width * focal + q * count + p, width, stride=focal), :] = ref[
                    c, step, p
                ].astype(F32)
    out_ref[...] = hold[...].astype(BF16).reshape(out_ref.shape)


def join_halves(ids, parts, mask, into=None):
    two, foc_count, count, freq, lanes = parts[0].shape
    focal = HALVES * count
    extra = [] if into is None else [into]
    return pl.pallas_call(
        join_kernel,
        name="join_halves",
        out_shape=jax.ShapeDtypeStruct((two, foc_count * freq, focal, 2 * lanes), BF16),
        grid_spec=pltpu.PrefetchScalarGridSpec(
            num_scalar_prefetch=1,
            grid=(foc_count,),
            in_specs=[VMEM_SPEC] * HALVES + [pl.BlockSpec(memory_space=pl.ANY)] * len(extra),
            out_specs=pl.BlockSpec(
                (two, freq, focal, lanes), lambda g, ids: (0, g, 0, ids[0] ^ mask)
            ),
            scratch_shapes=[pltpu.VMEM((two * freq * focal, lanes), F32)],
        ),
        input_output_aliases={1 + HALVES: 0} if extra else {},
        compiler_params=pltpu.CompilerParams(vmem_limit_bytes=VMEM_BYTES),
        cost_estimate=pl.CostEstimate(
            flops=0, bytes_accessed=8 * foc_count * freq * focal * lanes, transcendentals=0
        ),
    )(ids, *parts, *extra)


def add(left, right):
    return (left.astype(F32) + right.astype(F32)).astype(BF16)


def resident(counts, reflection, direct_wave, onset_receiver, onset_source):
    src_count, rcv_count, foc_count = counts
    ids = jnp.stack([lax.axis_index("src"), lax.axis_index("rcv"), lax.axis_index("foc")])
    ids = ids.astype(jnp.int32)
    focal = direct_wave.shape[2]
    pieces = range(foc_count)
    near = (0, 1)

    def to_foc(value, k):
        return value if k == 0 else swap(value, "foc", k, foc_count)

    def to_src(value):
        return swap(value, "src", 1, src_count)

    def to_core(value):
        return swap(value, "rcv", 1, rcv_count)

    def to_y(value):
        return swap(value, "rcv", 2, rcv_count)

    direct = [None] * foc_count
    direct[2] = split_wave(ids, direct_wave, 2, foc_count, False)
    rows, columns = basis(ids)
    later, rows, columns = lax.optimization_barrier((ids, rows, columns))
    direct[3] = split_wave(later, direct_wave, 3, foc_count, False)
    later, direct[3] = lax.optimization_barrier((ids, direct[3]))
    direct[1] = split_wave(later, direct_wave, 1, foc_count, True)
    direct[0] = split_wave(later, direct_wave, 0, foc_count, True)
    plan, arrays = [("both", 0, 0)], [direct[0]]
    for k in (2, 3, 1):
        got = to_foc(direct[k], k)
        if k in near:
            plan, arrays = plan + [("both", k, 0)], arrays + [got]
        else:
            plan = plan + [("own", k, 0), ("other", k, 0)]
            arrays = arrays + [got, to_src(got)]
    for iteration in range(ITERS):
        last = iteration == ITERS - 1
        keep, send = convolve_pieces(ids, reflection, tuple(plan), arrays, foc_count, focal)
        got = to_core(send)
        beyond = to_y(add(keep[1], got[1]))
        total = (keep[0].astype(F32) + got[0].astype(F32) + beyond.astype(F32)).astype(BF16)
        spectrum = [to_foc(total[k], k) for k in pieces]
        returned = mute_source(ids, onset_source, rows, columns, spectrum, last)
        mine = [to_foc(returned[k], k) for k in pieces]
        across = [to_y(value) for value in mine]
        groups = [mine, [to_core(v) for v in mine], across, [to_core(v) for v in across]]
        own, other = correlate_pieces(ids, reflection, groups)
        renewed = []
        early = []
        plan, arrays = [], []
        count = focal // HALVES
        for q in range(HALVES):
            far, close = 2 * q, 2 * q + 1
            got_far, got_close = to_src(other[far]), to_src(other[close])
            if q == 1:
                got_close, fresh = lax.optimization_barrier((got_close, fresh))
            ready = (
                to_foc(add(own[far][0], got_far[0]), 2),
                to_foc(add(own[far][1], got_far[1]), 3),
                to_foc(add(own[close][0], got_close[0]), 1),
                own[close],
                got_close,
            )
            if q == 1:
                ready, early = lax.optimization_barrier((ready, early))
            fresh = mute_receiver(
                ids, onset_receiver, rows, columns, ready, direct, q * count, near, last
            )
            if last:
                renewed.append(fresh)
                continue
            moved = [to_foc(fresh[k], k) for k in (2, 3, 1, 0)]
            if q == 0 and not last:
                before, early = moved, [to_src(moved[3])]
                continue
            before[:2], moved[2] = lax.optimization_barrier((before[:2], moved[2]))
            crossed = [to_src(before[0]), to_src(before[1]), to_src(before[2])] + early
            after = [to_src(moved[3]), to_src(moved[2])]
            after = [to_src(moved[0]), to_src(moved[1]), after[1], after[0]]
            arrays = before + crossed + moved + after
            plan = [(kind, k, start * count) for start in range(2) for kind in ("own", "other") for k in (2, 3, 1, 0)]
        if last:
            crossed = [to_src(value) for value in renewed]
            mine = returned[-1]
            across = to_y(mine)
            groups = [mine, to_core(mine), across, to_core(across)]
            muted_trace = trace_source(ids, onset_source, rows, groups)
            partly = join_halves(ids, renewed, 0)
            return join_halves(ids, crossed, 1, partly), muted_trace


def local(counts, reflection, direct_wave, onset_receiver, onset_source):
    src_count, rcv_count, foc_count = counts
    two, freq, sources, receivers = reflection.shape
    focal = direct_wave.shape[2]
    fits = (
        (src_count, rcv_count, foc_count) == (2, 4, 4)
        and sources == LANES
        and receivers == 2 * LANES
        and focal == 8
        and freq == 4 * BLOCK_W
        and freq * foc_count == F
    )
    if fits:
        return resident(counts, reflection, direct_wave, onset_receiver, onset_source)
    return general(reflection, direct_wave, onset_receiver, onset_source)


def solution(mesh):
    in_specs = (
        P(None, "foc", "src", "rcv"),
        P(None, None, "foc", "rcv"),
        P("foc", "rcv"),
        P("foc", "src"),
    )
    out_specs = (P(None, None, "foc", "rcv"), P("foc", "src", None))
    counts = (mesh.shape["src"], mesh.shape["rcv"], mesh.shape["foc"])
    return jax.shard_map(
        functools.partial(local, counts),
        mesh=mesh,
        in_specs=in_specs,
        out_specs=out_specs,
        check_vma=False,
    )
```

```python
import functools
import math

import jax
import jax.numpy as jnp
from jax import lax
from jax.experimental import pallas as pl
from jax.experimental.pallas import tpu as pltpu
from jax.sharding import PartitionSpec as P

F = 256
NT = 1024
ITERS = 2
LANES = 128
BLOCK_W = 16
HALVES = 2
GROUP_ORDER = (4, 3, 15, 5, 12, 2, 6, 9, 7, 14, 11, 1, 10, 13, 0, 8)
F32 = jnp.float32
BF16 = jnp.bfloat16
VMEM_BYTES = 24 * 1024 * 1024


def basis_table():
    frequency_bins = jnp.arange(F, dtype=jnp.int32) + 1
    samples = jnp.arange(NT, dtype=jnp.int32)
    phases = frequency_bins[:, None] * samples[None, :] % NT
    angles = phases.astype(jnp.float32) * (2.0 * math.pi / NT)
    norming = math.sqrt(2.0 / NT)
    return (jnp.stack([jnp.cos(angles), -jnp.sin(angles)]) * norming).astype(jnp.bfloat16)


def mute_traces(spectrum, onsets, basis_rows):
    focal_count = spectrum.shape[2]
    samples = jnp.arange(NT, dtype=jnp.int32)

    def one_focus(focal_index, carry):
        muted_all, returned_all = carry
        one_spectrum = lax.dynamic_slice_in_dim(spectrum, focal_index, 1, 2)
        one_onset = lax.dynamic_slice_in_dim(onsets, focal_index, 1, 0)
        signal = jnp.einsum(
            "cwpr,cwt->prt", one_spectrum, basis_rows, preferred_element_type=jnp.float32
        )
        window = samples[None, None, :] < one_onset[:, :, None]
        muted_one = jnp.where(window, signal, 0.0).astype(jnp.bfloat16)
        returned = jnp.einsum(
            "prt,cwt->cwpr", muted_one, basis_rows, preferred_element_type=jnp.float32
        )
        muted_all = lax.dynamic_update_slice_in_dim(muted_all, muted_one, focal_index, 0)
        returned_all = lax.dynamic_update_slice_in_dim(returned_all, returned, focal_index, 2)
        return (muted_all, returned_all)

    initial = (
        jnp.zeros((focal_count, spectrum.shape[3], NT), jnp.bfloat16),
        jnp.zeros(spectrum.shape, jnp.float32),
    )
    return lax.fori_loop(0, focal_count, one_focus, initial)


def convolve(reflection, focusing):
    real_out = jnp.einsum(
        "wsr,wpr->wps", reflection[0], focusing[0], preferred_element_type=jnp.float32
    ) - jnp.einsum("wsr,wpr->wps", reflection[1], focusing[1], preferred_element_type=jnp.float32)
    imag_out = jnp.einsum(
        "wsr,wpr->wps", reflection[0], focusing[1], preferred_element_type=jnp.float32
    ) + jnp.einsum("wsr,wpr->wps", reflection[1], focusing[0], preferred_element_type=jnp.float32)
    return jnp.stack([real_out, imag_out])


def correlate(reflection, spectrum):
    real_out = jnp.einsum(
        "wsr,wps->wpr", reflection[0], spectrum[0], preferred_element_type=jnp.float32
    ) + jnp.einsum("wsr,wps->wpr", reflection[1], spectrum[1], preferred_element_type=jnp.float32)
    imag_out = jnp.einsum(
        "wsr,wps->wpr", reflection[0], spectrum[1], preferred_element_type=jnp.float32
    ) - jnp.einsum("wsr,wps->wpr", reflection[1], spectrum[0], preferred_element_type=jnp.float32)
    return jnp.stack([real_out, imag_out])


def renew(shares, direct_wave, onset_receiver, basis_rows, source_index):
    share_width = shares.shape[3]
    offset = source_index * share_width
    onset_share = lax.dynamic_slice_in_dim(onset_receiver, offset, share_width, 1)
    direct_share = lax.dynamic_slice_in_dim(direct_wave, offset, share_width, 3)
    unused, update = mute_traces(shares, onset_share, basis_rows)
    renewed = (direct_share.astype(jnp.float32) + update).astype(jnp.bfloat16)
    return lax.all_gather(renewed, "src", axis=3, tiled=True)


def general(reflection, direct_wave, onset_receiver, onset_source):
    basis_rows = basis_table()
    source_index = lax.axis_index("src")
    whole_reflection = lax.all_gather(reflection, "foc", axis=1, tiled=True)
    focusing = direct_wave
    muted_trace = None
    for iteration in range(ITERS):
        partial_value = convolve(whole_reflection, focusing)
        spectrum = lax.psum(partial_value.astype(jnp.bfloat16), "rcv")
        muted_trace, returned = mute_traces(spectrum, onset_source, basis_rows)
        partial_adjoint = correlate(whole_reflection, returned.astype(jnp.bfloat16))
        shares = lax.psum_scatter(
            partial_adjoint.astype(jnp.bfloat16), "src", scatter_dimension=3, tiled=True
        )
        focusing = renew(shares, direct_wave, onset_receiver, basis_rows, source_index)
    return (focusing, muted_trace)


VMEM_SPEC = pl.BlockSpec(memory_space=pltpu.VMEM)
SMEM_SPEC = pl.BlockSpec(memory_space=pltpu.SMEM)


def swap(value, axis, mask, count):
    return lax.ppermute(value, axis, [(i, i ^ mask) for i in range(count)])


def call(kernel, name, out_shape, flops, size, operands, scratch=()):
    many = isinstance(out_shape, list)
    return pl.pallas_call(
        kernel,
        name=name,
        out_shape=out_shape,
        in_specs=[SMEM_SPEC] + [VMEM_SPEC] * (len(operands) - 1),
        out_specs=[VMEM_SPEC] * len(out_shape) if many else VMEM_SPEC,
        scratch_shapes=list(scratch),
        compiler_params=pltpu.CompilerParams(vmem_limit_bytes=VMEM_BYTES),
        cost_estimate=pl.CostEstimate(flops=flops, bytes_accessed=size, transcendentals=0),
    )(*operands)


def table(frequency, part, sample):
    phase = ((frequency + 1) * sample + part * (NT // 4)) & (NT - 1)
    x = (jnp.abs(phase - NT // 2) - NT // 4).astype(F32) * (4.0 / NT)
    square = x * x
    total = jnp.zeros_like(x)
    for order in (11, 9, 7, 5, 3, 1):
        sign = -1.0 if order % 4 == 3 else 1.0
        total = total * square + sign * (math.pi / 2) ** order / math.factorial(order)
    return (total * x * math.sqrt(2.0 / NT)).astype(BF16)


def basis_kernel(ids, rows_ref, columns_ref):
    size = rows_ref.shape[0]
    freq = BLOCK_W * 4
    pieces = size // (2 * freq)
    for k in range(pieces):
        first = (k ^ ids[2]) * freq
        for c in range(2):
            frequency = lax.broadcasted_iota(jnp.int32, (freq, NT), 0) + first
            sample = lax.broadcasted_iota(jnp.int32, (freq, NT), 1)
            start = (2 * k + c) * freq
            rows_ref[start : start + freq, :] = table(frequency, c, sample)
        lane = lax.broadcasted_iota(jnp.int32, (NT, 2 * freq), 1)
        sample = lax.broadcasted_iota(jnp.int32, (NT, 2 * freq), 0)
        part = (lane >= freq).astype(jnp.int32)
        start = 2 * k * freq
        columns_ref[:, start : start + 2 * freq] = table(lane - part * freq + first, part, sample)


def basis(ids):
    size = 2 * F
    return call(
        basis_kernel,
        "basis",
        [jax.ShapeDtypeStruct((size, NT), BF16), jax.ShapeDtypeStruct((NT, size), BF16)],
        40 * size * NT,
        4 * size * NT,
        (ids,),
    )


def split_kernel(both, ids, wave_ref, out_ref, hold):
    width, focal = wave_ref.shape[1], wave_ref.shape[2]
    for place in range(2 if both else 1):
        lanes = slice(place * LANES, (place + 1) * LANES)
        hold[...] = wave_ref[0, :, :, lanes].astype(F32).reshape(width * focal, LANES)
        for p in range(focal):
            rows = hold[pl.ds(p, width, stride=focal), :].astype(BF16)
            if both:
                out_ref[place, 0, p] = rows
            else:
                out_ref[0, p] = rows


def split_wave(ids, wave, piece, foc_count, both):
    freq = wave.shape[1] // foc_count
    focal = wave.shape[2]
    if both:
        shape = (2, 2, focal, freq, LANES)
        in_spec = pl.BlockSpec(
            (1, freq, focal, 2 * LANES), lambda c, ids: (c, ids[2] ^ piece, 0, 0)
        )
        out_spec = pl.BlockSpec((2, 1, focal, freq, LANES), lambda c, ids: (0, c, 0, 0, 0))
    else:
        shape = (2, focal, freq, LANES)
        in_spec = pl.BlockSpec(
            (1, freq, focal, LANES), lambda c, ids: (c, ids[2] ^ piece, 0, ids[0])
        )
        out_spec = pl.BlockSpec((1, focal, freq, LANES), lambda c, ids: (c, 0, 0, 0))
    return pl.pallas_call(
        functools.partial(split_kernel, both),
        name="split_wave",
        out_shape=jax.ShapeDtypeStruct(shape, BF16),
        grid_spec=pltpu.PrefetchScalarGridSpec(
            num_scalar_prefetch=1,
            grid=(2,),
            in_specs=[in_spec],
            out_specs=out_spec,
            scratch_shapes=[pltpu.VMEM((freq * focal, LANES), F32)],
        ),
        compiler_params=pltpu.CompilerParams(vmem_limit_bytes=VMEM_BYTES),
        cost_estimate=pl.CostEstimate(
            flops=0, bytes_accessed=8 * focal * freq * LANES, transcendentals=0
        ),
    )(ids, wave)


def convolve_kernel(plan, pieces, focal, ids, refl_ref, *refs):
    ins = refs[: len(plan)]
    keep_ref, send_ref, hold, result = refs[len(plan) :]
    half, me = ids[0], ids[1]
    sources = refl_ref.shape[2]
    rows = pieces * 2 * focal
    share = focal // 4

    def block(b, carry):
        first = pl.multiple_of(b * BLOCK_W, BLOCK_W)
        window = pl.ds(first, BLOCK_W)

        def put(place, k, c, start, value):
            size = value.shape[0] * BLOCK_W
            at = ((k * 2 + c) * focal + start) * BLOCK_W
            hold[place, at : at + size, :] = value.astype(F32).reshape(size, LANES)

        for ref, (kind, k, start) in zip(ins, plan):
            for c in range(2):
                if kind == "both":
                    put(0, k, c, start, ref[0, c, :, window, :])
                    put(1, k, c, start, ref[1, c, :, window, :])
                elif kind == "own":
                    put(half, k, c, start, ref[c, :, window, :])
                else:
                    put(1 - half, k, c, start, ref[c, :, window, :])
        for w in range(BLOCK_W):
            step = pl.ds(w, rows, stride=BLOCK_W)
            left = jnp.concatenate([hold[0, step, :], hold[1, step, :]], 1).astype(BF16)
            right = refl_ref[:, first + w].reshape(2 * sources, 2 * LANES)
            both = lax.dot_general(
                left, right, (((1,), (1,)), ((), ())), preferred_element_type=F32
            )
            by_real = both[:, :LANES].reshape(pieces, 2, focal, LANES)
            by_imag = both[:, LANES:].reshape(pieces, 2, focal, LANES)
            value = jnp.stack(
                [by_real[:, 0] - by_imag[:, 1], by_real[:, 1] + by_imag[:, 0]], 1
            )
            result[step, :] = value.reshape(rows, LANES)
        size = share * BLOCK_W
        for place, out in ((0, keep_ref), (1, send_ref)):
            for y in range(2):
                group = (2 * y + place) ^ me
                for k in range(pieces):
                    for c in range(2):
                        start = ((k * 2 + c) * focal + group * share) * BLOCK_W
                        part = result[pl.ds(pl.multiple_of(start, size), size), :]
                        out[y, k, c, :, window, :] = part.reshape(
                            share, BLOCK_W, LANES
                        ).astype(BF16)
        return carry

    lax.fori_loop(0, refl_ref.shape[1] // BLOCK_W, block, 0)


def convolve_pieces(ids, reflection, plan, arrays, pieces, focal):
    two, freq, sources, receivers = reflection.shape
    rows = pieces * 2 * focal
    out = jax.ShapeDtypeStruct((2, pieces, 2, focal // 4, freq, LANES), BF16)
    return call(
        functools.partial(convolve_kernel, plan, pieces, focal),
        "convolve",
        [out, out],
        2 * freq * rows * 256 * 256,
        freq * (2 * sources * 512 + rows * 768),
        (ids, reflection, *arrays),
        [
            pltpu.VMEM((2, rows * BLOCK_W, LANES), F32),
            pltpu.VMEM((rows * BLOCK_W, LANES), F32),
        ],
    )


def correlate_kernel(pieces, ids, refl_ref, *refs):
    ins = [[refs[GROUP_ORDER.index(j * pieces + k)] for k in range(pieces)] for j in range(4)]
    outs = refs[4 * pieces : -2]
    hold, result = refs[-2:]
    half, me = ids[0], ids[1]
    share = ins[0][0].shape[1]
    focal = 4 * share
    sources = refl_ref.shape[2]
    rows = pieces * focal
    part_size = focal // HALVES

    def block(b, carry):
        first = pl.multiple_of(b * BLOCK_W, BLOCK_W)
        window = pl.ds(first, BLOCK_W)
        size = share * BLOCK_W
        for j in range(4):
            group = j ^ me
            for k in range(pieces):
                start = pl.multiple_of((k * focal + group * share) * BLOCK_W, size)
                for c in range(2):
                    value = ins[j][k][c, :, window, :].astype(F32).reshape(size, LANES)
                    hold[c, pl.ds(start, size), :] = value
        for w in range(BLOCK_W):
            step = pl.ds(w, rows, stride=BLOCK_W)
            real = hold[0, step, :].astype(BF16)
            imag = hold[1, step, :].astype(BF16)
            left = jnp.concatenate(
                [jnp.concatenate([real, imag], 1), jnp.concatenate([imag, -real], 1)], 0
            )
            right = refl_ref[:, first + w].reshape(2 * sources, 2 * LANES)
            value = lax.dot_general(
                left, right, (((1,), (0,)), ((), ())), preferred_element_type=F32
            )
            step = pl.ds(w, 2 * rows, stride=BLOCK_W)
            result[0, step, :] = value[:, :LANES]
            result[1, step, :] = value[:, LANES:]
        size = part_size * BLOCK_W
        index = 0
        for place in (half, 1 - half):
            for q in range(HALVES):
                for group in PAIRS:
                    for i, k in enumerate(group):
                        for c in range(2):
                            at = ((c * pieces + k) * focal + q * part_size) * BLOCK_W
                            part = result[place, at : at + size, :]
                            outs[index][i, c, :, window, :] = part.reshape(
                                part_size, BLOCK_W, LANES
                            ).astype(BF16)
                    index += 1
        return carry

    lax.fori_loop(0, refl_ref.shape[1] // BLOCK_W, block, 0)


PAIRS = ((2, 3), (1, 0))


def correlate_pieces(ids, reflection, groups):
    pieces = len(groups[0])
    two, share, freq, lanes = groups[0][0].shape
    focal = 4 * share
    sources = reflection.shape[2]
    rows = pieces * 2 * focal
    out = jax.ShapeDtypeStruct((2, 2, focal // HALVES, freq, LANES), BF16)
    count = HALVES * len(PAIRS)
    results = call(
        functools.partial(correlate_kernel, pieces),
        "correlate",
        [out] * (2 * count),
        2 * freq * rows * 256 * 256,
        freq * (2 * sources * 512 + rows * 768),
        (ids, reflection, *[groups[i // pieces][i % pieces] for i in GROUP_ORDER]),
        [
            pltpu.VMEM((2, rows // 2 * BLOCK_W, LANES), F32),
            pltpu.VMEM((2, rows * BLOCK_W, LANES), F32),
        ],
    )
    return results[:count], results[count:]


def windowed(columns_ref, rows, onsets):
    signal = jnp.dot(columns_ref[...], rows, preferred_element_type=F32)
    sample = lax.broadcasted_iota(jnp.int32, signal.shape, 0)
    return jnp.where(sample < onsets, signal, 0.0).astype(BF16)


def mute_source_kernel(copy, ids, onset_ref, rows_ref, columns_ref, *refs):
    pieces = (len(refs) - copy) // 2
    ins, outs = refs[:pieces], refs[pieces : 2 * pieces]
    share, width = ins[0].shape[1], ins[0].shape[2]
    first = ids[1] * share
    if copy:
        for k in range(pieces):
            refs[-1][k] = ins[k][...]
    spectrum = jnp.concatenate(
        [
            jnp.concatenate([ref[c, p] for ref in ins for c in range(2)], 0)
            for p in range(share)
        ],
        1,
    )
    onsets = jnp.concatenate([onset_ref[pl.ds(first + p, 1), :] for p in range(share)], 1)
    muted = windowed(columns_ref, spectrum, onsets)
    back = jnp.dot(rows_ref[...], muted, preferred_element_type=F32).astype(BF16)
    for i, out in enumerate(outs):
        for c in range(2):
            for p in range(share):
                start = (2 * i + c) * width
                out[c, p] = back[start : start + width, p * LANES : (p + 1) * LANES]


def mute_source(ids, onset, rows, columns, pieces, copy):
    shape = pieces[0].shape
    outs = [jax.ShapeDtypeStruct(shape, BF16)] * len(pieces)
    if copy:
        outs = outs + [jax.ShapeDtypeStruct((len(pieces),) + shape, BF16)]
    return call(
        functools.partial(mute_source_kernel, int(copy)),
        "mute_source",
        outs,
        4 * NT * 2 * F * shape[1] * LANES,
        3 << 20,
        (ids, onset, rows, columns, *pieces),
    )


def trace_kernel(ids, onset_ref, rows_ref, *refs):
    ins, out_ref = refs[:4], refs[4]
    pieces, two, share = ins[0].shape[:3]
    step = pl.program_id(0)
    for j in range(4):

        @pl.when(step // share == j)
        def one():
            p = step % share
            spectrum = jnp.concatenate(
                [ins[j][k, c, p] for k in range(pieces) for c in range(2)], 0
            )
            signal = lax.dot_general(
                spectrum, rows_ref[...], (((0,), (0,)), ((), ())), preferred_element_type=F32
            )
            sample = lax.broadcasted_iota(jnp.int32, signal.shape, 1)
            out_ref[0] = jnp.where(sample < onset_ref[0], signal, 0.0).astype(BF16)


def trace_source(ids, onset, rows, groups):
    focal, sources = onset.shape
    share = groups[0].shape[2]

    def place(g, ids):
        return ((g // share) ^ ids[1]) * share + g % share, 0, 0

    return pl.pallas_call(
        trace_kernel,
        name="trace_source",
        out_shape=jax.ShapeDtypeStruct((focal, sources, NT), BF16),
        grid_spec=pltpu.PrefetchScalarGridSpec(
            num_scalar_prefetch=1,
            grid=(focal,),
            in_specs=[pl.BlockSpec((1, sources, 1), place)] + [VMEM_SPEC] * 5,
            out_specs=pl.BlockSpec((1, sources, NT), place),
        ),
        compiler_params=pltpu.CompilerParams(vmem_limit_bytes=VMEM_BYTES),
        cost_estimate=pl.CostEstimate(
            flops=2 * NT * 2 * F * focal * LANES, bytes_accessed=5 << 20, transcendentals=0
        ),
    )(ids, onset[:, :, None], rows, *groups)


def mute_receiver_kernel(first, both, last, ids, onset_ref, rows_ref, columns_ref, *refs):
    two, three, one, near, extra = refs[:5]
    pieces = 4
    direct = refs[5 : 5 + pieces]
    outs = refs[5 + pieces :]
    half = ids[0]
    count, width = one.shape[1], one.shape[2]
    lanes = pl.ds(pl.multiple_of(half * LANES, LANES), LANES)

    def part(k, c, p):
        if k == 0:
            return (near[1, c, p].astype(F32) + extra[1, c, p].astype(F32)).astype(BF16)
        return (None, one, two, three)[k][c, p]

    step = 2
    for start in range(0, count, step):
        group = range(start, start + step)
        spectrum = jnp.concatenate(
            [
                jnp.concatenate([part(k, c, p) for k in range(pieces) for c in range(2)], 0)
                for p in group
            ],
            1,
        )
        onsets = jnp.concatenate(
            [onset_ref[first + p : first + p + 1, lanes] for p in group], 1
        )
        muted = windowed(columns_ref, spectrum, onsets)
        back = jnp.dot(rows_ref[...], muted, preferred_element_type=F32)
        for k in range(pieces):
            for c in range(2):
                for i, p in enumerate(group):
                    at = (2 * k + c) * width
                    block = back[at : at + width, i * LANES : (i + 1) * LANES]
                    if k in both:
                        wave = direct[k][half, c, first + p]
                    else:
                        wave = direct[k][c, first + p]
                    value = (wave.astype(F32) + block).astype(BF16)
                    if last:
                        outs[0][c, k ^ ids[2], p] = value
                    else:
                        outs[k][c, p] = value


def mute_receiver(ids, onset, rows, columns, arrays, direct, first, both, last):
    shape = arrays[2].shape
    count, freq = shape[1], shape[2]
    if last:
        outs = jax.ShapeDtypeStruct((2, 4, count, freq, LANES), BF16)
    else:
        outs = [jax.ShapeDtypeStruct(shape, BF16)] * 4
    return call(
        functools.partial(mute_receiver_kernel, first, both, last),
        "mute_receiver",
        outs,
        4 * NT * 2 * F * count * LANES,
        4 << 20,
        (ids, onset, rows, columns, *arrays, *direct),
    )


def join_kernel(ids, *refs):
    ins, out_ref, hold = refs[:HALVES], refs[-2], refs[-1]
    two, foc_count, count, width, lanes = ins[0].shape
    focal = HALVES * count
    step = pl.program_id(0)
    for c in range(2):
        for q, ref in enumerate(ins):
            for p in range(count):
                hold[pl.ds(c * width * focal + q * count + p, width, stride=focal), :] = ref[
                    c, step, p
                ].astype(F32)
    out_ref[...] = hold[...].astype(BF16).reshape(out_ref.shape)


def join_halves(ids, parts, mask, into=None):
    two, foc_count, count, freq, lanes = parts[0].shape
    focal = HALVES * count
    extra = [] if into is None else [into]
    return pl.pallas_call(
        join_kernel,
        name="join_halves",
        out_shape=jax.ShapeDtypeStruct((two, foc_count * freq, focal, 2 * lanes), BF16),
        grid_spec=pltpu.PrefetchScalarGridSpec(
            num_scalar_prefetch=1,
            grid=(foc_count,),
            in_specs=[VMEM_SPEC] * HALVES + [pl.BlockSpec(memory_space=pl.ANY)] * len(extra),
            out_specs=pl.BlockSpec(
                (two, freq, focal, lanes), lambda g, ids: (0, g, 0, ids[0] ^ mask)
            ),
            scratch_shapes=[pltpu.VMEM((two * freq * focal, lanes), F32)],
        ),
        input_output_aliases={1 + HALVES: 0} if extra else {},
        compiler_params=pltpu.CompilerParams(vmem_limit_bytes=VMEM_BYTES),
        cost_estimate=pl.CostEstimate(
            flops=0, bytes_accessed=8 * foc_count * freq * focal * lanes, transcendentals=0
        ),
    )(ids, *parts, *extra)


def add(left, right):
    return (left.astype(F32) + right.astype(F32)).astype(BF16)


def resident(counts, reflection, direct_wave, onset_receiver, onset_source):
    src_count, rcv_count, foc_count = counts
    ids = jnp.stack([lax.axis_index("src"), lax.axis_index("rcv"), lax.axis_index("foc")])
    ids = ids.astype(jnp.int32)
    focal = direct_wave.shape[2]
    pieces = range(foc_count)
    near = (0, 1)

    def to_foc(value, k):
        return value if k == 0 else swap(value, "foc", k, foc_count)

    def to_src(value):
        return swap(value, "src", 1, src_count)

    def to_core(value):
        return swap(value, "rcv", 1, rcv_count)

    def to_y(value):
        return swap(value, "rcv", 2, rcv_count)

    def spread(value):
        across = to_y(value)
        return [value, to_core(value), across, to_core(across)]

    direct = [None] * foc_count
    direct[2] = split_wave(ids, direct_wave, 2, foc_count, False)
    rows, columns = basis(ids)
    later, rows, columns = lax.optimization_barrier((ids, rows, columns))
    direct[3] = split_wave(later, direct_wave, 3, foc_count, False)
    later, direct[3] = lax.optimization_barrier((ids, direct[3]))
    direct[1] = split_wave(later, direct_wave, 1, foc_count, True)
    direct[0] = split_wave(later, direct_wave, 0, foc_count, True)
    plan, arrays = [("both", 0, 0)], [direct[0]]
    for k in (2, 3, 1):
        got = to_foc(direct[k], k)
        if k in near:
            plan, arrays = plan + [("both", k, 0)], arrays + [got]
        else:
            plan = plan + [("own", k, 0), ("other", k, 0)]
            arrays = arrays + [got, to_src(got)]
    for iteration in range(ITERS):
        last = iteration == ITERS - 1
        keep, send = convolve_pieces(ids, reflection, tuple(plan), arrays, foc_count, focal)
        got = to_core(send)
        beyond = to_y(add(keep[1], got[1]))
        total = (keep[0].astype(F32) + got[0].astype(F32) + beyond.astype(F32)).astype(BF16)
        spectrum = [to_foc(total[k], k) for k in pieces]
        returned = mute_source(ids, onset_source, rows, columns, spectrum, last)
        mine = [to_foc(returned[k], k) for k in pieces]
        across = [to_y(value) for value in mine]
        groups = [mine, [to_core(v) for v in mine], across, [to_core(v) for v in across]]
        own, other = correlate_pieces(ids, reflection, groups)
        renewed = []
        early = []
        plan, arrays = [], []
        count = focal // HALVES
        for q in range(HALVES):
            far, close = 2 * q, 2 * q + 1
            got_far, got_close = to_src(other[far]), to_src(other[close])
            if q == 1:
                got_close, fresh = lax.optimization_barrier((got_close, fresh))
            ready = (
                to_foc(add(own[far][0], got_far[0]), 2),
                to_foc(add(own[far][1], got_far[1]), 3),
                to_foc(add(own[close][0], got_close[0]), 1),
                own[close],
                got_close,
            )
            if q == 1:
                ready, early = lax.optimization_barrier((ready, early))
            fresh = mute_receiver(
                ids, onset_receiver, rows, columns, ready, direct, q * count, near, last
            )
            if last:
                renewed.append(fresh)
                continue
            moved = [to_foc(fresh[k], k) for k in (2, 3, 1, 0)]
            if q == 0:
                before, early = moved, [to_src(moved[3])]
                continue
            after = [to_src(moved[3])]
            before[:2], moved[2], after = lax.optimization_barrier(
                (before[:2], moved[2], after)
            )
            crossed = [to_src(value) for value in before[:3]] + early
            after.append(to_src(moved[2]))
            after = [to_src(moved[0]), to_src(moved[1]), after[1], after[0]]
            arrays = before + crossed + moved + after
            plan = [
                (kind, k, start * count)
                for start in range(2)
                for kind in ("own", "other")
                for k in (2, 3, 1, 0)
            ]
        if last:
            crossed = [to_src(value) for value in renewed]
            muted_trace = trace_source(ids, onset_source, rows, spread(returned[-1]))
            partly = join_halves(ids, renewed, 0)
            return join_halves(ids, crossed, 1, partly), muted_trace


def local(counts, reflection, direct_wave, onset_receiver, onset_source):
    src_count, rcv_count, foc_count = counts
    two, freq, sources, receivers = reflection.shape
    focal = direct_wave.shape[2]
    fits = (
        (src_count, rcv_count, foc_count) == (2, 4, 4)
        and sources == LANES
        and receivers == 2 * LANES
        and focal == 8
        and freq == 4 * BLOCK_W
        and freq * foc_count == F
    )
    if fits:
        return resident(counts, reflection, direct_wave, onset_receiver, onset_source)
    return general(reflection, direct_wave, onset_receiver, onset_source)


def solution(mesh):
    in_specs = (
        P(None, "foc", "src", "rcv"),
        P(None, None, "foc", "rcv"),
        P("foc", "rcv"),
        P("foc", "src"),
    )
    out_specs = (P(None, None, "foc", "rcv"), P("foc", "src", None))
    counts = (mesh.shape["src"], mesh.shape["rcv"], mesh.shape["foc"])
    return jax.shard_map(
        functools.partial(local, counts),
        mesh=mesh,
        in_specs=in_specs,
        out_specs=out_specs,
        check_vma=False,
    )
```

```python
import functools
import math

import jax
import jax.numpy as jnp
from jax import lax
from jax.experimental import pallas as pl
from jax.experimental.pallas import tpu as pltpu
from jax.sharding import PartitionSpec as P

F = 256
NT = 1024
ITERS = 2
LANES = 128
BLOCK_W = 16
PITCH = 24
HALVES = 2
GROUP_ORDER = (4, 3, 15, 5, 12, 2, 6, 9, 7, 14, 11, 1, 10, 13, 0, 8)
F32 = jnp.float32
BF16 = jnp.bfloat16
VMEM_BYTES = 24 * 1024 * 1024


def basis_table():
    frequency_bins = jnp.arange(F, dtype=jnp.int32) + 1
    samples = jnp.arange(NT, dtype=jnp.int32)
    phases = frequency_bins[:, None] * samples[None, :] % NT
    angles = phases.astype(jnp.float32) * (2.0 * math.pi / NT)
    norming = math.sqrt(2.0 / NT)
    return (jnp.stack([jnp.cos(angles), -jnp.sin(angles)]) * norming).astype(jnp.bfloat16)


def mute_traces(spectrum, onsets, basis_rows):
    focal_count = spectrum.shape[2]
    samples = jnp.arange(NT, dtype=jnp.int32)

    def one_focus(focal_index, carry):
        muted_all, returned_all = carry
        one_spectrum = lax.dynamic_slice_in_dim(spectrum, focal_index, 1, 2)
        one_onset = lax.dynamic_slice_in_dim(onsets, focal_index, 1, 0)
        signal = jnp.einsum(
            "cwpr,cwt->prt", one_spectrum, basis_rows, preferred_element_type=jnp.float32
        )
        window = samples[None, None, :] < one_onset[:, :, None]
        muted_one = jnp.where(window, signal, 0.0).astype(jnp.bfloat16)
        returned = jnp.einsum(
            "prt,cwt->cwpr", muted_one, basis_rows, preferred_element_type=jnp.float32
        )
        muted_all = lax.dynamic_update_slice_in_dim(muted_all, muted_one, focal_index, 0)
        returned_all = lax.dynamic_update_slice_in_dim(returned_all, returned, focal_index, 2)
        return (muted_all, returned_all)

    initial = (
        jnp.zeros((focal_count, spectrum.shape[3], NT), jnp.bfloat16),
        jnp.zeros(spectrum.shape, jnp.float32),
    )
    return lax.fori_loop(0, focal_count, one_focus, initial)


def convolve(reflection, focusing):
    real_out = jnp.einsum(
        "wsr,wpr->wps", reflection[0], focusing[0], preferred_element_type=jnp.float32
    ) - jnp.einsum("wsr,wpr->wps", reflection[1], focusing[1], preferred_element_type=jnp.float32)
    imag_out = jnp.einsum(
        "wsr,wpr->wps", reflection[0], focusing[1], preferred_element_type=jnp.float32
    ) + jnp.einsum("wsr,wpr->wps", reflection[1], focusing[0], preferred_element_type=jnp.float32)
    return jnp.stack([real_out, imag_out])


def correlate(reflection, spectrum):
    real_out = jnp.einsum(
        "wsr,wps->wpr", reflection[0], spectrum[0], preferred_element_type=jnp.float32
    ) + jnp.einsum("wsr,wps->wpr", reflection[1], spectrum[1], preferred_element_type=jnp.float32)
    imag_out = jnp.einsum(
        "wsr,wps->wpr", reflection[0], spectrum[1], preferred_element_type=jnp.float32
    ) - jnp.einsum("wsr,wps->wpr", reflection[1], spectrum[0], preferred_element_type=jnp.float32)
    return jnp.stack([real_out, imag_out])


def renew(shares, direct_wave, onset_receiver, basis_rows, source_index):
    share_width = shares.shape[3]
    offset = source_index * share_width
    onset_share = lax.dynamic_slice_in_dim(onset_receiver, offset, share_width, 1)
    direct_share = lax.dynamic_slice_in_dim(direct_wave, offset, share_width, 3)
    unused, update = mute_traces(shares, onset_share, basis_rows)
    renewed = (direct_share.astype(jnp.float32) + update).astype(jnp.bfloat16)
    return lax.all_gather(renewed, "src", axis=3, tiled=True)


def general(reflection, direct_wave, onset_receiver, onset_source):
    basis_rows = basis_table()
    source_index = lax.axis_index("src")
    whole_reflection = lax.all_gather(reflection, "foc", axis=1, tiled=True)
    focusing = direct_wave
    muted_trace = None
    for iteration in range(ITERS):
        partial_value = convolve(whole_reflection, focusing)
        spectrum = lax.psum(partial_value.astype(jnp.bfloat16), "rcv")
        muted_trace, returned = mute_traces(spectrum, onset_source, basis_rows)
        partial_adjoint = correlate(whole_reflection, returned.astype(jnp.bfloat16))
        shares = lax.psum_scatter(
            partial_adjoint.astype(jnp.bfloat16), "src", scatter_dimension=3, tiled=True
        )
        focusing = renew(shares, direct_wave, onset_receiver, basis_rows, source_index)
    return (focusing, muted_trace)


VMEM_SPEC = pl.BlockSpec(memory_space=pltpu.VMEM)
SMEM_SPEC = pl.BlockSpec(memory_space=pltpu.SMEM)


def swap(value, axis, mask, count):
    return lax.ppermute(value, axis, [(i, i ^ mask) for i in range(count)])


def call(kernel, name, out_shape, flops, size, operands, scratch=()):
    many = isinstance(out_shape, list)
    return pl.pallas_call(
        kernel,
        name=name,
        out_shape=out_shape,
        in_specs=[SMEM_SPEC] + [VMEM_SPEC] * (len(operands) - 1),
        out_specs=[VMEM_SPEC] * len(out_shape) if many else VMEM_SPEC,
        scratch_shapes=list(scratch),
        compiler_params=pltpu.CompilerParams(vmem_limit_bytes=VMEM_BYTES),
        cost_estimate=pl.CostEstimate(flops=flops, bytes_accessed=size, transcendentals=0),
    )(*operands)


def table(frequency, part, sample):
    phase = ((frequency + 1) * sample + part * (NT // 4)) & (NT - 1)
    x = (jnp.abs(phase - NT // 2) - NT // 4).astype(F32) * (4.0 / NT)
    square = x * x
    total = jnp.zeros_like(x)
    for order in (11, 9, 7, 5, 3, 1):
        sign = -1.0 if order % 4 == 3 else 1.0
        total = total * square + sign * (math.pi / 2) ** order / math.factorial(order)
    return (total * x * math.sqrt(2.0 / NT)).astype(BF16)


def basis_kernel(ids, rows_ref, columns_ref):
    size = rows_ref.shape[0]
    freq = BLOCK_W * 4
    pieces = size // (2 * freq)
    for k in range(pieces):
        first = (k ^ ids[2]) * freq
        for c in range(2):
            frequency = lax.broadcasted_iota(jnp.int32, (freq, NT), 0) + first
            sample = lax.broadcasted_iota(jnp.int32, (freq, NT), 1)
            start = (2 * k + c) * freq
            rows_ref[start : start + freq, :] = table(frequency, c, sample)
        lane = lax.broadcasted_iota(jnp.int32, (NT, 2 * freq), 1)
        sample = lax.broadcasted_iota(jnp.int32, (NT, 2 * freq), 0)
        part = (lane >= freq).astype(jnp.int32)
        start = 2 * k * freq
        columns_ref[:, start : start + 2 * freq] = table(lane - part * freq + first, part, sample)


def basis(ids):
    size = 2 * F
    return call(
        basis_kernel,
        "basis",
        [jax.ShapeDtypeStruct((size, NT), BF16), jax.ShapeDtypeStruct((NT, size), BF16)],
        40 * size * NT,
        4 * size * NT,
        (ids,),
    )


def split_kernel(both, ids, wave_ref, out_ref, hold):
    width, focal = wave_ref.shape[1], wave_ref.shape[2]
    for place in range(2 if both else 1):
        lanes = slice(place * LANES, (place + 1) * LANES)
        hold[...] = wave_ref[0, :, :, lanes].astype(F32).reshape(width * focal, LANES)
        for p in range(focal):
            rows = hold[pl.ds(p, width, stride=focal), :].astype(BF16)
            if both:
                out_ref[place, 0, p] = rows
            else:
                out_ref[0, p] = rows


def split_wave(ids, wave, piece, foc_count, both):
    freq = wave.shape[1] // foc_count
    focal = wave.shape[2]
    if both:
        shape = (2, 2, focal, freq, LANES)
        in_spec = pl.BlockSpec(
            (1, freq, focal, 2 * LANES), lambda c, ids: (c, ids[2] ^ piece, 0, 0)
        )
        out_spec = pl.BlockSpec((2, 1, focal, freq, LANES), lambda c, ids: (0, c, 0, 0, 0))
    else:
        shape = (2, focal, freq, LANES)
        in_spec = pl.BlockSpec(
            (1, freq, focal, LANES), lambda c, ids: (c, ids[2] ^ piece, 0, ids[0])
        )
        out_spec = pl.BlockSpec((1, focal, freq, LANES), lambda c, ids: (c, 0, 0, 0))
    return pl.pallas_call(
        functools.partial(split_kernel, both),
        name="split_wave",
        out_shape=jax.ShapeDtypeStruct(shape, BF16),
        grid_spec=pltpu.PrefetchScalarGridSpec(
            num_scalar_prefetch=1,
            grid=(2,),
            in_specs=[in_spec],
            out_specs=out_spec,
            scratch_shapes=[pltpu.VMEM((freq * focal, LANES), F32)],
        ),
        compiler_params=pltpu.CompilerParams(vmem_limit_bytes=VMEM_BYTES),
        cost_estimate=pl.CostEstimate(
            flops=0, bytes_accessed=8 * focal * freq * LANES, transcendentals=0
        ),
    )(ids, wave)


def convolve_kernel(plan, pieces, focal, ids, refl_ref, *refs):
    ins = refs[: len(plan)]
    keep_ref, send_ref, hold, result = refs[len(plan) :]
    half, me = ids[0], ids[1]
    sources = refl_ref.shape[2]
    rows = pieces * 2 * focal
    share = focal // 4

    def block(b, carry):
        first = pl.multiple_of(b * BLOCK_W, BLOCK_W)
        window = pl.ds(first, BLOCK_W)

        def put(place, k, c, start, value):
            for p in range(value.shape[0]):
                at = ((k * 2 + c) * focal + start + p) * PITCH
                hold[place, at : at + BLOCK_W, :] = value[p].astype(F32)

        for ref, (kind, k, start) in zip(ins, plan):
            for c in range(2):
                if kind == "both":
                    put(0, k, c, start, ref[0, c, :, window, :])
                    put(1, k, c, start, ref[1, c, :, window, :])
                elif kind == "own":
                    put(half, k, c, start, ref[c, :, window, :])
                else:
                    put(1 - half, k, c, start, ref[c, :, window, :])
        for w in range(BLOCK_W):
            step = pl.ds(w, rows, stride=PITCH)
            left = jnp.concatenate([hold[0, step, :], hold[1, step, :]], 1).astype(BF16)
            right = refl_ref[:, first + w].reshape(2 * sources, 2 * LANES)
            both = lax.dot_general(
                left, right, (((1,), (1,)), ((), ())), preferred_element_type=F32
            )
            by_real = both[:, :LANES].reshape(pieces, 2, focal, LANES)
            by_imag = both[:, LANES:].reshape(pieces, 2, focal, LANES)
            value = jnp.stack(
                [by_real[:, 0] - by_imag[:, 1], by_real[:, 1] + by_imag[:, 0]], 1
            )
            result[step, :] = value.reshape(rows, LANES)
        for place, out in ((0, keep_ref), (1, send_ref)):
            for y in range(2):
                group = (2 * y + place) ^ me
                for k in range(pieces):
                    for c in range(2):
                        for p in range(share):
                            start = ((k * 2 + c) * focal + group * share + p) * PITCH
                            part = result[pl.ds(pl.multiple_of(start, 8), BLOCK_W), :]
                            out[y, k, c, p, window, :] = part.astype(BF16)
        return carry

    lax.fori_loop(0, refl_ref.shape[1] // BLOCK_W, block, 0)


def convolve_pieces(ids, reflection, plan, arrays, pieces, focal):
    two, freq, sources, receivers = reflection.shape
    rows = pieces * 2 * focal
    out = jax.ShapeDtypeStruct((2, pieces, 2, focal // 4, freq, LANES), BF16)
    return call(
        functools.partial(convolve_kernel, plan, pieces, focal),
        "convolve",
        [out, out],
        2 * freq * rows * 256 * 256,
        freq * (2 * sources * 512 + rows * 768),
        (ids, reflection, *arrays),
        [
            pltpu.VMEM((2, rows * PITCH, LANES), F32),
            pltpu.VMEM((rows * PITCH, LANES), F32),
        ],
    )


def correlate_kernel(pieces, ids, refl_ref, *refs):
    ins = [[refs[GROUP_ORDER.index(j * pieces + k)] for k in range(pieces)] for j in range(4)]
    outs = refs[4 * pieces : -2]
    hold, result = refs[-2:]
    half, me = ids[0], ids[1]
    share = ins[0][0].shape[1]
    focal = 4 * share
    sources = refl_ref.shape[2]
    rows = pieces * focal
    part_size = focal // HALVES

    def block(b, carry):
        first = pl.multiple_of(b * BLOCK_W, BLOCK_W)
        window = pl.ds(first, BLOCK_W)
        for j in range(4):
            group = j ^ me
            for k in range(pieces):
                for p in range(share):
                    start = pl.multiple_of((k * focal + group * share + p) * PITCH, 8)
                    for c in range(2):
                        value = ins[j][k][c, p, window, :].astype(F32)
                        hold[c, pl.ds(start, BLOCK_W), :] = value
        for w in range(BLOCK_W):
            step = pl.ds(w, rows, stride=PITCH)
            real = hold[0, step, :].astype(BF16)
            imag = hold[1, step, :].astype(BF16)
            left = jnp.concatenate(
                [jnp.concatenate([real, imag], 1), jnp.concatenate([imag, -real], 1)], 0
            )
            right = refl_ref[:, first + w].reshape(2 * sources, 2 * LANES)
            value = lax.dot_general(
                left, right, (((1,), (0,)), ((), ())), preferred_element_type=F32
            )
            step = pl.ds(w, 2 * rows, stride=PITCH)
            result[0, step, :] = value[:, :LANES]
            result[1, step, :] = value[:, LANES:]
        index = 0
        for place in (half, 1 - half):
            for q in range(HALVES):
                for group in PAIRS:
                    for i, k in enumerate(group):
                        for c in range(2):
                            for p in range(part_size):
                                at = ((c * pieces + k) * focal + q * part_size + p) * PITCH
                                part = result[place, at : at + BLOCK_W, :]
                                outs[index][i, c, p, window, :] = part.astype(BF16)
                    index += 1
        return carry

    lax.fori_loop(0, refl_ref.shape[1] // BLOCK_W, block, 0)


PAIRS = ((2, 3), (1, 0))


def correlate_pieces(ids, reflection, groups):
    pieces = len(groups[0])
    two, share, freq, lanes = groups[0][0].shape
    focal = 4 * share
    sources = reflection.shape[2]
    rows = pieces * 2 * focal
    out = jax.ShapeDtypeStruct((2, 2, focal // HALVES, freq, LANES), BF16)
    count = HALVES * len(PAIRS)
    results = call(
        functools.partial(correlate_kernel, pieces),
        "correlate",
        [out] * (2 * count),
        2 * freq * rows * 256 * 256,
        freq * (2 * sources * 512 + rows * 768),
        (ids, reflection, *[groups[i // pieces][i % pieces] for i in GROUP_ORDER]),
        [
            pltpu.VMEM((2, rows // 2 * PITCH, LANES), F32),
            pltpu.VMEM((2, rows * PITCH, LANES), F32),
        ],
    )
    return results[:count], results[count:]


def windowed(columns_ref, rows, onsets):
    signal = jnp.dot(columns_ref[...], rows, preferred_element_type=F32)
    sample = lax.broadcasted_iota(jnp.int32, signal.shape, 0)
    return jnp.where(sample < onsets, signal, 0.0).astype(BF16)


def mute_source_kernel(copy, ids, onset_ref, rows_ref, columns_ref, *refs):
    pieces = (len(refs) - copy) // 2
    ins, outs = refs[:pieces], refs[pieces : 2 * pieces]
    share, width = ins[0].shape[1], ins[0].shape[2]
    first = ids[1] * share
    if copy:
        for k in range(pieces):
            refs[-1][k] = ins[k][...]
    spectrum = jnp.concatenate(
        [
            jnp.concatenate([ref[c, p] for ref in ins for c in range(2)], 0)
            for p in range(share)
        ],
        1,
    )
    onsets = jnp.concatenate([onset_ref[pl.ds(first + p, 1), :] for p in range(share)], 1)
    muted = windowed(columns_ref, spectrum, onsets)
    back = jnp.dot(rows_ref[...], muted, preferred_element_type=F32).astype(BF16)
    for i, out in enumerate(outs):
        for c in range(2):
            for p in range(share):
                start = (2 * i + c) * width
                out[c, p] = back[start : start + width, p * LANES : (p + 1) * LANES]


def mute_source(ids, onset, rows, columns, pieces, copy):
    shape = pieces[0].shape
    outs = [jax.ShapeDtypeStruct(shape, BF16)] * len(pieces)
    if copy:
        outs = outs + [jax.ShapeDtypeStruct((len(pieces),) + shape, BF16)]
    return call(
        functools.partial(mute_source_kernel, int(copy)),
        "mute_source",
        outs,
        4 * NT * 2 * F * shape[1] * LANES,
        3 << 20,
        (ids, onset, rows, columns, *pieces),
    )


def trace_kernel(ids, onset_ref, rows_ref, *refs):
    ins, out_ref = refs[:4], refs[4]
    pieces, two, share = ins[0].shape[:3]
    step = pl.program_id(0)
    for j in range(4):

        @pl.when(step // share == j)
        def one():
            p = step % share
            spectrum = jnp.concatenate(
                [ins[j][k, c, p] for k in range(pieces) for c in range(2)], 0
            )
            signal = lax.dot_general(
                spectrum, rows_ref[...], (((0,), (0,)), ((), ())), preferred_element_type=F32
            )
            sample = lax.broadcasted_iota(jnp.int32, signal.shape, 1)
            out_ref[0] = jnp.where(sample < onset_ref[0], signal, 0.0).astype(BF16)


def trace_source(ids, onset, rows, groups):
    focal, sources = onset.shape
    share = groups[0].shape[2]

    def place(g, ids):
        return ((g // share) ^ ids[1]) * share + g % share, 0, 0

    return pl.pallas_call(
        trace_kernel,
        name="trace_source",
        out_shape=jax.ShapeDtypeStruct((focal, sources, NT), BF16),
        grid_spec=pltpu.PrefetchScalarGridSpec(
            num_scalar_prefetch=1,
            grid=(focal,),
            in_specs=[pl.BlockSpec((1, sources, 1), place)] + [VMEM_SPEC] * 5,
            out_specs=pl.BlockSpec((1, sources, NT), place),
        ),
        compiler_params=pltpu.CompilerParams(vmem_limit_bytes=VMEM_BYTES),
        cost_estimate=pl.CostEstimate(
            flops=2 * NT * 2 * F * focal * LANES, bytes_accessed=5 << 20, transcendentals=0
        ),
    )(ids, onset[:, :, None], rows, *groups)


def mute_receiver_kernel(first, both, last, ids, onset_ref, rows_ref, columns_ref, *refs):
    two, three, one, near, extra = refs[:5]
    pieces = 4
    direct = refs[5 : 5 + pieces]
    outs = refs[5 + pieces :]
    half = ids[0]
    count, width = one.shape[1], one.shape[2]
    lanes = pl.ds(pl.multiple_of(half * LANES, LANES), LANES)

    def part(k, c, p):
        if k == 0:
            return (near[1, c, p].astype(F32) + extra[1, c, p].astype(F32)).astype(BF16)
        return (None, one, two, three)[k][c, p]

    step = 2
    for start in range(0, count, step):
        group = range(start, start + step)
        spectrum = jnp.concatenate(
            [
                jnp.concatenate([part(k, c, p) for k in range(pieces) for c in range(2)], 0)
                for p in group
            ],
            1,
        )
        onsets = jnp.concatenate(
            [onset_ref[first + p : first + p + 1, lanes] for p in group], 1
        )
        muted = windowed(columns_ref, spectrum, onsets)
        back = jnp.dot(rows_ref[...], muted, preferred_element_type=F32)
        for k in range(pieces):
            for c in range(2):
                for i, p in enumerate(group):
                    at = (2 * k + c) * width
                    block = back[at : at + width, i * LANES : (i + 1) * LANES]
                    if k in both:
                        wave = direct[k][half, c, first + p]
                    else:
                        wave = direct[k][c, first + p]
                    value = (wave.astype(F32) + block).astype(BF16)
                    if last:
                        outs[0][c, k ^ ids[2], p] = value
                    else:
                        outs[k][c, p] = value


def mute_receiver(ids, onset, rows, columns, arrays, direct, first, both, last):
    shape = arrays[2].shape
    count, freq = shape[1], shape[2]
    if last:
        outs = jax.ShapeDtypeStruct((2, 4, count, freq, LANES), BF16)
    else:
        outs = [jax.ShapeDtypeStruct(shape, BF16)] * 4
    return call(
        functools.partial(mute_receiver_kernel, first, both, last),
        "mute_receiver",
        outs,
        4 * NT * 2 * F * count * LANES,
        4 << 20,
        (ids, onset, rows, columns, *arrays, *direct),
    )


def join_kernel(ids, *refs):
    ins, out_ref, hold = refs[:HALVES], refs[-2], refs[-1]
    two, foc_count, count, width, lanes = ins[0].shape
    focal = HALVES * count
    step = pl.program_id(0)
    for c in range(2):
        for q, ref in enumerate(ins):
            for p in range(count):
                hold[pl.ds(c * width * focal + q * count + p, width, stride=focal), :] = ref[
                    c, step, p
                ].astype(F32)
    out_ref[...] = hold[...].astype(BF16).reshape(out_ref.shape)


def join_halves(ids, parts, mask, into=None):
    two, foc_count, count, freq, lanes = parts[0].shape
    focal = HALVES * count
    extra = [] if into is None else [into]
    return pl.pallas_call(
        join_kernel,
        name="join_halves",
        out_shape=jax.ShapeDtypeStruct((two, foc_count * freq, focal, 2 * lanes), BF16),
        grid_spec=pltpu.PrefetchScalarGridSpec(
            num_scalar_prefetch=1,
            grid=(foc_count,),
            in_specs=[VMEM_SPEC] * HALVES + [pl.BlockSpec(memory_space=pl.ANY)] * len(extra),
            out_specs=pl.BlockSpec(
                (two, freq, focal, lanes), lambda g, ids: (0, g, 0, ids[0] ^ mask)
            ),
            scratch_shapes=[pltpu.VMEM((two * freq * focal, lanes), F32)],
        ),
        input_output_aliases={1 + HALVES: 0} if extra else {},
        compiler_params=pltpu.CompilerParams(vmem_limit_bytes=VMEM_BYTES),
        cost_estimate=pl.CostEstimate(
            flops=0, bytes_accessed=8 * foc_count * freq * focal * lanes, transcendentals=0
        ),
    )(ids, *parts, *extra)


def add(left, right):
    return (left.astype(F32) + right.astype(F32)).astype(BF16)


def resident(counts, reflection, direct_wave, onset_receiver, onset_source):
    src_count, rcv_count, foc_count = counts
    ids = jnp.stack([lax.axis_index("src"), lax.axis_index("rcv"), lax.axis_index("foc")])
    ids = ids.astype(jnp.int32)
    focal = direct_wave.shape[2]
    pieces = range(foc_count)
    near = (0, 1)

    def to_foc(value, k):
        return value if k == 0 else swap(value, "foc", k, foc_count)

    def to_src(value):
        return swap(value, "src", 1, src_count)

    def to_core(value):
        return swap(value, "rcv", 1, rcv_count)

    def to_y(value):
        return swap(value, "rcv", 2, rcv_count)

    def spread(value):
        across = to_y(value)
        return [value, to_core(value), across, to_core(across)]

    direct = [None] * foc_count
    direct[2] = split_wave(ids, direct_wave, 2, foc_count, False)
    rows, columns = basis(ids)
    later, rows, columns = lax.optimization_barrier((ids, rows, columns))
    direct[3] = split_wave(later, direct_wave, 3, foc_count, False)
    later, direct[3] = lax.optimization_barrier((ids, direct[3]))
    direct[1] = split_wave(later, direct_wave, 1, foc_count, True)
    direct[0] = split_wave(later, direct_wave, 0, foc_count, True)
    plan, arrays = [("both", 0, 0)], [direct[0]]
    for k in (2, 3, 1):
        got = to_foc(direct[k], k)
        if k in near:
            plan, arrays = plan + [("both", k, 0)], arrays + [got]
        else:
            plan = plan + [("own", k, 0), ("other", k, 0)]
            arrays = arrays + [got, to_src(got)]
    for iteration in range(ITERS):
        last = iteration == ITERS - 1
        keep, send = convolve_pieces(ids, reflection, tuple(plan), arrays, foc_count, focal)
        got = to_core(send)
        beyond = to_y(add(keep[1], got[1]))
        total = (keep[0].astype(F32) + got[0].astype(F32) + beyond.astype(F32)).astype(BF16)
        spectrum = [to_foc(total[k], k) for k in pieces]
        returned = mute_source(ids, onset_source, rows, columns, spectrum, last)
        mine = [to_foc(returned[k], k) for k in pieces]
        across = [to_y(value) for value in mine]
        groups = [mine, [to_core(v) for v in mine], across, [to_core(v) for v in across]]
        own, other = correlate_pieces(ids, reflection, groups)
        renewed = []
        early = []
        plan, arrays = [], []
        count = focal // HALVES
        for q in range(HALVES):
            far, close = 2 * q, 2 * q + 1
            got_far, got_close = to_src(other[far]), to_src(other[close])
            if q == 1:
                got_close, fresh = lax.optimization_barrier((got_close, fresh))
            ready = (
                to_foc(add(own[far][0], got_far[0]), 2),
                to_foc(add(own[far][1], got_far[1]), 3),
                to_foc(add(own[close][0], got_close[0]), 1),
                own[close],
                got_close,
            )
            if q == 1:
                ready, early = lax.optimization_barrier((ready, early))
            fresh = mute_receiver(
                ids, onset_receiver, rows, columns, ready, direct, q * count, near, last
            )
            if last:
                renewed.append(fresh)
                continue
            moved = [to_foc(fresh[k], k) for k in (2, 3, 1, 0)]
            if q == 0:
                before, early = moved, [to_src(moved[3])]
                continue
            after = [to_src(moved[3])]
            before[:2], moved[2], after = lax.optimization_barrier(
                (before[:2], moved[2], after)
            )
            crossed = [to_src(value) for value in before[:3]] + early
            after.append(to_src(moved[2]))
            after = [to_src(moved[0]), to_src(moved[1]), after[1], after[0]]
            arrays = before + crossed + moved + after
            plan = [
                (kind, k, start * count)
                for start in range(2)
                for kind in ("own", "other")
                for k in (2, 3, 1, 0)
            ]
        if last:
            crossed = [to_src(value) for value in renewed]
            muted_trace = trace_source(ids, onset_source, rows, spread(returned[-1]))
            partly = join_halves(ids, renewed, 0)
            return join_halves(ids, crossed, 1, partly), muted_trace


def local(counts, reflection, direct_wave, onset_receiver, onset_source):
    src_count, rcv_count, foc_count = counts
    two, freq, sources, receivers = reflection.shape
    focal = direct_wave.shape[2]
    fits = (
        (src_count, rcv_count, foc_count) == (2, 4, 4)
        and sources == LANES
        and receivers == 2 * LANES
        and focal == 8
        and freq == 4 * BLOCK_W
        and freq * foc_count == F
    )
    if fits:
        return resident(counts, reflection, direct_wave, onset_receiver, onset_source)
    return general(reflection, direct_wave, onset_receiver, onset_source)


def solution(mesh):
    in_specs = (
        P(None, "foc", "src", "rcv"),
        P(None, None, "foc", "rcv"),
        P("foc", "rcv"),
        P("foc", "src"),
    )
    out_specs = (P(None, None, "foc", "rcv"), P("foc", "src", None))
    counts = (mesh.shape["src"], mesh.shape["rcv"], mesh.shape["foc"])
    return jax.shard_map(
        functools.partial(local, counts),
        mesh=mesh,
        in_specs=in_specs,
        out_specs=out_specs,
        check_vma=False,
    )
```

```python
import functools
import math

import jax
import jax.numpy as jnp
from jax import lax
from jax.experimental import pallas as pl
from jax.experimental.pallas import tpu as pltpu
from jax.sharding import PartitionSpec as P

F = 256
NT = 1024
ITERS = 2
LANES = 128
BLOCK_W = 16
PITCH = 24
HALVES = 2
GROUP_ORDER = (4, 3, 15, 5, 12, 2, 6, 9, 7, 14, 11, 1, 10, 13, 0, 8)
F32 = jnp.float32
BF16 = jnp.bfloat16
VMEM_BYTES = 24 * 1024 * 1024


def basis_table():
    frequency_bins = jnp.arange(F, dtype=jnp.int32) + 1
    samples = jnp.arange(NT, dtype=jnp.int32)
    phases = frequency_bins[:, None] * samples[None, :] % NT
    angles = phases.astype(jnp.float32) * (2.0 * math.pi / NT)
    norming = math.sqrt(2.0 / NT)
    return (jnp.stack([jnp.cos(angles), -jnp.sin(angles)]) * norming).astype(jnp.bfloat16)


def mute_traces(spectrum, onsets, basis_rows):
    focal_count = spectrum.shape[2]
    samples = jnp.arange(NT, dtype=jnp.int32)

    def one_focus(focal_index, carry):
        muted_all, returned_all = carry
        one_spectrum = lax.dynamic_slice_in_dim(spectrum, focal_index, 1, 2)
        one_onset = lax.dynamic_slice_in_dim(onsets, focal_index, 1, 0)
        signal = jnp.einsum(
            "cwpr,cwt->prt", one_spectrum, basis_rows, preferred_element_type=jnp.float32
        )
        window = samples[None, None, :] < one_onset[:, :, None]
        muted_one = jnp.where(window, signal, 0.0).astype(jnp.bfloat16)
        returned = jnp.einsum(
            "prt,cwt->cwpr", muted_one, basis_rows, preferred_element_type=jnp.float32
        )
        muted_all = lax.dynamic_update_slice_in_dim(muted_all, muted_one, focal_index, 0)
        returned_all = lax.dynamic_update_slice_in_dim(returned_all, returned, focal_index, 2)
        return (muted_all, returned_all)

    initial = (
        jnp.zeros((focal_count, spectrum.shape[3], NT), jnp.bfloat16),
        jnp.zeros(spectrum.shape, jnp.float32),
    )
    return lax.fori_loop(0, focal_count, one_focus, initial)


def convolve(reflection, focusing):
    real_out = jnp.einsum(
        "wsr,wpr->wps", reflection[0], focusing[0], preferred_element_type=jnp.float32
    ) - jnp.einsum("wsr,wpr->wps", reflection[1], focusing[1], preferred_element_type=jnp.float32)
    imag_out = jnp.einsum(
        "wsr,wpr->wps", reflection[0], focusing[1], preferred_element_type=jnp.float32
    ) + jnp.einsum("wsr,wpr->wps", reflection[1], focusing[0], preferred_element_type=jnp.float32)
    return jnp.stack([real_out, imag_out])


def correlate(reflection, spectrum):
    real_out = jnp.einsum(
        "wsr,wps->wpr", reflection[0], spectrum[0], preferred_element_type=jnp.float32
    ) + jnp.einsum("wsr,wps->wpr", reflection[1], spectrum[1], preferred_element_type=jnp.float32)
    imag_out = jnp.einsum(
        "wsr,wps->wpr", reflection[0], spectrum[1], preferred_element_type=jnp.float32
    ) - jnp.einsum("wsr,wps->wpr", reflection[1], spectrum[0], preferred_element_type=jnp.float32)
    return jnp.stack([real_out, imag_out])


def renew(shares, direct_wave, onset_receiver, basis_rows, source_index):
    share_width = shares.shape[3]
    offset = source_index * share_width
    onset_share = lax.dynamic_slice_in_dim(onset_receiver, offset, share_width, 1)
    direct_share = lax.dynamic_slice_in_dim(direct_wave, offset, share_width, 3)
    unused, update = mute_traces(shares, onset_share, basis_rows)
    renewed = (direct_share.astype(jnp.float32) + update).astype(jnp.bfloat16)
    return lax.all_gather(renewed, "src", axis=3, tiled=True)


def general(reflection, direct_wave, onset_receiver, onset_source):
    basis_rows = basis_table()
    source_index = lax.axis_index("src")
    whole_reflection = lax.all_gather(reflection, "foc", axis=1, tiled=True)
    focusing = direct_wave
    muted_trace = None
    for iteration in range(ITERS):
        partial_value = convolve(whole_reflection, focusing)
        spectrum = lax.psum(partial_value.astype(jnp.bfloat16), "rcv")
        muted_trace, returned = mute_traces(spectrum, onset_source, basis_rows)
        partial_adjoint = correlate(whole_reflection, returned.astype(jnp.bfloat16))
        shares = lax.psum_scatter(
            partial_adjoint.astype(jnp.bfloat16), "src", scatter_dimension=3, tiled=True
        )
        focusing = renew(shares, direct_wave, onset_receiver, basis_rows, source_index)
    return (focusing, muted_trace)


VMEM_SPEC = pl.BlockSpec(memory_space=pltpu.VMEM)
SMEM_SPEC = pl.BlockSpec(memory_space=pltpu.SMEM)


def swap(value, axis, mask, count):
    return lax.ppermute(value, axis, [(i, i ^ mask) for i in range(count)])


def call(kernel, name, out_shape, flops, size, operands, scratch=()):
    many = isinstance(out_shape, list)
    return pl.pallas_call(
        kernel,
        name=name,
        out_shape=out_shape,
        in_specs=[SMEM_SPEC] + [VMEM_SPEC] * (len(operands) - 1),
        out_specs=[VMEM_SPEC] * len(out_shape) if many else VMEM_SPEC,
        scratch_shapes=list(scratch),
        compiler_params=pltpu.CompilerParams(vmem_limit_bytes=VMEM_BYTES),
        cost_estimate=pl.CostEstimate(flops=flops, bytes_accessed=size, transcendentals=0),
    )(*operands)


def table(frequency, part, sample):
    phase = ((frequency + 1) * sample + part * (NT // 4)) & (NT - 1)
    x = (jnp.abs(phase - NT // 2) - NT // 4).astype(F32) * (4.0 / NT)
    square = x * x
    total = jnp.zeros_like(x)
    for order in (11, 9, 7, 5, 3, 1):
        sign = -1.0 if order % 4 == 3 else 1.0
        total = total * square + sign * (math.pi / 2) ** order / math.factorial(order)
    return (total * x * math.sqrt(2.0 / NT)).astype(BF16)


def basis_kernel(ids, rows_ref, columns_ref):
    size = rows_ref.shape[0]
    freq = BLOCK_W * 4
    pieces = size // (2 * freq)
    for k in range(pieces):
        first = (k ^ ids[2]) * freq
        for c in range(2):
            frequency = lax.broadcasted_iota(jnp.int32, (freq, NT), 0) + first
            sample = lax.broadcasted_iota(jnp.int32, (freq, NT), 1)
            start = (2 * k + c) * freq
            rows_ref[start : start + freq, :] = table(frequency, c, sample)
        lane = lax.broadcasted_iota(jnp.int32, (NT, 2 * freq), 1)
        sample = lax.broadcasted_iota(jnp.int32, (NT, 2 * freq), 0)
        part = (lane >= freq).astype(jnp.int32)
        start = 2 * k * freq
        columns_ref[:, start : start + 2 * freq] = table(lane - part * freq + first, part, sample)


def basis(ids):
    size = 2 * F
    return call(
        basis_kernel,
        "basis",
        [jax.ShapeDtypeStruct((size, NT), BF16), jax.ShapeDtypeStruct((NT, size), BF16)],
        40 * size * NT,
        4 * size * NT,
        (ids,),
    )


def split_kernel(both, ids, wave_ref, out_ref, hold):
    width, focal = wave_ref.shape[1], wave_ref.shape[2]
    for place in range(2 if both else 1):
        lanes = slice(place * LANES, (place + 1) * LANES)
        hold[...] = wave_ref[0, :, :, lanes].astype(F32).reshape(width * focal, LANES)
        for p in range(focal):
            rows = hold[pl.ds(p, width, stride=focal), :].astype(BF16)
            if both:
                out_ref[place, 0, p] = rows
            else:
                out_ref[0, p] = rows


def split_wave(ids, wave, piece, foc_count, both):
    freq = wave.shape[1] // foc_count
    focal = wave.shape[2]
    if both:
        shape = (2, 2, focal, freq, LANES)
        in_spec = pl.BlockSpec(
            (1, freq, focal, 2 * LANES), lambda c, ids: (c, ids[2] ^ piece, 0, 0)
        )
        out_spec = pl.BlockSpec((2, 1, focal, freq, LANES), lambda c, ids: (0, c, 0, 0, 0))
    else:
        shape = (2, focal, freq, LANES)
        in_spec = pl.BlockSpec(
            (1, freq, focal, LANES), lambda c, ids: (c, ids[2] ^ piece, 0, ids[0])
        )
        out_spec = pl.BlockSpec((1, focal, freq, LANES), lambda c, ids: (c, 0, 0, 0))
    return pl.pallas_call(
        functools.partial(split_kernel, both),
        name="split_wave",
        out_shape=jax.ShapeDtypeStruct(shape, BF16),
        grid_spec=pltpu.PrefetchScalarGridSpec(
            num_scalar_prefetch=1,
            grid=(2,),
            in_specs=[in_spec],
            out_specs=out_spec,
            scratch_shapes=[pltpu.VMEM((freq * focal, LANES), F32)],
        ),
        compiler_params=pltpu.CompilerParams(vmem_limit_bytes=VMEM_BYTES),
        cost_estimate=pl.CostEstimate(
            flops=0, bytes_accessed=8 * focal * freq * LANES, transcendentals=0
        ),
    )(ids, pltpu.with_memory_space_constraint(wave, pltpu.HBM))


def convolve_kernel(plan, pieces, focal, ids, refl_ref, *refs):
    ins = refs[: len(plan)]
    keep_ref, send_ref, hold, result = refs[len(plan) :]
    half, me = ids[0], ids[1]
    sources = refl_ref.shape[2]
    rows = pieces * 2 * focal
    share = focal // 4

    def block(b, carry):
        first = pl.multiple_of(b * BLOCK_W, BLOCK_W)
        window = pl.ds(first, BLOCK_W)

        def put(place, k, c, start, value):
            for p in range(value.shape[0]):
                at = ((k * 2 + c) * focal + start + p) * PITCH
                hold[place, at : at + BLOCK_W, :] = value[p].astype(F32)

        for ref, (kind, k, start) in zip(ins, plan):
            for c in range(2):
                if kind == "both":
                    put(0, k, c, start, ref[0, c, :, window, :])
                    put(1, k, c, start, ref[1, c, :, window, :])
                elif kind == "own":
                    put(half, k, c, start, ref[c, :, window, :])
                else:
                    put(1 - half, k, c, start, ref[c, :, window, :])
        for w in range(BLOCK_W):
            step = pl.ds(w, rows, stride=PITCH)
            left = jnp.concatenate([hold[0, step, :], hold[1, step, :]], 1).astype(BF16)
            right = refl_ref[:, first + w].reshape(2 * sources, 2 * LANES)
            both = lax.dot_general(
                left, right, (((1,), (1,)), ((), ())), preferred_element_type=F32
            )
            by_real = both[:, :LANES].reshape(pieces, 2, focal, LANES)
            by_imag = both[:, LANES:].reshape(pieces, 2, focal, LANES)
            value = jnp.stack(
                [by_real[:, 0] - by_imag[:, 1], by_real[:, 1] + by_imag[:, 0]], 1
            )
            result[step, :] = value.reshape(rows, LANES)
        for place, out in ((0, keep_ref), (1, send_ref)):
            for y in range(2):
                group = (2 * y + place) ^ me
                for k in range(pieces):
                    for c in range(2):
                        for p in range(share):
                            start = ((k * 2 + c) * focal + group * share + p) * PITCH
                            part = result[pl.ds(pl.multiple_of(start, 8), BLOCK_W), :]
                            out[y, k, c, p, window, :] = part.astype(BF16)
        return carry

    lax.fori_loop(0, refl_ref.shape[1] // BLOCK_W, block, 0)


def convolve_pieces(ids, reflection, plan, arrays, pieces, focal):
    two, freq, sources, receivers = reflection.shape
    rows = pieces * 2 * focal
    out = jax.ShapeDtypeStruct((2, pieces, 2, focal // 4, freq, LANES), BF16)
    return call(
        functools.partial(convolve_kernel, plan, pieces, focal),
        "convolve",
        [out, out],
        2 * freq * rows * 256 * 256,
        freq * (2 * sources * 512 + rows * 768),
        (ids, reflection, *arrays),
        [
            pltpu.VMEM((2, rows * PITCH, LANES), F32),
            pltpu.VMEM((rows * PITCH, LANES), F32),
        ],
    )


def correlate_kernel(pieces, ids, refl_ref, *refs):
    ins = [[refs[GROUP_ORDER.index(j * pieces + k)] for k in range(pieces)] for j in range(4)]
    outs = refs[4 * pieces : -2]
    hold, result = refs[-2:]
    half, me = ids[0], ids[1]
    share = ins[0][0].shape[1]
    focal = 4 * share
    sources = refl_ref.shape[2]
    rows = pieces * focal
    part_size = focal // HALVES

    def block(b, carry):
        first = pl.multiple_of(b * BLOCK_W, BLOCK_W)
        window = pl.ds(first, BLOCK_W)
        for j in range(4):
            group = j ^ me
            for k in range(pieces):
                for p in range(share):
                    start = pl.multiple_of((k * focal + group * share + p) * PITCH, 8)
                    for c in range(2):
                        value = ins[j][k][c, p, window, :].astype(F32)
                        hold[c, pl.ds(start, BLOCK_W), :] = value
        for w in range(BLOCK_W):
            step = pl.ds(w, rows, stride=PITCH)
            real = hold[0, step, :].astype(BF16)
            imag = hold[1, step, :].astype(BF16)
            left = jnp.concatenate(
                [jnp.concatenate([real, imag], 1), jnp.concatenate([imag, -real], 1)], 0
            )
            right = refl_ref[:, first + w].reshape(2 * sources, 2 * LANES)
            value = lax.dot_general(
                left, right, (((1,), (0,)), ((), ())), preferred_element_type=F32
            )
            step = pl.ds(w, 2 * rows, stride=PITCH)
            result[0, step, :] = value[:, :LANES]
            result[1, step, :] = value[:, LANES:]
        index = 0
        for place in (half, 1 - half):
            for q in range(HALVES):
                for group in PAIRS:
                    for i, k in enumerate(group):
                        for c in range(2):
                            for p in range(part_size):
                                at = ((c * pieces + k) * focal + q * part_size + p) * PITCH
                                part = result[place, at : at + BLOCK_W, :]
                                outs[index][i, c, p, window, :] = part.astype(BF16)
                    index += 1
        return carry

    lax.fori_loop(0, refl_ref.shape[1] // BLOCK_W, block, 0)


PAIRS = ((2, 3), (1, 0))


def correlate_pieces(ids, reflection, groups):
    pieces = len(groups[0])
    two, share, freq, lanes = groups[0][0].shape
    focal = 4 * share
    sources = reflection.shape[2]
    rows = pieces * 2 * focal
    out = jax.ShapeDtypeStruct((2, 2, focal // HALVES, freq, LANES), BF16)
    count = HALVES * len(PAIRS)
    results = call(
        functools.partial(correlate_kernel, pieces),
        "correlate",
        [out] * (2 * count),
        2 * freq * rows * 256 * 256,
        freq * (2 * sources * 512 + rows * 768),
        (ids, reflection, *[groups[i // pieces][i % pieces] for i in GROUP_ORDER]),
        [
            pltpu.VMEM((2, rows // 2 * PITCH, LANES), F32),
            pltpu.VMEM((2, rows * PITCH, LANES), F32),
        ],
    )
    return results[:count], results[count:]


def windowed(columns_ref, rows, onsets):
    signal = jnp.dot(columns_ref[...], rows, preferred_element_type=F32)
    sample = lax.broadcasted_iota(jnp.int32, signal.shape, 0)
    return jnp.where(sample < onsets, signal, 0.0).astype(BF16)


def mute_source_kernel(copy, ids, onset_ref, rows_ref, columns_ref, *refs):
    pieces = (len(refs) - copy) // 2
    ins, outs = refs[:pieces], refs[pieces : 2 * pieces]
    share, width = ins[0].shape[1], ins[0].shape[2]
    first = ids[1] * share
    if copy:
        for k in range(pieces):
            refs[-1][k] = ins[k][...]
    spectrum = jnp.concatenate(
        [
            jnp.concatenate([ref[c, p] for ref in ins for c in range(2)], 0)
            for p in range(share)
        ],
        1,
    )
    onsets = jnp.concatenate([onset_ref[pl.ds(first + p, 1), :] for p in range(share)], 1)
    muted = windowed(columns_ref, spectrum, onsets)
    back = jnp.dot(rows_ref[...], muted, preferred_element_type=F32).astype(BF16)
    for i, out in enumerate(outs):
        for c in range(2):
            for p in range(share):
                start = (2 * i + c) * width
                out[c, p] = back[start : start + width, p * LANES : (p + 1) * LANES]


def mute_source(ids, onset, rows, columns, pieces, copy):
    shape = pieces[0].shape
    outs = [jax.ShapeDtypeStruct(shape, BF16)] * len(pieces)
    if copy:
        outs = outs + [jax.ShapeDtypeStruct((len(pieces),) + shape, BF16)]
    return call(
        functools.partial(mute_source_kernel, int(copy)),
        "mute_source",
        outs,
        4 * NT * 2 * F * shape[1] * LANES,
        3 << 20,
        (ids, onset, rows, columns, *pieces),
    )


def trace_kernel(ids, onset_ref, rows_ref, *refs):
    ins, out_ref = refs[:4], refs[4]
    pieces, two, share = ins[0].shape[:3]
    step = pl.program_id(0)
    for j in range(4):

        @pl.when(step // share == j)
        def one():
            p = step % share
            spectrum = jnp.concatenate(
                [ins[j][k, c, p] for k in range(pieces) for c in range(2)], 0
            )
            signal = lax.dot_general(
                spectrum, rows_ref[...], (((0,), (0,)), ((), ())), preferred_element_type=F32
            )
            sample = lax.broadcasted_iota(jnp.int32, signal.shape, 1)
            out_ref[0] = jnp.where(sample < onset_ref[0], signal, 0.0).astype(BF16)


def trace_source(ids, onset, rows, groups):
    focal, sources = onset.shape
    share = groups[0].shape[2]

    def place(g, ids):
        return ((g // share) ^ ids[1]) * share + g % share, 0, 0

    return pl.pallas_call(
        trace_kernel,
        name="trace_source",
        out_shape=jax.ShapeDtypeStruct((focal, sources, NT), BF16),
        grid_spec=pltpu.PrefetchScalarGridSpec(
            num_scalar_prefetch=1,
            grid=(focal,),
            in_specs=[pl.BlockSpec((1, sources, 1), place)] + [VMEM_SPEC] * 5,
            out_specs=pl.BlockSpec((1, sources, NT), place),
        ),
        compiler_params=pltpu.CompilerParams(vmem_limit_bytes=VMEM_BYTES),
        cost_estimate=pl.CostEstimate(
            flops=2 * NT * 2 * F * focal * LANES, bytes_accessed=5 << 20, transcendentals=0
        ),
    )(ids, onset[:, :, None], rows, *groups)


def mute_receiver_kernel(first, both, last, ids, onset_ref, rows_ref, columns_ref, *refs):
    two, three, one, near, extra = refs[:5]
    pieces = 4
    direct = refs[5 : 5 + pieces]
    outs = refs[5 + pieces :]
    half = ids[0]
    count, width = one.shape[1], one.shape[2]
    lanes = pl.ds(pl.multiple_of(half * LANES, LANES), LANES)

    def part(k, c, p):
        if k == 0:
            return (near[1, c, p].astype(F32) + extra[1, c, p].astype(F32)).astype(BF16)
        return (None, one, two, three)[k][c, p]

    step = 2
    for start in range(0, count, step):
        group = range(start, start + step)
        spectrum = jnp.concatenate(
            [
                jnp.concatenate([part(k, c, p) for k in range(pieces) for c in range(2)], 0)
                for p in group
            ],
            1,
        )
        onsets = jnp.concatenate(
            [onset_ref[first + p : first + p + 1, lanes] for p in group], 1
        )
        muted = windowed(columns_ref, spectrum, onsets)
        back = jnp.dot(rows_ref[...], muted, preferred_element_type=F32)
        for k in range(pieces):
            for c in range(2):
                for i, p in enumerate(group):
                    at = (2 * k + c) * width
                    block = back[at : at + width, i * LANES : (i + 1) * LANES]
                    if k in both:
                        wave = direct[k][half, c, first + p]
                    else:
                        wave = direct[k][c, first + p]
                    value = (wave.astype(F32) + block).astype(BF16)
                    if last:
                        outs[0][c, k ^ ids[2], p] = value
                    else:
                        outs[k][c, p] = value


def mute_receiver(ids, onset, rows, columns, arrays, direct, first, both, last):
    shape = arrays[2].shape
    count, freq = shape[1], shape[2]
    if last:
        outs = jax.ShapeDtypeStruct((2, 4, count, freq, LANES), BF16)
    else:
        outs = [jax.ShapeDtypeStruct(shape, BF16)] * 4
    return call(
        functools.partial(mute_receiver_kernel, first, both, last),
        "mute_receiver",
        outs,
        4 * NT * 2 * F * count * LANES,
        4 << 20,
        (ids, onset, rows, columns, *arrays, *direct),
    )


def join_kernel(ids, *refs):
    ins, out_ref, hold = refs[:HALVES], refs[-2], refs[-1]
    two, foc_count, count, width, lanes = ins[0].shape
    focal = HALVES * count
    step = pl.program_id(0)
    for c in range(2):
        for q, ref in enumerate(ins):
            for p in range(count):
                hold[pl.ds(c * width * focal + q * count + p, width, stride=focal), :] = ref[
                    c, step, p
                ].astype(F32)
    out_ref[...] = hold[...].astype(BF16).reshape(out_ref.shape)


def join_halves(ids, parts, mask, into=None):
    two, foc_count, count, freq, lanes = parts[0].shape
    focal = HALVES * count
    extra = [] if into is None else [into]
    return pl.pallas_call(
        join_kernel,
        name="join_halves",
        out_shape=jax.ShapeDtypeStruct((two, foc_count * freq, focal, 2 * lanes), BF16),
        grid_spec=pltpu.PrefetchScalarGridSpec(
            num_scalar_prefetch=1,
            grid=(foc_count,),
            in_specs=[VMEM_SPEC] * HALVES + [pl.BlockSpec(memory_space=pl.ANY)] * len(extra),
            out_specs=pl.BlockSpec(
                (two, freq, focal, lanes), lambda g, ids: (0, g, 0, ids[0] ^ mask)
            ),
            scratch_shapes=[pltpu.VMEM((two * freq * focal, lanes), F32)],
        ),
        input_output_aliases={1 + HALVES: 0} if extra else {},
        compiler_params=pltpu.CompilerParams(vmem_limit_bytes=VMEM_BYTES),
        cost_estimate=pl.CostEstimate(
            flops=0, bytes_accessed=8 * foc_count * freq * focal * lanes, transcendentals=0
        ),
    )(ids, *parts, *extra)


def add(left, right):
    return (left.astype(F32) + right.astype(F32)).astype(BF16)


def resident(counts, reflection, direct_wave, onset_receiver, onset_source):
    src_count, rcv_count, foc_count = counts
    ids = jnp.stack([lax.axis_index("src"), lax.axis_index("rcv"), lax.axis_index("foc")])
    ids = ids.astype(jnp.int32)
    focal = direct_wave.shape[2]
    pieces = range(foc_count)
    near = (0, 1)

    def to_foc(value, k):
        return value if k == 0 else swap(value, "foc", k, foc_count)

    def to_src(value):
        return swap(value, "src", 1, src_count)

    def to_core(value):
        return swap(value, "rcv", 1, rcv_count)

    def to_y(value):
        return swap(value, "rcv", 2, rcv_count)

    def spread(value):
        across = to_y(value)
        return [value, to_core(value), across, to_core(across)]

    direct = [None] * foc_count
    direct[2] = split_wave(ids, direct_wave, 2, foc_count, False)
    rows, columns = basis(ids)
    later, rows, columns = lax.optimization_barrier((ids, rows, columns))
    direct[3] = split_wave(later, direct_wave, 3, foc_count, False)
    later, direct[3] = lax.optimization_barrier((ids, direct[3]))
    direct[1] = split_wave(later, direct_wave, 1, foc_count, True)
    direct[0] = split_wave(later, direct_wave, 0, foc_count, True)
    plan, arrays = [("both", 0, 0)], [direct[0]]
    for k in (2, 3, 1):
        got = to_foc(direct[k], k)
        if k in near:
            plan, arrays = plan + [("both", k, 0)], arrays + [got]
        else:
            plan = plan + [("own", k, 0), ("other", k, 0)]
            arrays = arrays + [got, to_src(got)]
    for iteration in range(ITERS):
        last = iteration == ITERS - 1
        keep, send = convolve_pieces(ids, reflection, tuple(plan), arrays, foc_count, focal)
        got = to_core(send)
        beyond = to_y(add(keep[1], got[1]))
        total = (keep[0].astype(F32) + got[0].astype(F32) + beyond.astype(F32)).astype(BF16)
        spectrum = [to_foc(total[k], k) for k in pieces]
        returned = mute_source(ids, onset_source, rows, columns, spectrum, last)
        mine = [to_foc(returned[k], k) for k in pieces]
        across = [to_y(value) for value in mine]
        groups = [mine, [to_core(v) for v in mine], across, [to_core(v) for v in across]]
        own, other = correlate_pieces(ids, reflection, groups)
        renewed = []
        early = []
        plan, arrays = [], []
        count = focal // HALVES
        for q in range(HALVES):
            far, close = 2 * q, 2 * q + 1
            got_far, got_close = to_src(other[far]), to_src(other[close])
            if q == 1:
                got_close, fresh = lax.optimization_barrier((got_close, fresh))
            ready = (
                to_foc(add(own[far][0], got_far[0]), 2),
                to_foc(add(own[far][1], got_far[1]), 3),
                to_foc(add(own[close][0], got_close[0]), 1),
                own[close],
                got_close,
            )
            if q == 1:
                ready, early = lax.optimization_barrier((ready, early))
            fresh = mute_receiver(
                ids, onset_receiver, rows, columns, ready, direct, q * count, near, last
            )
            if last:
                renewed.append(fresh)
                continue
            moved = [to_foc(fresh[k], k) for k in (2, 3, 1, 0)]
            if q == 0:
                before, early = moved, [to_src(moved[3])]
                continue
            after = [to_src(moved[3])]
            before[:2], moved[2], after = lax.optimization_barrier(
                (before[:2], moved[2], after)
            )
            crossed = [to_src(value) for value in before[:3]] + early
            after.append(to_src(moved[2]))
            after = [to_src(moved[0]), to_src(moved[1]), after[1], after[0]]
            arrays = before + crossed + moved + after
            plan = [
                (kind, k, start * count)
                for start in range(2)
                for kind in ("own", "other")
                for k in (2, 3, 1, 0)
            ]
        if last:
            crossed = [to_src(value) for value in renewed]
            muted_trace = trace_source(ids, onset_source, rows, spread(returned[-1]))
            partly = join_halves(ids, renewed, 0)
            return join_halves(ids, crossed, 1, partly), muted_trace


def local(counts, reflection, direct_wave, onset_receiver, onset_source):
    src_count, rcv_count, foc_count = counts
    two, freq, sources, receivers = reflection.shape
    focal = direct_wave.shape[2]
    fits = (
        (src_count, rcv_count, foc_count) == (2, 4, 4)
        and sources == LANES
        and receivers == 2 * LANES
        and focal == 8
        and freq == 4 * BLOCK_W
        and freq * foc_count == F
    )
    if fits:
        return resident(counts, reflection, direct_wave, onset_receiver, onset_source)
    return general(reflection, direct_wave, onset_receiver, onset_source)


def solution(mesh):
    in_specs = (
        P(None, "foc", "src", "rcv"),
        P(None, None, "foc", "rcv"),
        P("foc", "rcv"),
        P("foc", "src"),
    )
    out_specs = (P(None, None, "foc", "rcv"), P("foc", "src", None))
    counts = (mesh.shape["src"], mesh.shape["rcv"], mesh.shape["foc"])
    return jax.shard_map(
        functools.partial(local, counts),
        mesh=mesh,
        in_specs=in_specs,
        out_specs=out_specs,
        check_vma=False,
    )
```

```python
import functools
import math

import jax
import jax.numpy as jnp
from jax import lax
from jax.experimental import pallas as pl
from jax.experimental.pallas import tpu as pltpu
from jax.sharding import PartitionSpec as P

F = 256
NT = 1024
ITERS = 2
LANES = 128
BLOCK_W = 16
PITCH = 24
HALVES = 2
GROUP_ORDER = (4, 3, 15, 5, 12, 2, 6, 9, 7, 14, 11, 1, 10, 13, 0, 8)
F32 = jnp.float32
BF16 = jnp.bfloat16
VMEM_BYTES = 24 * 1024 * 1024


def basis_table():
    frequency_bins = jnp.arange(F, dtype=jnp.int32) + 1
    samples = jnp.arange(NT, dtype=jnp.int32)
    phases = frequency_bins[:, None] * samples[None, :] % NT
    angles = phases.astype(jnp.float32) * (2.0 * math.pi / NT)
    norming = math.sqrt(2.0 / NT)
    return (jnp.stack([jnp.cos(angles), -jnp.sin(angles)]) * norming).astype(jnp.bfloat16)


def mute_traces(spectrum, onsets, basis_rows):
    focal_count = spectrum.shape[2]
    samples = jnp.arange(NT, dtype=jnp.int32)

    def one_focus(focal_index, carry):
        muted_all, returned_all = carry
        one_spectrum = lax.dynamic_slice_in_dim(spectrum, focal_index, 1, 2)
        one_onset = lax.dynamic_slice_in_dim(onsets, focal_index, 1, 0)
        signal = jnp.einsum(
            "cwpr,cwt->prt", one_spectrum, basis_rows, preferred_element_type=jnp.float32
        )
        window = samples[None, None, :] < one_onset[:, :, None]
        muted_one = jnp.where(window, signal, 0.0).astype(jnp.bfloat16)
        returned = jnp.einsum(
            "prt,cwt->cwpr", muted_one, basis_rows, preferred_element_type=jnp.float32
        )
        muted_all = lax.dynamic_update_slice_in_dim(muted_all, muted_one, focal_index, 0)
        returned_all = lax.dynamic_update_slice_in_dim(returned_all, returned, focal_index, 2)
        return (muted_all, returned_all)

    initial = (
        jnp.zeros((focal_count, spectrum.shape[3], NT), jnp.bfloat16),
        jnp.zeros(spectrum.shape, jnp.float32),
    )
    return lax.fori_loop(0, focal_count, one_focus, initial)


def convolve(reflection, focusing):
    real_out = jnp.einsum(
        "wsr,wpr->wps", reflection[0], focusing[0], preferred_element_type=jnp.float32
    ) - jnp.einsum("wsr,wpr->wps", reflection[1], focusing[1], preferred_element_type=jnp.float32)
    imag_out = jnp.einsum(
        "wsr,wpr->wps", reflection[0], focusing[1], preferred_element_type=jnp.float32
    ) + jnp.einsum("wsr,wpr->wps", reflection[1], focusing[0], preferred_element_type=jnp.float32)
    return jnp.stack([real_out, imag_out])


def correlate(reflection, spectrum):
    real_out = jnp.einsum(
        "wsr,wps->wpr", reflection[0], spectrum[0], preferred_element_type=jnp.float32
    ) + jnp.einsum("wsr,wps->wpr", reflection[1], spectrum[1], preferred_element_type=jnp.float32)
    imag_out = jnp.einsum(
        "wsr,wps->wpr", reflection[0], spectrum[1], preferred_element_type=jnp.float32
    ) - jnp.einsum("wsr,wps->wpr", reflection[1], spectrum[0], preferred_element_type=jnp.float32)
    return jnp.stack([real_out, imag_out])


def renew(shares, direct_wave, onset_receiver, basis_rows, source_index):
    share_width = shares.shape[3]
    offset = source_index * share_width
    onset_share = lax.dynamic_slice_in_dim(onset_receiver, offset, share_width, 1)
    direct_share = lax.dynamic_slice_in_dim(direct_wave, offset, share_width, 3)
    unused, update = mute_traces(shares, onset_share, basis_rows)
    renewed = (direct_share.astype(jnp.float32) + update).astype(jnp.bfloat16)
    return lax.all_gather(renewed, "src", axis=3, tiled=True)


def general(reflection, direct_wave, onset_receiver, onset_source):
    basis_rows = basis_table()
    source_index = lax.axis_index("src")
    whole_reflection = lax.all_gather(reflection, "foc", axis=1, tiled=True)
    focusing = direct_wave
    muted_trace = None
    for iteration in range(ITERS):
        partial_value = convolve(whole_reflection, focusing)
        spectrum = lax.psum(partial_value.astype(jnp.bfloat16), "rcv")
        muted_trace, returned = mute_traces(spectrum, onset_source, basis_rows)
        partial_adjoint = correlate(whole_reflection, returned.astype(jnp.bfloat16))
        shares = lax.psum_scatter(
            partial_adjoint.astype(jnp.bfloat16), "src", scatter_dimension=3, tiled=True
        )
        focusing = renew(shares, direct_wave, onset_receiver, basis_rows, source_index)
    return (focusing, muted_trace)


VMEM_SPEC = pl.BlockSpec(memory_space=pltpu.VMEM)
SMEM_SPEC = pl.BlockSpec(memory_space=pltpu.SMEM)


def swap(value, axis, mask, count):
    return lax.ppermute(value, axis, [(i, i ^ mask) for i in range(count)])


def call(kernel, name, out_shape, flops, size, operands, scratch=()):
    many = isinstance(out_shape, list)
    return pl.pallas_call(
        kernel,
        name=name,
        out_shape=out_shape,
        in_specs=[SMEM_SPEC] + [VMEM_SPEC] * (len(operands) - 1),
        out_specs=[VMEM_SPEC] * len(out_shape) if many else VMEM_SPEC,
        scratch_shapes=list(scratch),
        compiler_params=pltpu.CompilerParams(vmem_limit_bytes=VMEM_BYTES),
        cost_estimate=pl.CostEstimate(flops=flops, bytes_accessed=size, transcendentals=0),
    )(*operands)


def table(frequency, part, sample):
    phase = ((frequency + 1) * sample + part * (NT // 4)) & (NT - 1)
    x = (jnp.abs(phase - NT // 2) - NT // 4).astype(F32) * (4.0 / NT)
    square = x * x
    total = jnp.zeros_like(x)
    for order in (11, 9, 7, 5, 3, 1):
        sign = -1.0 if order % 4 == 3 else 1.0
        total = total * square + sign * (math.pi / 2) ** order / math.factorial(order)
    return (total * x * math.sqrt(2.0 / NT)).astype(BF16)


def basis_kernel(ids, rows_ref, columns_ref):
    size = rows_ref.shape[0]
    freq = BLOCK_W * 4
    pieces = size // (2 * freq)
    for k in range(pieces):
        first = (k ^ ids[2]) * freq
        for c in range(2):
            frequency = lax.broadcasted_iota(jnp.int32, (freq, NT), 0) + first
            sample = lax.broadcasted_iota(jnp.int32, (freq, NT), 1)
            start = (2 * k + c) * freq
            rows_ref[start : start + freq, :] = table(frequency, c, sample)
        lane = lax.broadcasted_iota(jnp.int32, (NT, 2 * freq), 1)
        sample = lax.broadcasted_iota(jnp.int32, (NT, 2 * freq), 0)
        part = (lane >= freq).astype(jnp.int32)
        start = 2 * k * freq
        columns_ref[:, start : start + 2 * freq] = table(lane - part * freq + first, part, sample)


def basis(ids):
    size = 2 * F
    return call(
        basis_kernel,
        "basis",
        [jax.ShapeDtypeStruct((size, NT), BF16), jax.ShapeDtypeStruct((NT, size), BF16)],
        40 * size * NT,
        4 * size * NT,
        (ids,),
    )


def split_kernel(both, ids, wave_ref, out_ref, hold):
    width, focal = wave_ref.shape[1], wave_ref.shape[2]
    for place in range(2 if both else 1):
        lanes = slice(place * LANES, (place + 1) * LANES)
        hold[...] = wave_ref[0, :, :, lanes].astype(F32).reshape(width * focal, LANES)
        for p in range(focal):
            rows = hold[pl.ds(p, width, stride=focal), :].astype(BF16)
            if both:
                out_ref[place, 0, p] = rows
            else:
                out_ref[0, p] = rows


def split_wave(ids, wave, piece, foc_count, both):
    freq = wave.shape[1] // foc_count
    focal = wave.shape[2]
    if both:
        shape = (2, 2, focal, freq, LANES)
        in_spec = pl.BlockSpec(
            (1, freq, focal, 2 * LANES), lambda c, ids: (c, ids[2] ^ piece, 0, 0)
        )
        out_spec = pl.BlockSpec((2, 1, focal, freq, LANES), lambda c, ids: (0, c, 0, 0, 0))
    else:
        shape = (2, focal, freq, LANES)
        in_spec = pl.BlockSpec(
            (1, freq, focal, LANES), lambda c, ids: (c, ids[2] ^ piece, 0, ids[0])
        )
        out_spec = pl.BlockSpec((1, focal, freq, LANES), lambda c, ids: (c, 0, 0, 0))
    return pl.pallas_call(
        functools.partial(split_kernel, both),
        name="split_wave",
        out_shape=jax.ShapeDtypeStruct(shape, BF16),
        grid_spec=pltpu.PrefetchScalarGridSpec(
            num_scalar_prefetch=1,
            grid=(2,),
            in_specs=[in_spec],
            out_specs=out_spec,
            scratch_shapes=[pltpu.VMEM((freq * focal, LANES), F32)],
        ),
        compiler_params=pltpu.CompilerParams(vmem_limit_bytes=VMEM_BYTES),
        cost_estimate=pl.CostEstimate(
            flops=0, bytes_accessed=8 * focal * freq * LANES, transcendentals=0
        ),
    )(ids, pltpu.with_memory_space_constraint(wave, pltpu.HBM))


def convolve_kernel(plan, pieces, focal, ids, refl_ref, *refs):
    ins = refs[: len(plan)]
    keep_ref, send_ref, hold, result = refs[len(plan) :]
    half, me = ids[0], ids[1]
    sources = refl_ref.shape[2]
    rows = pieces * 2 * focal
    share = focal // 4

    def block(b, carry):
        first = pl.multiple_of(b * BLOCK_W, BLOCK_W)
        window = pl.ds(first, BLOCK_W)

        def put(place, k, c, start, value):
            for p in range(value.shape[0]):
                at = ((k * 2 + c) * focal + start + p) * PITCH
                hold[place, at : at + BLOCK_W, :] = value[p].astype(F32)

        for ref, (kind, k, start) in zip(ins, plan):
            for c in range(2):
                if kind == "both":
                    put(0, k, c, start, ref[0, c, :, window, :])
                    put(1, k, c, start, ref[1, c, :, window, :])
                elif kind == "own":
                    put(half, k, c, start, ref[c, :, window, :])
                else:
                    put(1 - half, k, c, start, ref[c, :, window, :])
        for w in range(BLOCK_W):
            step = pl.ds(w, rows, stride=PITCH)
            left = jnp.concatenate([hold[0, step, :], hold[1, step, :]], 1).astype(BF16)
            right = refl_ref[:, first + w].reshape(2 * sources, 2 * LANES)
            both = lax.dot_general(
                left, right, (((1,), (1,)), ((), ())), preferred_element_type=F32
            )
            by_real = both[:, :LANES].reshape(pieces, 2, focal, LANES)
            by_imag = both[:, LANES:].reshape(pieces, 2, focal, LANES)
            value = jnp.stack(
                [by_real[:, 0] - by_imag[:, 1], by_real[:, 1] + by_imag[:, 0]], 1
            )
            result[step, :] = value.reshape(rows, LANES)
        for place, out in ((0, keep_ref), (1, send_ref)):
            for y in range(2):
                group = (2 * y + place) ^ me
                for k in range(pieces):
                    for c in range(2):
                        for p in range(share):
                            start = ((k * 2 + c) * focal + group * share + p) * PITCH
                            part = result[pl.ds(pl.multiple_of(start, 8), BLOCK_W), :]
                            out[y, k, c, p, window, :] = part.astype(BF16)
        return carry

    lax.fori_loop(0, refl_ref.shape[1] // BLOCK_W, block, 0, unroll=2)


def convolve_pieces(ids, reflection, plan, arrays, pieces, focal):
    two, freq, sources, receivers = reflection.shape
    rows = pieces * 2 * focal
    out = jax.ShapeDtypeStruct((2, pieces, 2, focal // 4, freq, LANES), BF16)
    return call(
        functools.partial(convolve_kernel, plan, pieces, focal),
        "convolve",
        [out, out],
        2 * freq * rows * 256 * 256,
        freq * (2 * sources * 512 + rows * 768),
        (ids, reflection, *arrays),
        [
            pltpu.VMEM((2, rows * PITCH, LANES), F32),
            pltpu.VMEM((rows * PITCH, LANES), F32),
        ],
    )


def correlate_kernel(pieces, ids, refl_ref, *refs):
    ins = [[refs[GROUP_ORDER.index(j * pieces + k)] for k in range(pieces)] for j in range(4)]
    outs = refs[4 * pieces : -2]
    hold, result = refs[-2:]
    half, me = ids[0], ids[1]
    share = ins[0][0].shape[1]
    focal = 4 * share
    sources = refl_ref.shape[2]
    rows = pieces * focal
    part_size = focal // HALVES

    def block(b, carry):
        first = pl.multiple_of(b * BLOCK_W, BLOCK_W)
        window = pl.ds(first, BLOCK_W)
        for j in range(4):
            group = j ^ me
            for k in range(pieces):
                for p in range(share):
                    start = pl.multiple_of((k * focal + group * share + p) * PITCH, 8)
                    for c in range(2):
                        value = ins[j][k][c, p, window, :].astype(F32)
                        hold[c, pl.ds(start, BLOCK_W), :] = value
        for w in range(BLOCK_W):
            step = pl.ds(w, rows, stride=PITCH)
            real = hold[0, step, :].astype(BF16)
            imag = hold[1, step, :].astype(BF16)
            left = jnp.concatenate(
                [jnp.concatenate([real, imag], 1), jnp.concatenate([imag, -real], 1)], 0
            )
            right = refl_ref[:, first + w].reshape(2 * sources, 2 * LANES)
            value = lax.dot_general(
                left, right, (((1,), (0,)), ((), ())), preferred_element_type=F32
            )
            step = pl.ds(w, 2 * rows, stride=PITCH)
            result[0, step, :] = value[:, :LANES]
            result[1, step, :] = value[:, LANES:]
        index = 0
        for place in (half, 1 - half):
            for q in range(HALVES):
                for group in PAIRS:
                    for i, k in enumerate(group):
                        for c in range(2):
                            for p in range(part_size):
                                at = ((c * pieces + k) * focal + q * part_size + p) * PITCH
                                part = result[place, at : at + BLOCK_W, :]
                                outs[index][i, c, p, window, :] = part.astype(BF16)
                    index += 1
        return carry

    lax.fori_loop(0, refl_ref.shape[1] // BLOCK_W, block, 0, unroll=2)


PAIRS = ((2, 3), (1, 0))


def correlate_pieces(ids, reflection, groups):
    pieces = len(groups[0])
    two, share, freq, lanes = groups[0][0].shape
    focal = 4 * share
    sources = reflection.shape[2]
    rows = pieces * 2 * focal
    out = jax.ShapeDtypeStruct((2, 2, focal // HALVES, freq, LANES), BF16)
    count = HALVES * len(PAIRS)
    results = call(
        functools.partial(correlate_kernel, pieces),
        "correlate",
        [out] * (2 * count),
        2 * freq * rows * 256 * 256,
        freq * (2 * sources * 512 + rows * 768),
        (ids, reflection, *[groups[i // pieces][i % pieces] for i in GROUP_ORDER]),
        [
            pltpu.VMEM((2, rows // 2 * PITCH, LANES), F32),
            pltpu.VMEM((2, rows * PITCH, LANES), F32),
        ],
    )
    return results[:count], results[count:]


def windowed(columns_ref, rows, onsets):
    signal = jnp.dot(columns_ref[...], rows, preferred_element_type=F32)
    sample = lax.broadcasted_iota(jnp.int32, signal.shape, 0)
    return jnp.where(sample < onsets, signal, 0.0).astype(BF16)


def mute_source_kernel(copy, ids, onset_ref, rows_ref, columns_ref, *refs):
    pieces = (len(refs) - copy) // 2
    ins, outs = refs[:pieces], refs[pieces : 2 * pieces]
    share, width = ins[0].shape[1], ins[0].shape[2]
    first = ids[1] * share
    if copy:
        for k in range(pieces):
            refs[-1][k] = ins[k][...]
    spectrum = jnp.concatenate(
        [
            jnp.concatenate([ref[c, p] for ref in ins for c in range(2)], 0)
            for p in range(share)
        ],
        1,
    )
    onsets = jnp.concatenate([onset_ref[pl.ds(first + p, 1), :] for p in range(share)], 1)
    muted = windowed(columns_ref, spectrum, onsets)
    back = jnp.dot(rows_ref[...], muted, preferred_element_type=F32).astype(BF16)
    for i, out in enumerate(outs):
        for c in range(2):
            for p in range(share):
                start = (2 * i + c) * width
                out[c, p] = back[start : start + width, p * LANES : (p + 1) * LANES]


def mute_source(ids, onset, rows, columns, pieces, copy):
    shape = pieces[0].shape
    outs = [jax.ShapeDtypeStruct(shape, BF16)] * len(pieces)
    if copy:
        outs = outs + [jax.ShapeDtypeStruct((len(pieces),) + shape, BF16)]
    return call(
        functools.partial(mute_source_kernel, int(copy)),
        "mute_source",
        outs,
        4 * NT * 2 * F * shape[1] * LANES,
        3 << 20,
        (ids, onset, rows, columns, *pieces),
    )


def trace_kernel(ids, onset_ref, rows_ref, *refs):
    ins, out_ref = refs[:4], refs[4]
    pieces, two, share = ins[0].shape[:3]
    step = pl.program_id(0)
    for j in range(4):

        @pl.when(step // share == j)
        def one():
            p = step % share
            spectrum = jnp.concatenate(
                [ins[j][k, c, p] for k in range(pieces) for c in range(2)], 0
            )
            signal = lax.dot_general(
                spectrum, rows_ref[...], (((0,), (0,)), ((), ())), preferred_element_type=F32
            )
            sample = lax.broadcasted_iota(jnp.int32, signal.shape, 1)
            out_ref[0] = jnp.where(sample < onset_ref[0], signal, 0.0).astype(BF16)


def trace_source(ids, onset, rows, groups):
    focal, sources = onset.shape
    share = groups[0].shape[2]

    def place(g, ids):
        return ((g // share) ^ ids[1]) * share + g % share, 0, 0

    return pl.pallas_call(
        trace_kernel,
        name="trace_source",
        out_shape=jax.ShapeDtypeStruct((focal, sources, NT), BF16),
        grid_spec=pltpu.PrefetchScalarGridSpec(
            num_scalar_prefetch=1,
            grid=(focal,),
            in_specs=[pl.BlockSpec((1, sources, 1), place)] + [VMEM_SPEC] * 5,
            out_specs=pl.BlockSpec((1, sources, NT), place),
        ),
        compiler_params=pltpu.CompilerParams(vmem_limit_bytes=VMEM_BYTES),
        cost_estimate=pl.CostEstimate(
            flops=2 * NT * 2 * F * focal * LANES, bytes_accessed=5 << 20, transcendentals=0
        ),
    )(ids, onset[:, :, None], rows, *groups)


def mute_receiver_kernel(first, both, last, ids, onset_ref, rows_ref, columns_ref, *refs):
    two, three, one, near, extra = refs[:5]
    pieces = 4
    direct = refs[5 : 5 + pieces]
    outs = refs[5 + pieces :]
    half = ids[0]
    count, width = one.shape[1], one.shape[2]
    lanes = pl.ds(pl.multiple_of(half * LANES, LANES), LANES)

    def part(k, c, p):
        if k == 0:
            return (near[1, c, p].astype(F32) + extra[1, c, p].astype(F32)).astype(BF16)
        return (None, one, two, three)[k][c, p]

    step = 2
    for start in range(0, count, step):
        group = range(start, start + step)
        spectrum = jnp.concatenate(
            [
                jnp.concatenate([part(k, c, p) for k in range(pieces) for c in range(2)], 0)
                for p in group
            ],
            1,
        )
        onsets = jnp.concatenate(
            [onset_ref[first + p : first + p + 1, lanes] for p in group], 1
        )
        muted = windowed(columns_ref, spectrum, onsets)
        back = jnp.dot(rows_ref[...], muted, preferred_element_type=F32)
        for k in range(pieces):
            for c in range(2):
                for i, p in enumerate(group):
                    at = (2 * k + c) * width
                    block = back[at : at + width, i * LANES : (i + 1) * LANES]
                    if k in both:
                        wave = direct[k][half, c, first + p]
                    else:
                        wave = direct[k][c, first + p]
                    value = (wave.astype(F32) + block).astype(BF16)
                    if last:
                        outs[0][c, k ^ ids[2], p] = value
                    else:
                        outs[k][c, p] = value


def mute_receiver(ids, onset, rows, columns, arrays, direct, first, both, last):
    shape = arrays[2].shape
    count, freq = shape[1], shape[2]
    if last:
        outs = jax.ShapeDtypeStruct((2, 4, count, freq, LANES), BF16)
    else:
        outs = [jax.ShapeDtypeStruct(shape, BF16)] * 4
    return call(
        functools.partial(mute_receiver_kernel, first, both, last),
        "mute_receiver",
        outs,
        4 * NT * 2 * F * count * LANES,
        4 << 20,
        (ids, onset, rows, columns, *arrays, *direct),
    )


def join_kernel(ids, *refs):
    ins, out_ref, hold = refs[:HALVES], refs[-2], refs[-1]
    two, foc_count, count, width, lanes = ins[0].shape
    focal = HALVES * count
    step = pl.program_id(0)
    for c in range(2):
        for q, ref in enumerate(ins):
            for p in range(count):
                hold[pl.ds(c * width * focal + q * count + p, width, stride=focal), :] = ref[
                    c, step, p
                ].astype(F32)
    out_ref[...] = hold[...].astype(BF16).reshape(out_ref.shape)


def join_halves(ids, parts, mask, into=None):
    two, foc_count, count, freq, lanes = parts[0].shape
    focal = HALVES * count
    extra = [] if into is None else [into]
    return pl.pallas_call(
        join_kernel,
        name="join_halves",
        out_shape=jax.ShapeDtypeStruct((two, foc_count * freq, focal, 2 * lanes), BF16),
        grid_spec=pltpu.PrefetchScalarGridSpec(
            num_scalar_prefetch=1,
            grid=(foc_count,),
            in_specs=[VMEM_SPEC] * HALVES + [pl.BlockSpec(memory_space=pl.ANY)] * len(extra),
            out_specs=pl.BlockSpec(
                (two, freq, focal, lanes), lambda g, ids: (0, g, 0, ids[0] ^ mask)
            ),
            scratch_shapes=[pltpu.VMEM((two * freq * focal, lanes), F32)],
        ),
        input_output_aliases={1 + HALVES: 0} if extra else {},
        compiler_params=pltpu.CompilerParams(vmem_limit_bytes=VMEM_BYTES),
        cost_estimate=pl.CostEstimate(
            flops=0, bytes_accessed=8 * foc_count * freq * focal * lanes, transcendentals=0
        ),
    )(ids, *parts, *extra)


def add(left, right):
    return (left.astype(F32) + right.astype(F32)).astype(BF16)


def resident(counts, reflection, direct_wave, onset_receiver, onset_source):
    src_count, rcv_count, foc_count = counts
    ids = jnp.stack([lax.axis_index("src"), lax.axis_index("rcv"), lax.axis_index("foc")])
    ids = ids.astype(jnp.int32)
    focal = direct_wave.shape[2]
    pieces = range(foc_count)
    near = (0, 1)

    def to_foc(value, k):
        return value if k == 0 else swap(value, "foc", k, foc_count)

    def to_src(value):
        return swap(value, "src", 1, src_count)

    def to_core(value):
        return swap(value, "rcv", 1, rcv_count)

    def to_y(value):
        return swap(value, "rcv", 2, rcv_count)

    def spread(value):
        across = to_y(value)
        return [value, to_core(value), across, to_core(across)]

    direct = [None] * foc_count
    direct[2] = split_wave(ids, direct_wave, 2, foc_count, False)
    rows, columns = basis(ids)
    later, rows, columns = lax.optimization_barrier((ids, rows, columns))
    direct[3] = split_wave(later, direct_wave, 3, foc_count, False)
    later, direct[3] = lax.optimization_barrier((ids, direct[3]))
    direct[1] = split_wave(later, direct_wave, 1, foc_count, True)
    direct[0] = split_wave(later, direct_wave, 0, foc_count, True)
    plan, arrays = [("both", 0, 0)], [direct[0]]
    for k in (2, 3, 1):
        got = to_foc(direct[k], k)
        if k in near:
            plan, arrays = plan + [("both", k, 0)], arrays + [got]
        else:
            plan = plan + [("own", k, 0), ("other", k, 0)]
            arrays = arrays + [got, to_src(got)]
    for iteration in range(ITERS):
        last = iteration == ITERS - 1
        keep, send = convolve_pieces(ids, reflection, tuple(plan), arrays, foc_count, focal)
        got = to_core(send)
        beyond = to_y(add(keep[1], got[1]))
        total = (keep[0].astype(F32) + got[0].astype(F32) + beyond.astype(F32)).astype(BF16)
        spectrum = [to_foc(total[k], k) for k in pieces]
        returned = mute_source(ids, onset_source, rows, columns, spectrum, last)
        mine = [to_foc(returned[k], k) for k in pieces]
        across = [to_y(value) for value in mine]
        groups = [mine, [to_core(v) for v in mine], across, [to_core(v) for v in across]]
        own, other = correlate_pieces(ids, reflection, groups)
        renewed = []
        early = []
        plan, arrays = [], []
        count = focal // HALVES
        for q in range(HALVES):
            far, close = 2 * q, 2 * q + 1
            got_far, got_close = to_src(other[far]), to_src(other[close])
            if q == 1:
                got_close, fresh = lax.optimization_barrier((got_close, fresh))
            ready = (
                to_foc(add(own[far][0], got_far[0]), 2),
                to_foc(add(own[far][1], got_far[1]), 3),
                to_foc(add(own[close][0], got_close[0]), 1),
                own[close],
                got_close,
            )
            if q == 1:
                ready, early = lax.optimization_barrier((ready, early))
            fresh = mute_receiver(
                ids, onset_receiver, rows, columns, ready, direct, q * count, near, last
            )
            if last:
                renewed.append(fresh)
                continue
            moved = [to_foc(fresh[k], k) for k in (2, 3, 1, 0)]
            if q == 0:
                before, early = moved, [to_src(moved[3])]
                continue
            after = [to_src(moved[3])]
            before[:2], moved[2], after = lax.optimization_barrier(
                (before[:2], moved[2], after)
            )
            crossed = [to_src(value) for value in before[:3]] + early
            after.append(to_src(moved[2]))
            after = [to_src(moved[0]), to_src(moved[1]), after[1], after[0]]
            arrays = before + crossed + moved + after
            plan = [
                (kind, k, start * count)
                for start in range(2)
                for kind in ("own", "other")
                for k in (2, 3, 1, 0)
            ]
        if last:
            crossed = [to_src(value) for value in renewed]
            muted_trace = trace_source(ids, onset_source, rows, spread(returned[-1]))
            partly = join_halves(ids, renewed, 0)
            return join_halves(ids, crossed, 1, partly), muted_trace


def local(counts, reflection, direct_wave, onset_receiver, onset_source):
    src_count, rcv_count, foc_count = counts
    two, freq, sources, receivers = reflection.shape
    focal = direct_wave.shape[2]
    fits = (
        (src_count, rcv_count, foc_count) == (2, 4, 4)
        and sources == LANES
        and receivers == 2 * LANES
        and focal == 8
        and freq == 4 * BLOCK_W
        and freq * foc_count == F
    )
    if fits:
        return resident(counts, reflection, direct_wave, onset_receiver, onset_source)
    return general(reflection, direct_wave, onset_receiver, onset_source)


def solution(mesh):
    in_specs = (
        P(None, "foc", "src", "rcv"),
        P(None, None, "foc", "rcv"),
        P("foc", "rcv"),
        P("foc", "src"),
    )
    out_specs = (P(None, None, "foc", "rcv"), P("foc", "src", None))
    counts = (mesh.shape["src"], mesh.shape["rcv"], mesh.shape["foc"])
    return jax.shard_map(
        functools.partial(local, counts),
        mesh=mesh,
        in_specs=in_specs,
        out_specs=out_specs,
        check_vma=False,
    )
```
